256 devices in a mesh: section: 4 (over x_lo, core), ctx: 64 (over y, x_hi, z).
Axes of the slice: x: 4 (x_hi: 2, x_lo: 2; x = x_hi * 2 + x_lo), y: 4, z: 8, core: 2. Of those that a mesh axis runs over, the one named last changes fastest.
Arguments:
- block_order: int32 [64], replicated, may hold values from 0 to 63, each once
- queries: bfloat16 [4, 512, 2560], P('section', 'ctx'), may hold values from -400 to 400
- cache_keys: bfloat16 [8192, 2560], P('ctx', 'section'), may hold values from -6 to 6
- cache_values: bfloat16 [8192, 2560], P('ctx', 'section'), may hold values from -6 to 6
- attention_out: bfloat16 [4, 512, 2560], P('section', 'ctx'), may hold values from -6 to 6
- output_grad: bfloat16 [4, 512, 2560], P('section', 'ctx'), may hold values from -1536 to 1536
Outputs:
- grad_queries: bfloat16 [4, 512, 2560], P('section', 'ctx')
- grad_keys: bfloat16 [8192, 2560], P('ctx', 'section')
- grad_values: bfloat16 [8192, 2560], P('ctx', 'section')
The draws below stay inside these ranges and needn't reach their ends.
Inputs may be any that keep to these rules, and one draw needn't show every extreme that they name: `block_order`: every block number once.
All inputs are finite; a program needn't handle non-finite values.
Results may differ from the reference program's by a relative error of at most 0.012.
Values may be sent and summed in bfloat16 or wider, within the bound.
A program may use at most 64 MiB of HBM per device.

```python
import jax
import jax.numpy as jnp
from jax import lax

HEADS = 20
HEAD_DIM = 128
KV_DEV = 128
QR = 8
KV_LEN = 8192
QW = 512
LAYERS = 4
N_SECTION = 4
N_CTX = 64


def shared_plan(key):
    base_key = jax.random.fold_in(key, 101)
    key_total = KV_DEV * N_CTX
    features = HEADS * HEAD_DIM
    key_a = jax.random.fold_in(base_key, 0)
    cache_keys = jax.random.truncated_normal(key_a, -6.0, 6.0, (key_total, features))
    return cache_keys


def draw_cache_keys(key, part):
    cache_keys = shared_plan(key)
    return cache_keys.astype(jnp.bfloat16)


def draw_queries(key, part):
    base_key = jax.random.fold_in(key, 202)
    shape = (N_SECTION, QR * N_CTX, HEADS * HEAD_DIM)
    values = jax.random.truncated_normal(base_key, -6.0, 6.0, shape)
    return values.astype(jnp.bfloat16)


def draw_output_grad(key, part):
    base_key = jax.random.fold_in(key, 303)
    spread = KV_DEV * N_CTX / 32.0
    shape = (N_SECTION, QR * N_CTX, HEADS * HEAD_DIM)
    values = jax.random.truncated_normal(base_key, -6.0, 6.0, shape) * spread
    return values.astype(jnp.bfloat16)


def steps_of(stream_key, dims, pieces, least, high):
    loudness, own = 1.0, jax.random.fold_in(stream_key, 6)
    for axis_at, parts in pieces:
        steps = jnp.exp(jax.random.uniform(jax.random.fold_in(own, axis_at), (parts,), jnp.float32, least / len(pieces), high / len(pieces)))
        loudness = loudness * jnp.repeat(steps, dims[axis_at] // parts).reshape([-1 if axis == axis_at else 1 for axis in range(len(dims))])
    return loudness


def scatter_about(stream_key, extent, scale, limit, shards=(), kind=jnp.bfloat16):
    values = scale * jax.random.normal(stream_key, extent, jnp.float32)
    if shards:
        values = values * steps_of(stream_key, extent, shards, -0.22, 0.18)
    return jnp.clip(values, -limit, limit).astype(kind)


def setup_inputs(seed: int = 0) -> dict:
    key_of = jax.random.split(jax.random.key(seed), 7)
    return {
        "block_order": jax.random.permutation(key_of[0], N_CTX).astype(jnp.int32),
        "queries": draw_queries(jax.random.fold_in(key_of[6], 71), 0),
        "cache_keys": draw_cache_keys(jax.random.fold_in(key_of[6], 71), 0),
        "cache_values": scatter_about(key_of[3], (KV_LEN, HEADS * HEAD_DIM), 1.0, 6.0, ((0, 64), (1, 4))),
        "attention_out": scatter_about(key_of[4], (LAYERS, QW, HEADS * HEAD_DIM), 1.0, 6.0, ((0, 4), (1, 64))),
        "output_grad": draw_output_grad(jax.random.fold_in(key_of[6], 71), 0),
    }


masked_score = -1e30


def reference(block_order, queries, cache_keys, cache_values, attention_out, output_grad):
    key_total = cache_keys.shape[0]
    query_count = queries.shape[1]
    features = cache_keys.shape[1]
    scaling = HEAD_DIM ** -0.5
    key_rows = jnp.arange(key_total, dtype=jnp.int32)
    key_pos = block_order[key_rows // KV_DEV].astype(jnp.int32) * KV_DEV + key_rows % KV_DEV
    query_pos = key_total - query_count + jnp.arange(query_count, dtype=jnp.int32)
    visible = key_pos[None, :] <= query_pos[:, None]
    key_heads = cache_keys.reshape(key_total, HEADS, HEAD_DIM).transpose(1, 0, 2)
    value_heads = cache_values.reshape(key_total, HEADS, HEAD_DIM).transpose(1, 0, 2)

    def layer_step(running, layer_data):
        query_one, grad_one, out_one = layer_data
        delta_terms = jnp.sum((grad_one.astype(jnp.float32) * out_one.astype(jnp.float32)).reshape(query_count, HEADS, HEAD_DIM), axis=2).T
        query_heads = query_one.reshape(query_count, HEADS, HEAD_DIM).transpose(1, 0, 2)
        grad_heads = grad_one.reshape(query_count, HEADS, HEAD_DIM).transpose(1, 0, 2)

        def head_step(packed):
            query_head, grad_head, delta_head, key_head, value_head = packed
            scores = jnp.dot(query_head, key_head.T, preferred_element_type=jnp.float32) * scaling
            scores = jnp.where(visible, scores, masked_score)
            row_max = jnp.max(scores, axis=1, keepdims=True)
            row_sum = jnp.sum(jnp.where(visible, jnp.exp(scores - row_max), 0.0), axis=1, keepdims=True)
            log_total = row_max + jnp.log(row_sum)
            prob = jnp.where(visible, jnp.exp(scores - log_total), 0.0)
            prob_b = prob.astype(jnp.bfloat16)
            value_grad = jnp.dot(prob_b.T, grad_head, preferred_element_type=jnp.float32)
            prob_grad = jnp.dot(grad_head, value_head.T, preferred_element_type=jnp.float32)
            score_grad = (prob * (prob_grad - delta_head[:, None]) * scaling).astype(jnp.bfloat16)
            query_grad = jnp.dot(score_grad, key_head, preferred_element_type=jnp.float32)
            key_grad = jnp.dot(score_grad.T, query_head, preferred_element_type=jnp.float32)
            return query_grad, key_grad, value_grad

        query_grad, key_grad, value_grad = lax.map(head_step, (query_heads, grad_heads, delta_terms, key_heads, value_heads))
        return (running[0] + key_grad, running[1] + value_grad), query_grad

    zeros = jnp.zeros((HEADS, key_total, HEAD_DIM), jnp.float32)
    sums, query_grads = lax.scan(layer_step, (zeros, zeros), (queries, output_grad, attention_out))
    grad_queries = query_grads.transpose(0, 2, 1, 3).reshape(queries.shape[0], query_count, features).astype(jnp.bfloat16)
    grad_keys = sums[0].transpose(1, 0, 2).reshape(key_total, features).astype(jnp.bfloat16)
    grad_values = sums[1].transpose(1, 0, 2).reshape(key_total, features).astype(jnp.bfloat16)
    return grad_queries, grad_keys, grad_values
```

```python
import jax
import jax.numpy as jnp
from jax import lax
from jax.experimental import pallas as pl
from jax.experimental.pallas import tpu as pltpu
from jax.sharding import PartitionSpec as P

MESH = pl.DeviceIdType.MESH
F32 = jnp.float32
BF16 = jnp.bfloat16

NS, NY, NX, NZ = 4, 4, 2, 8
HG, HD, GF = 5, 128, 640
KR = 128
KV = NY * KR
QR = 8
NB = NX * NY
ZR = NB * QR
QW = NZ * ZR
SCALE = HD ** -0.5
MASKED = -1e30
RT = 128


def nt(a, b):
    return lax.dot_general(a, b, (((1,), (1,)), ((), ())), preferred_element_type=F32)


def tn(a, b):
    return lax.dot_general(a, b, (((0,), (0,)), ((), ())), preferred_element_type=F32)


def nn(a, b):
    return lax.dot_general(a, b, (((1,), (0,)), ((), ())), preferred_element_type=F32)


def kernel(order, q_in, do_in, o_in, k_in, v_in, dq_out, dk_out, dv_out,
           pk, pdel, p1, p1d, g, gd0, gd, kv, q3, do3, delc, pu, ds0, m3, lse3, c3, ls, lsx, lz,
           dqa, dkv, sqr, sql, rqr, rql, kvs, kvr, tb, p8, p9s, p9,
           s1, r1, s1d, r1d, s2, r2, s2d, r2d, sz, rz, szd, rzd, sy, ry, sl, rl, sx, rx,
           sg, rg, sk, rk, s8, r8, s9, r9):
    s = lax.axis_index("section")
    c = lax.axis_index("ctx")
    y = c // (NX * NZ)
    xh = (c // NZ) % NX
    z = c % NZ

    def dev(s_, y_, x_, z_):
        return (s_, (y_ * NX + x_) * NZ + z_)

    def rc(src, dst, ssem, rsem, to):
        return pltpu.make_async_remote_copy(
            src_ref=src, dst_ref=dst, send_sem=ssem, recv_sem=rsem,
            device_id=to, device_id_type=MESH)

    def up(v, n, mod):
        return (v + n) % mod

    def dn(v, n, mod):
        return (v + mod - n) % mod

    me = (s, c)
    others = [(j, k) for j in range(NY) for k in range(NX) if (j, k) != (0, 0)]

    bar = pltpu.get_barrier_semaphore()
    partners = [dev(up(s, j, NS), y, xh, z) for j in range(1, NS)]
    partners += [dev(s, up(y, j, NY), up(xh, k, NX), z) for j, k in others]
    partners += [dev(s, y, xh, up(z, j, NZ)) for j in range(1, NZ)]
    for p in partners:
        pl.semaphore_signal(bar, inc=1, device_id=p, device_id_type=MESH)

    lane = lax.broadcasted_iota(jnp.int32, (QR, 128), 1)
    for t in range(NS):
        cols = slice(t * GF, (t + 1) * GF)
        qf = q_in[0, :, cols].astype(F32)
        df = do_in[0, :, cols].astype(F32)
        of = o_in[0, :, cols].astype(F32)
        pk[t] = jnp.concatenate([qf, df], axis=0).astype(BF16)
        prod = df * of
        tile = jnp.zeros((QR, 128), F32)
        for h in range(HG):
            d = jnp.sum(prod[:, h * HD:(h + 1) * HD], axis=1, keepdims=True)
            tile = jnp.where(lane == h, d, tile)
        pdel[t] = tile
    for h in range(HG):
        kv[y, 0, h] = k_in[:, h * HD:(h + 1) * HD]
        kv[y, 1, h] = v_in[:, h * HD:(h + 1) * HD]

    pl.semaphore_wait(bar, len(partners))

    sends = []

    def go(cp):
        cp.start()
        sends.append(cp)

    for j in range(1, NS):
        t = up(s, j, NS)
        go(rc(pk.at[t], p1.at[s], s1.at[j], r1.at[j], (t, c)))
        go(rc(pdel.at[t], p1d.at[s], s1d.at[j], r1d.at[j], (t, c)))

    yr, yl = up(y, 1, NY), dn(y, 1, NY)
    y2 = up(y, 2, NY)
    dyr, dyl = dev(s, yr, xh, z), dev(s, yl, xh, z)
    for a in range(2):
        go(rc(kv.at[y, a], kv.at[y, a], sy.at[0, a], ry.at[0, a], dyr))
        go(rc(kv.at[y, a], kv.at[y, a], sy.at[1, a], ry.at[1, a], dyl))

    p1[s] = pk[s]
    p1d[s] = pdel[s]
    for j in range(1, NS):
        f = dn(s, j, NS)
        rc(p1.at[f], p1.at[f], s1.at[j], r1.at[j], me).wait_recv()
        rc(p1d.at[f], p1d.at[f], s1d.at[j], r1d.at[j], me).wait_recv()

    mine = xh * NY + y
    for j, k in others:
        ty, tx = up(y, j, NY), up(xh, k, NX)
        to = dev(s, ty, tx, z)
        go(rc(p1.at[ty], g.at[z, mine], s2.at[j, k], r2.at[j, k], to))
        go(rc(p1d.at[ty], gd0.at[mine], s2d.at[j, k], r2d.at[j, k], to))
    g[z, mine] = p1[y]
    gd0[mine] = p1d[y]
    for j, k in others:
        f = dn(xh, k, NX) * NY + dn(y, j, NY)
        rc(g.at[z, f], g.at[z, f], s2.at[j, k], r2.at[j, k], me).wait_recv()
        rc(gd0.at[f], gd0.at[f], s2d.at[j, k], r2d.at[j, k], me).wait_recv()
    tile = gd0[0]
    for b in range(1, NB):
        tile = tile + pltpu.roll(gd0[b], b * QR, 1)
    gd[z] = tile

    zr, zl = up(z, 1, NZ), dn(z, 1, NZ)
    dzr, dzl = dev(s, y, xh, zr), dev(s, y, xh, zl)
    half = NB // 2

    def zmsg(d, t, hf):
        src = dn(z, t - 1, NZ) if d == 0 else up(z, t - 1, NZ)
        ref = g.at[src, pl.ds(hf * half, half)]
        return rc(ref, ref, sz.at[d, t - 1, hf], rz.at[d, t - 1, hf], dzr if d == 0 else dzl)

    def zin(d, t, hf):
        src = dn(z, t, NZ) if d == 0 else up(z, t, NZ)
        ref = g.at[src, pl.ds(hf * half, half)]
        return rc(ref, ref, sz.at[d, t - 1, hf], rz.at[d, t - 1, hf], me)

    def zdmsg(d, t):
        src = dn(z, t - 1, NZ) if d == 0 else up(z, t - 1, NZ)
        return rc(gd.at[src], gd.at[src], szd.at[d, t - 1], rzd.at[d, t - 1], dzr if d == 0 else dzl)

    def zdin(d, t):
        src = dn(z, t, NZ) if d == 0 else up(z, t, NZ)
        return rc(gd.at[src], gd.at[src], szd.at[d, t - 1], rzd.at[d, t - 1], me)

    def unpack(zc):
        blk = g[zc].astype(F32).reshape(NB, 2, QR, GF)
        qc = blk[:, 0].reshape(ZR, GF).astype(BF16)
        dc = blk[:, 1].reshape(ZR, GF).astype(BF16)
        rows = pl.ds(pl.multiple_of(zc * ZR, ZR), ZR)
        for h in range(HG):
            q3[h, rows] = qc[:, h * HD:(h + 1) * HD]
            do3[h, rows] = dc[:, h * HD:(h + 1) * HD]
        tile = gd[zc]
        for b in range(NB):
            piece = tile if b == 0 else pltpu.roll(tile, 128 - b * QR, 1)
            delc[pl.ds(pl.multiple_of(zc * ZR + b * QR, QR), QR)] = piece

    for t in range(1, NZ // 2 + 1):
        last = t == NZ // 2
        for hf in range(2):
            for d in range(2):
                if last and hf != d:
                    continue
                if t > 1:
                    zin(d, t - 1, hf).wait_recv()
                go(zmsg(d, t, hf))
        if last:
            for d in range(2):
                zin(d, t - 1, 1 - d).wait_recv()
        for d in range(2):
            if t > 1:
                zdin(d, t - 1).wait_recv()
            if not (last and d == 1):
                go(zdmsg(d, t))
        if t == 1:
            rc(kv.at[yl, 0], kv.at[yl, 0], sy.at[0, 0], ry.at[0, 0], me).wait_recv()
            go(rc(kv.at[yl, 0], kv.at[yl, 0], sy.at[2, 0], ry.at[2, 0], dyr))
            rc(kv.at[yr, 1], kv.at[yr, 1], sy.at[1, 1], ry.at[1, 1], me).wait_recv()
            go(rc(kv.at[yr, 1], kv.at[yr, 1], sy.at[2, 1], ry.at[2, 1], dyl))
            unpack(z)
        else:
            unpack(dn(z, t - 1, NZ))
            unpack(up(z, t - 1, NZ))
    zin(0, NZ // 2, 0).wait_recv()
    zin(1, NZ // 2, 1).wait_recv()
    zdin(0, NZ // 2).wait_recv()
    unpack(up(z, NZ // 2, NZ))
    rc(kv.at[yl, 1], kv.at[yl, 1], sy.at[0, 1], ry.at[0, 1], me).wait_recv()
    rc(kv.at[yr, 0], kv.at[yr, 0], sy.at[1, 0], ry.at[1, 0], me).wait_recv()
    rc(kv.at[y2, 0], kv.at[y2, 0], sy.at[2, 0], ry.at[2, 0], me).wait_recv()
    rc(kv.at[y2, 1], kv.at[y2, 1], sy.at[2, 1], ry.at[2, 1], me).wait_recv()

    kcol = lax.broadcasted_iota(jnp.int32, (1, KV), 1)
    kblk = kcol // KR
    base = jnp.zeros((1, KV), jnp.int32)
    for b in range(NY):
        base = jnp.where(kblk == b, order[(b * NX + xh) * NZ + z], base)
    kpos = base * KR + kcol % KR
    first = NY * NX * NZ * KR - QW

    def qpos(rt):
        r = lax.broadcasted_iota(jnp.int32, (RT, 1), 0) + rt * RT
        rz_, rx_, ry_, rr = r // ZR, (r // (NY * QR)) % NX, (r // QR) % NY, r % QR
        return first + ((ry_ * NX + rx_) * NZ + rz_) * QR + rr

    NR = QW // RT

    def scores(h, _):
        kh = kv[:, 0, h].reshape(KV, HD)
        for rt in range(NR):
            rows = slice(rt * RT, (rt + 1) * RT)
            sc = nt(q3[h, rows], kh) * SCALE
            sc = jnp.where(kpos <= qpos(rt), sc, MASKED)
            m = jnp.max(sc, axis=1, keepdims=True)
            p = jnp.exp(sc - m)
            l = jnp.sum(p, axis=1, keepdims=True)
            pu[h, rows] = p
            m3[h, rows] = jnp.broadcast_to(m, (RT, 128))
            lse3[h, rows] = jnp.broadcast_to(m + jnp.log(l), (RT, 128))
        return 0

    lax.fori_loop(0, HG, scores, 0)

    lane2 = lax.broadcasted_iota(jnp.int32, (RT, 128), 1)
    for rt in range(NR):
        rows = slice(rt * RT, (rt + 1) * RT)
        st = jnp.zeros((RT, 128), F32)
        for h in range(HG):
            st = jnp.where(lane2 == h, lse3[h, rows], st)
        ls[:, rows] = st.T[:8]
    dx = dev(s, y, up(xh, 1, NX), z)
    cpx = rc(ls, lsx, sx.at[0], rx.at[0], dx)
    go(cpx)

    def dprob(h, _):
        vh = kv[:, 1, h].reshape(KV, HD)
        for rt in range(NR):
            rows = slice(rt * RT, (rt + 1) * RT)
            dl = jnp.zeros((RT, 128), F32)
            dl = jnp.sum(jnp.where(lane2 == h, delc[rows], dl), axis=1, keepdims=True)
            dp = nt(do3[h, rows], vh)
            ds0[h, rows] = pu[h, rows] * (dp - dl) * SCALE
        return 0

    cpx.wait_recv()
    a, b = ls[...], lsx[...]
    mx = jnp.maximum(a, b)
    lz[z] = mx + jnp.log(jnp.exp(a - mx) + jnp.exp(b - mx))
    for j in range(1, NZ):
        go(rc(lz.at[z], lz.at[z], sl.at[j], rl.at[j], dev(s, y, xh, up(z, j, NZ))))
    lax.fori_loop(0, HG, dprob, 0)
    for j in range(1, NZ):
        f = dn(z, j, NZ)
        rc(lz.at[f], lz.at[f], sl.at[j], rl.at[j], me).wait_recv()
    mx = lz[0]
    for j in range(1, NZ):
        mx = jnp.maximum(mx, lz[j])
    tot = jnp.exp(lz[0] - mx)
    for j in range(1, NZ):
        tot = tot + jnp.exp(lz[j] - mx)
    lt = mx + jnp.log(tot)
    for rt in range(NR):
        rows = slice(rt * RT, (rt + 1) * RT)
        tt = jnp.concatenate([lt[:, rows], jnp.zeros((120, RT), F32)], axis=0).T
        for h in range(HG):
            cc = jnp.exp(m3[h, rows] - jnp.broadcast_to(tt[:, h:h + 1], (RT, 128)))
            c3[h, rows] = cc

    def grads(h, _):
        kh = kv[:, 0, h].reshape(KV, HD)
        dkt = jnp.zeros((HD, KV), F32)
        dvt = jnp.zeros((HD, KV), F32)
        cols = pl.ds(pl.multiple_of(h * HD, HD), HD)
        for rt in range(NR):
            rows = slice(rt * RT, (rt + 1) * RT)
            cc = c3[h, rows][:, :1]
            pb = (pu[h, rows] * cc).astype(BF16)
            db = (ds0[h, rows] * cc).astype(BF16)
            dvt = dvt + tn(do3[h, rows], pb)
            dkt = dkt + tn(q3[h, rows], db)
            dq = nn(db, kh)
            for i in range(RT // ZR):
                dqa[rt * (RT // ZR) + i, :, cols] = dq[i * ZR:(i + 1) * ZR]
        for b in range(NY):
            dkv[b, 0, h] = dkt[:, b * KR:(b + 1) * KR].T
            dkv[b, 1, h] = dvt[:, b * KR:(b + 1) * KR].T
        return 0

    lax.fori_loop(0, HG, grads, 0)

    kvs[0, 0] = dkv[y2, 0].astype(BF16)
    go(rc(kvs.at[0, 0], kvr.at[0, 0], sk.at[0, 0], rk.at[0, 0], dyr))
    kvs[0, 1] = dkv[y2, 1].astype(BF16)
    go(rc(kvs.at[0, 1], kvr.at[0, 1], sk.at[0, 1], rk.at[0, 1], dyl))
    kvs[1, 1] = dkv[yr, 1].astype(BF16)
    go(rc(kvs.at[1, 1], kvr.at[1, 1], sk.at[1, 1], rk.at[1, 1], dyr))
    kvs[2, 0] = dkv[yl, 0].astype(BF16)
    go(rc(kvs.at[2, 0], kvr.at[2, 0], sk.at[2, 0], rk.at[2, 0], dyl))

    NH = NZ // 2
    HR = ZR // 2

    def qmsg(d, t):
        snd, rcv = (sqr, rqr) if d == 0 else (sql, rql)
        a_, b_ = snd.at[t - 1], rcv.at[t - 1]
        if t == NH:
            part = pl.ds(d * HR, HR)
            a_, b_ = snd.at[t - 1, part], rcv.at[t - 1, part]
        return rc(a_, b_, sg.at[d, t - 1], rg.at[d, t - 1], dzr if d == 0 else dzl)

    for t in range(NH, 0, -1):
        for d in range(2):
            snd, rcv = (sqr, rqr) if d == 0 else (sql, rql)
            dest = up(z, t, NZ) if d == 0 else dn(z, t, NZ)
            part = slice(d * HR, (d + 1) * HR)
            if t == NH:
                snd[t - 1, part] = dqa[dest, part].astype(BF16)
            else:
                qmsg(d, t + 1).wait_recv()
                if t == NH - 1:
                    rest = slice((1 - d) * HR, (2 - d) * HR)
                    snd[t - 1, rest] = dqa[dest, rest].astype(BF16)
                    snd[t - 1, part] = (dqa[dest, part] + rcv[t, part].astype(F32)).astype(BF16)
                else:
                    snd[t - 1] = (dqa[dest] + rcv[t].astype(F32)).astype(BF16)
            go(qmsg(d, t))
        if t == NH - 1:
            rc(kvr.at[0, 0], kvr.at[0, 0], sk.at[0, 0], rk.at[0, 0], me).wait_recv()
            kvs[1, 0] = (dkv[yr, 0] + kvr[0, 0].astype(F32)).astype(BF16)
            go(rc(kvs.at[1, 0], kvr.at[1, 0], sk.at[1, 0], rk.at[1, 0], dyr))
            rc(kvr.at[0, 1], kvr.at[0, 1], sk.at[0, 1], rk.at[0, 1], me).wait_recv()
            kvs[2, 1] = (dkv[yl, 1] + kvr[0, 1].astype(F32)).astype(BF16)
            go(rc(kvs.at[2, 1], kvr.at[2, 1], sk.at[2, 1], rk.at[2, 1], dyl))
    qmsg(0, 1).wait_recv()
    qmsg(1, 1).wait_recv()
    tb[...] = (dqa[z] + rqr[0].astype(F32) + rql[0].astype(F32)).reshape(NB, QR, GF)

    for j, k in others:
        ty, tx = up(y, j, NY), up(xh, k, NX)
        go(rc(tb.at[tx * NY + ty], p8.at[xh, y], s8.at[j, k], r8.at[j, k], dev(s, ty, tx, z)))
    p8[xh, y] = tb[mine]
    for j, k in others:
        fx, fy = dn(xh, k, NX), dn(y, j, NY)
        rc(p8.at[fx, fy], p8.at[fx, fy], s8.at[j, k], r8.at[j, k], me).wait_recv()
    p9s[...] = p8[0] + p8[1]
    for j in range(1, NS):
        t = up(s, j, NS)
        go(rc(p9s.at[t], p9.at[s], s9.at[j], r9.at[j], (t, c)))
    p9[s] = p9s[s]
    for j in range(1, NS):
        f = dn(s, j, NS)
        rc(p9.at[f], p9.at[f], s9.at[j], r9.at[j], me).wait_recv()
    for t in range(NS):
        dq_out[0, :, t * GF:(t + 1) * GF] = p9[t].astype(BF16)

    for a in range(2):
        rc(kvr.at[1, a], kvr.at[1, a], sk.at[1, a], rk.at[1, a], me).wait_recv()
        rc(kvr.at[2, a], kvr.at[2, a], sk.at[2, a], rk.at[2, a], me).wait_recv()
        out = dk_out if a == 0 else dv_out
        for h in range(HG):
            acc = dkv[y, a, h] + kvr[1, a, h].astype(F32) + kvr[2, a, h].astype(F32)
            out[:, h * HD:(h + 1) * HD] = acc.astype(BF16)
    for cp in sends:
        cp.wait_send()


def local(block_order, queries, cache_keys, cache_values, attention_out, output_grad):
    dma = pltpu.SemaphoreType.DMA
    vm = pltpu.VMEM
    scratch = [
        vm((NS, 16, GF), BF16), vm((NS, QR, 128), F32), vm((NS, 16, GF), BF16), vm((NS, QR, 128), F32),
        vm((NZ, NB, 16, GF), BF16), vm((NB, QR, 128), F32), vm((NZ, QR, 128), F32),
        vm((NY, 2, HG, KR, HD), BF16), vm((HG, QW, HD), BF16), vm((HG, QW, HD), BF16), vm((QW, 128), F32),
        vm((HG, QW, KV), F32), vm((HG, QW, KV), F32),
        vm((HG, QW, 128), F32), vm((HG, QW, 128), F32), vm((HG, QW, 128), F32),
        vm((8, QW), F32), vm((8, QW), F32), vm((NZ, 8, QW), F32),
        vm((NZ, ZR, GF), F32), vm((NY, 2, HG, KR, HD), F32),
        vm((4, ZR, GF), BF16), vm((4, ZR, GF), BF16), vm((4, ZR, GF), BF16), vm((4, ZR, GF), BF16),
        vm((3, 2, HG, KR, HD), BF16), vm((3, 2, HG, KR, HD), BF16),
        vm((NB, QR, GF), F32), vm((NX, NY, QR, GF), F32), vm((NS, QR, GF), F32), vm((NS, QR, GF), F32),
        dma((NS,)), dma((NS,)), dma((NS,)), dma((NS,)),
        dma((NY, NX)), dma((NY, NX)), dma((NY, NX)), dma((NY, NX)),
        dma((2, 4, 2)), dma((2, 4, 2)), dma((2, 4)), dma((2, 4)),
        dma((3, 2)), dma((3, 2)), dma((NZ,)), dma((NZ,)), dma((1,)), dma((1,)),
        dma((2, 4)), dma((2, 4)), dma((3, 2)), dma((3, 2)),
        dma((NY, NX)), dma((NY, NX)), dma((NS,)), dma((NS,)),
    ]
    vspec = pl.BlockSpec(memory_space=pltpu.VMEM)
    dq, dk, dv = pl.pallas_call(
        kernel,
        out_shape=(
            jax.ShapeDtypeStruct((1, QR, NS * GF), BF16),
            jax.ShapeDtypeStruct((KR, GF), BF16),
            jax.ShapeDtypeStruct((KR, GF), BF16),
        ),
        in_specs=[pl.BlockSpec(memory_space=pltpu.SMEM)] + [vspec] * 5,
        out_specs=(vspec, vspec, vspec),
        scratch_shapes=scratch,
        compiler_params=pltpu.CompilerParams(
            collective_id=0, has_side_effects=True, vmem_limit_bytes=56 << 20),
    )(block_order, queries, output_grad, attention_out, cache_keys, cache_values)
    return dq, dk, dv


def solution(mesh):
    in_specs = (
        P(),
        P("section", "ctx", None),
        P("ctx", "section"),
        P("ctx", "section"),
        P("section", "ctx", None),
        P("section", "ctx", None),
    )
    out_specs = (P("section", "ctx", None), P("ctx", "section"), P("ctx", "section"))
    return jax.shard_map(local, mesh=mesh, in_specs=in_specs, out_specs=out_specs, check_vma=False)
```

```python
import jax
import jax.numpy as jnp
from jax import lax
from jax.experimental import pallas as pl
from jax.experimental.pallas import tpu as pltpu
from jax.sharding import PartitionSpec as P

MESH = pl.DeviceIdType.MESH
F32 = jnp.float32
BF16 = jnp.bfloat16

NS, NY, NX, NZ = 4, 4, 2, 8
HG, HD, GF = 5, 128, 640
KR = 128
KV = NY * KR
QR = 8
NB = NX * NY
ZR = NB * QR
QW = NZ * ZR
NT = NZ // 2
SCALE = HD ** -0.5
MASKED = -1e30
RT = 128
NR = QW // RT
GROUPS = ((0, 1, 2), (3, 4))


def nt(a, b):
    return lax.dot_general(a, b, (((1,), (1,)), ((), ())), preferred_element_type=F32)


def tn(a, b):
    return lax.dot_general(a, b, (((0,), (0,)), ((), ())), preferred_element_type=F32)


def nn(a, b):
    return lax.dot_general(a, b, (((1,), (0,)), ((), ())), preferred_element_type=F32)


def kernel(order, q_in, do_in, o_in, k_in, v_in, dq_out, dk_out, dv_out,
           qv, dov, ov, kin, vin, pk, p1, g, gd, kv, q3, do3, delc, pu, ds0, m3, lse3, c3, lz,
           pbs, dbs, dqa, qs, qr, dkv, ks1, kr1, ks2, kr2, tb, p8,
           sin, s1, r1, sz, rz, szd, rzd, sy, ry, sf, rf, sl, rl, sg, rg, sk, rk, s8, r8):
    s = lax.axis_index("section")
    c = lax.axis_index("ctx")
    y = c // (NX * NZ)
    xh = (c // NZ) % NX
    z = c % NZ
    me = (s, c)
    own = s == y

    def dev(s_, y_, x_, z_):
        return (s_, (y_ * NX + x_) * NZ + z_)

    def rc(src, dst, ssem, rsem, to):
        return pltpu.make_async_remote_copy(
            src_ref=src, dst_ref=dst, send_sem=ssem, recv_sem=rsem,
            device_id=to, device_id_type=MESH)

    def arrived(dst, rsem):
        rc(dst, dst, rsem, rsem, me).wait_recv()

    def up(v, n, mod):
        return (v + n) % mod

    def dn(v, n, mod):
        return (v + mod - n) % mod

    sends = []

    def go(cp):
        cp.start()
        sends.append(cp)

    yr, yl, y2 = up(y, 1, NY), dn(y, 1, NY), up(y, 2, NY)
    bar = pltpu.get_barrier_semaphore()

    def greet(to):
        pl.semaphore_signal(bar, inc=1, device_id=to, device_id_type=MESH)

    count = 0
    for j in range(NZ):
        for k in range(NX):
            if (j, k) != (0, 0):
                greet(dev(s, y, up(xh, k, NX), up(z, j, NZ)))
                count += 1
    for t in (yr, yl):
        greet(dev(s, t, xh, z))
        count += 1
    for i in range(4):
        for k in range(NX):
            if (i, k) != (0, 0):
                greet(dev(up(s, i, NS), s, up(xh, k, NX), z))
                greet(dev(y, up(y, i, NY), up(xh, k, NX), z))
                count += 2

    @pl.when(jnp.logical_not(own))
    def _():
        greet(dev(s, s, xh, z))
        greet(dev(y, y, xh, z))

    loads = []
    for i, (a, b) in enumerate(((q_in, qv), (do_in, dov), (o_in, ov), (k_in, kin), (v_in, vin))):
        cp = pltpu.make_async_copy(a, b, sin.at[i])
        cp.start()
        loads.append(cp)
    for cp in loads:
        cp.wait()

    lane = lax.broadcasted_iota(jnp.int32, (QR, 128), 1)
    for t in range(NS):
        cols = slice(t * GF, (t + 1) * GF)
        qf = qv[0, :, cols].astype(F32)
        df = dov[0, :, cols].astype(F32)
        prod = df * ov[0, :, cols].astype(F32)
        both = jnp.concatenate([qf, df], axis=0).astype(BF16)
        tile = jnp.zeros((QR, 128), F32)
        for h in range(HG):
            pk[t, h] = both[:, h * HD:(h + 1) * HD]
            d = jnp.sum(prod[:, h * HD:(h + 1) * HD], axis=1, keepdims=True)
            tile = jnp.where(lane == h, d, tile)
        hi = tile.astype(BF16).astype(F32)
        mid = (tile - hi).astype(BF16).astype(F32)
        lo = tile - hi - mid
        pk[t, HG] = jnp.concatenate([hi + pltpu.roll(lo, QR, 1), mid], axis=0).astype(BF16)

    pl.semaphore_wait(bar, count + 2 - 2 * own.astype(jnp.int32))

    mine = xh * NY + y
    for k in range(NX):
        for i in range(NS):
            t = up(s, i, NS)
            cp = rc(pk.at[t], p1.at[mine], s1.at[i, k], r1.at[k, y], dev(t, s, up(xh, k, NX), z))
            if (i, k) == (0, 0):
                self_in = cp

                @pl.when(jnp.logical_not(own))
                def _():
                    cp.start()
            else:
                go(cp)

    @pl.when(own)
    def _():
        p1[mine] = pk[s]

    dyr, dyl = dev(s, yr, xh, z), dev(s, yl, xh, z)
    for h in range(HG):
        kv[y, h, 0] = kin[:, h * HD:(h + 1) * HD]
        kv[y, h, 1] = vin[:, h * HD:(h + 1) * HD]
        go(rc(kv.at[y, h], kv.at[y, h], sy.at[0, h], ry.at[0, h], dyr))
        go(rc(kv.at[y, h], kv.at[y, h], sy.at[1, h], ry.at[1, h], dyl))

    def kv_forward(h):
        arrived(kv.at[yl, h], ry.at[0, h])
        go(rc(kv.at[yl, h, 0], kv.at[yl, h, 0], sf.at[0, h], rf.at[0, h], dyr))
        arrived(kv.at[yr, h], ry.at[1, h])
        go(rc(kv.at[yr, h, 1], kv.at[yr, h, 1], sf.at[1, h], rf.at[1, h], dyl))

    def kv_ready(h):
        arrived(kv.at[y2, h, 0], rf.at[0, h])
        arrived(kv.at[y2, h, 1], rf.at[1, h])

    kcol = lax.broadcasted_iota(jnp.int32, (1, KV), 1)
    kblk = kcol // KR
    base = jnp.zeros((1, KV), jnp.int32)
    for b in range(NY):
        base = jnp.where(kblk == b, order[(b * NX + xh) * NZ + z], base)
    kpos = base * KR + kcol % KR
    first = NY * NX * NZ * KR - QW
    zrow = lax.broadcasted_iota(jnp.int32, (ZR, 1), 0)
    zpos = first + (((zrow // QR) % NY) * NX + zrow // (NY * QR)) * NZ * QR + zrow % QR

    for k in range(NX):
        for b in range(NY):
            slot = dn(xh, k, NX) * NY + b
            if k == 0:
                @pl.when(jnp.logical_not(own & (y == b)))
                def _():
                    arrived(p1.at[slot], r1.at[k, b])
            else:
                arrived(p1.at[slot], r1.at[k, b])
    zr, zl = up(z, 1, NZ), dn(z, 1, NZ)
    dzr, dzl = dev(s, y, xh, zr), dev(s, y, xh, zl)
    half = NB // 2

    def zref(d, t, h):
        src = dn(z, t, NZ) if d == 0 else up(z, t, NZ)
        return src, g.at[src, h]

    def zsend(d, t, h):
        _, ref = zref(d, t - 1, h)
        if t == NT:
            ref = ref.at[pl.ds(d * half, half)]
        go(rc(ref, ref, sz.at[d, t - 1, h], rz.at[d, t - 1, h], dzr if d == 0 else dzl))

    def zwait(d, t, h):
        _, ref = zref(d, t, h)
        if t == NT:
            ref = ref.at[pl.ds(d * half, half)]
        arrived(ref, rz.at[d, t - 1, h])

    def dsend(d, t):
        src, _ = zref(d, t - 1, 0)
        go(rc(gd.at[src], gd.at[src], szd.at[d, t - 1], rzd.at[d, t - 1], dzr if d == 0 else dzl))

    def dwait(d, t):
        src, _ = zref(d, t, 0)
        arrived(gd.at[src], rzd.at[d, t - 1])

    def delta_rows(zc):
        tile = gd[zc]
        for b in range(NB):
            piece = tile if b == 0 else pltpu.roll(tile, 128 - b * QR, 1)
            delc[pl.ds(pl.multiple_of(zc * ZR + b * QR, QR), QR)] = piece

    def chunks(t):
        return (z, up(z, NT, NZ)) if t == NT else (dn(z, t, NZ), up(z, t, NZ))

    def rowsof(zc):
        return pl.ds(pl.multiple_of(zc * ZR, ZR), ZR)

    def pair(ref, h, t):
        a, b = chunks(t)
        return jnp.concatenate([ref[h, rowsof(a)], ref[h, rowsof(b)]], axis=0)

    def put(ref, h, t, v):
        a, b = chunks(t)
        ref[h, rowsof(a)] = v[:ZR]
        ref[h, rowsof(b)] = v[ZR:]

    def score_tile(h, t):
        qs_ = []
        for zc in chunks(t):
            blk = g[zc, h].astype(F32).reshape(NB, 2, QR, HD)
            qc = blk[:, 0].reshape(ZR, HD).astype(BF16)
            q3[h, rowsof(zc)] = qc
            do3[h, rowsof(zc)] = blk[:, 1].reshape(ZR, HD).astype(BF16)
            qs_.append(qc)
        kh = kv[:, h, 0].reshape(KV, HD)
        sc = nt(jnp.concatenate(qs_, axis=0), kh) * SCALE
        a, b = chunks(t)
        qpos = jnp.concatenate([zpos + a * QR, zpos + b * QR], axis=0)
        sc = jnp.where(kpos <= qpos, sc, MASKED)
        m = jnp.max(sc, axis=1, keepdims=True)
        p = jnp.exp(sc - m)
        l = jnp.sum(p, axis=1, keepdims=True)
        put(pu, h, t, p)
        put(m3, h, t, jnp.broadcast_to(m, (RT, 128)))
        put(lse3, h, t, jnp.broadcast_to(m + jnp.log(l), (RT, 128)))

    def dprob_tile(h, t):
        vh = kv[:, h, 1].reshape(KV, HD)
        a, b = chunks(t)
        dl = jnp.concatenate([delc[rowsof(a)], delc[rowsof(b)]], axis=0)[:, h:h + 1]
        dp = nt(pair(do3, h, t), vh)
        put(ds0, h, t, pair(pu, h, t) * (dp - dl) * SCALE)

    lane2 = lax.broadcasted_iota(jnp.int32, (RT, 128), 1)

    def stats_send(gi):
        heads = GROUPS[gi]
        st = jnp.zeros((RT, 128), F32)
        for hi_, h in enumerate(heads):
            for rt in range(NR):
                st = jnp.where(lane2 == hi_ * NR + rt, lse3[h, rt * RT:(rt + 1) * RT], st)
        lz[gi, mz] = st.T[:16]
        for j in range(NZ):
            for k in range(NX):
                if (j, k) != (0, 0):
                    to = dev(s, y, up(xh, k, NX), up(z, j, NZ))
                    go(rc(lz.at[gi, mz], lz.at[gi, mz], sl.at[gi, k, j], rl.at[gi, k, j], to))

    mz = xh * NZ + z

    def stats_wait(gi):
        for j in range(NZ):
            for k in range(NX):
                if (j, k) != (0, 0):
                    f = dn(xh, k, NX) * NZ + dn(z, j, NZ)
                    arrived(lz.at[gi, f], rl.at[gi, k, j])
        mx = lz[gi, 0]
        for f in range(1, NX * NZ):
            mx = jnp.maximum(mx, lz[gi, f])
        tot = jnp.exp(lz[gi, 0] - mx)
        for f in range(1, NX * NZ):
            tot = tot + jnp.exp(lz[gi, f] - mx)
        lt = mx + jnp.log(tot)
        tt = jnp.concatenate([lt, jnp.zeros((112, 128), F32)], axis=0).T
        for hi_, h in enumerate(GROUPS[gi]):
            for rt in range(NR):
                rows = slice(rt * RT, (rt + 1) * RT)
                i = hi_ * NR + rt
                c3[h, rows] = jnp.exp(m3[h, rows] - jnp.broadcast_to(tt[:, i:i + 1], (RT, 128)))

    for h in range(HG):
        for b in range(NB):
            g[z, h, b] = p1[b, h]
    tile = jnp.zeros((QR, 128), F32)
    for b in range(NB):
        d2 = p1[b, HG].astype(F32)
        top = d2[:QR]
        d1 = jnp.where(lane < QR, top + d2[QR:] + pltpu.roll(top, 128 - QR, 1), 0.0)
        tile = tile + (d1 if b == 0 else pltpu.roll(d1, b * QR, 1))
    gd[z] = tile

    order_ = sorted((h + 3 * (t - 1), t, h) for t in range(1, NT + 2) for h in range(HG))
    late = []
    for _, t, h in order_:
        if t > 1:
            zwait(0, t - 1, h)
            zwait(1, t - 1, h)
        if t <= NT:
            zsend(0, t, h)
            zsend(1, t, h)
        if h == 0:
            if t > 1:
                dwait(0, t - 1)
                if t <= NT:
                    dwait(1, t - 1)
            if t <= NT:
                dsend(0, t)
                if t < NT:
                    dsend(1, t)
        if t == 1:
            kv_forward(h)
        if t > 1:
            if h == 0:
                for zc in chunks(t - 1):
                    delta_rows(zc)
            if t == 2:
                kv_ready(h)
            score_tile(h, t - 1)
            if t <= NT:
                dprob_tile(h, t - 1)
            else:
                late.append(h)
            if t == NT + 1:
                for gi, heads in enumerate(GROUPS):
                    if h == heads[-1]:
                        stats_send(gi)
                        for hh in late:
                            dprob_tile(hh, NT)
                        late = []

    def grads(h):
        kh = kv[:, h, 0].reshape(KV, HD)
        for rt in range(NR):
            rows = slice(rt * RT, (rt + 1) * RT)
            cc = c3[h, rows][:, :1]
            pbs[rows] = (pu[h, rows] * cc).astype(BF16)
            dbs[rows] = (ds0[h, rows] * cc).astype(BF16)
        dq = nn(dbs[...], kh)
        dqa[h] = dq.reshape(NZ, ZR, HD)
        qs[h] = dq.reshape(NZ, ZR, HD).astype(BF16)
        for j in range(1, NZ):
            t = up(z, j, NZ)
            go(rc(qs.at[h, t], qr.at[h, z], sg.at[h, j], rg.at[h, j], dev(s, y, xh, t)))
        dkt = tn(q3[h], dbs[...])
        dvt = tn(do3[h], pbs[...])
        for b in range(NY):
            dkv[h, b, 0] = dkt[:, b * KR:(b + 1) * KR].T
            dkv[h, b, 1] = dvt[:, b * KR:(b + 1) * KR].T
        ks1[h, 0, 0] = dkv[h, y2, 0].astype(BF16)
        ks1[h, 0, 1] = dkv[h, yr, 1].astype(BF16)
        ks1[h, 1, 0] = dkv[h, y2, 1].astype(BF16)
        ks1[h, 1, 1] = dkv[h, yl, 0].astype(BF16)
        go(rc(ks1.at[h, 0], kr1.at[h, 0], sk.at[0, 0, h], rk.at[0, 0, h], dyr))
        go(rc(ks1.at[h, 1], kr1.at[h, 1], sk.at[0, 1, h], rk.at[0, 1, h], dyl))

    def second_leg(h):
        arrived(kr1.at[h, 0], rk.at[0, 0, h])
        ks2[h, 0] = (dkv[h, yr, 0] + kr1[h, 0, 0].astype(F32)).astype(BF16)
        go(rc(ks2.at[h, 0], kr2.at[h, 0], sk.at[1, 0, h], rk.at[1, 0, h], dyr))
        arrived(kr1.at[h, 1], rk.at[0, 1, h])
        ks2[h, 1] = (dkv[h, yl, 1] + kr1[h, 1, 0].astype(F32)).astype(BF16)
        go(rc(ks2.at[h, 1], kr2.at[h, 1], sk.at[1, 1, h], rk.at[1, 1, h], dyl))

    def query_sum(h):
        acc = dqa[h, z]
        for j in range(1, NZ):
            f = dn(z, j, NZ)
            arrived(qr.at[h, f], rg.at[h, j])
            acc = acc + qr[h, f].astype(F32)
        tb[:, h] = acc.reshape(NB, QR, HD)

    def cache_out(h):
        arrived(kr2.at[h, 0], rk.at[1, 0, h])
        arrived(kr2.at[h, 1], rk.at[1, 1, h])
        cols = slice(h * HD, (h + 1) * HD)
        dk_out[:, cols] = (dkv[h, y, 0] + kr1[h, 1, 1].astype(F32) + kr2[h, 0].astype(F32)).astype(BF16)
        dv_out[:, cols] = (dkv[h, y, 1] + kr1[h, 0, 1].astype(F32) + kr2[h, 1].astype(F32)).astype(BF16)

    for gi, heads in enumerate(GROUPS):
        stats_wait(gi)
        for h in heads:
            grads(h)
            if h > 0:
                second_leg(h - 1)
                query_sum(h - 1)
    second_leg(HG - 1)
    query_sum(HG - 1)

    for j in range(NY):
        for k in range(NX):
            ty, tx = up(y, j, NY), up(xh, k, NX)
            cp = rc(tb.at[tx * NY + ty], p8.at[k, s], s8.at[j, k], r8.at[k, s], dev(y, ty, tx, z))
            if (j, k) == (0, 0):
                self_out = cp

                @pl.when(jnp.logical_not(own))
                def _():
                    cp.start()
            else:
                go(cp)

    @pl.when(own)
    def _():
        p8[0, s] = tb[mine]

    for h in range(HG):
        cache_out(h)

    for k in range(NX):
        for b in range(NS):
            if k == 0:
                @pl.when(jnp.logical_not(own & (s == b)))
                def _():
                    arrived(p8.at[k, b], r8.at[k, b])
            else:
                arrived(p8.at[k, b], r8.at[k, b])
    for b in range(NS):
        for h in range(HG):
            col = b * GF + h * HD
            dq_out[0, :, col:col + HD] = (p8[0, b, h] + p8[1, b, h]).astype(BF16)

    @pl.when(jnp.logical_not(own))
    def _():
        self_in.wait_send()
        self_out.wait_send()

    for cp in sends:
        cp.wait_send()


def local(block_order, queries, cache_keys, cache_values, attention_out, output_grad):
    dma = pltpu.SemaphoreType.DMA
    vm = pltpu.VMEM
    row = queries.shape
    scratch = [
        vm(row, BF16), vm(row, BF16), vm(row, BF16), vm((KR, GF), BF16), vm((KR, GF), BF16),
        vm((NS, HG + 1, 16, HD), BF16), vm((NB, HG + 1, 16, HD), BF16),
        vm((NZ, HG, NB, 16, HD), BF16), vm((NZ, QR, 128), F32),
        vm((NY, HG, 2, KR, HD), BF16), vm((HG, QW, HD), BF16), vm((HG, QW, HD), BF16), vm((QW, 128), F32),
        vm((HG, QW, KV), F32), vm((HG, QW, KV), F32),
        vm((HG, QW, 128), F32), vm((HG, QW, 128), F32), vm((HG, QW, 128), F32),
        vm((2, NX * NZ, 16, 128), F32),
        vm((QW, KV), BF16), vm((QW, KV), BF16),
        vm((HG, NZ, ZR, HD), F32), vm((HG, NZ, ZR, HD), BF16), vm((HG, NZ, ZR, HD), BF16),
        vm((HG, NY, 2, KR, HD), F32),
        vm((HG, 2, 2, KR, HD), BF16), vm((HG, 2, 2, KR, HD), BF16),
        vm((HG, 2, KR, HD), BF16), vm((HG, 2, KR, HD), BF16),
        vm((NB, HG, QR, HD), F32), vm((NX, NS, HG, QR, HD), F32),
        dma((5,)), dma((NS, NX)), dma((NX, NY)),
        dma((2, NT, HG)), dma((2, NT, HG)), dma((2, NT)), dma((2, NT)),
        dma((2, HG)), dma((2, HG)), dma((2, HG)), dma((2, HG)),
        dma((2, NX, NZ)), dma((2, NX, NZ)), dma((HG, NZ)), dma((HG, NZ)),
        dma((2, 2, HG)), dma((2, 2, HG)), dma((NY, NX)), dma((NX, NS)),
    ]
    vspec = pl.BlockSpec(memory_space=pltpu.VMEM)
    hbm = pl.BlockSpec(memory_space=pl.ANY)
    dq, dk, dv = pl.pallas_call(
        kernel,
        out_shape=(
            jax.ShapeDtypeStruct((1, QR, NS * GF), BF16),
            jax.ShapeDtypeStruct((KR, GF), BF16),
            jax.ShapeDtypeStruct((KR, GF), BF16),
        ),
        in_specs=[pl.BlockSpec(memory_space=pltpu.SMEM)] + [hbm] * 5,
        out_specs=(vspec, vspec, vspec),
        scratch_shapes=scratch,
        compiler_params=pltpu.CompilerParams(
            collective_id=0, has_side_effects=True, vmem_limit_bytes=56 << 20),
    )(block_order, queries, output_grad, attention_out, cache_keys, cache_values)
    return dq, dk, dv


def solution(mesh):
    in_specs = (
        P(),
        P("section", "ctx", None),
        P("ctx", "section"),
        P("ctx", "section"),
        P("section", "ctx", None),
        P("section", "ctx", None),
    )
    out_specs = (P("section", "ctx", None), P("ctx", "section"), P("ctx", "section"))
    return jax.shard_map(local, mesh=mesh, in_specs=in_specs, out_specs=out_specs, check_vma=False)
```

```python
import jax
import jax.numpy as jnp
from jax import lax
from jax.experimental import pallas as pl
from jax.experimental.pallas import tpu as pltpu
from jax.sharding import PartitionSpec as P

MESH = pl.DeviceIdType.MESH
F32 = jnp.float32
BF16 = jnp.bfloat16

NS, NY, NX, NZ = 4, 4, 2, 8
HG, HD, GF = 5, 128, 640
KR = 128
KV = NY * KR
QR = 8
NB = NX * NY
ZR = NB * QR
QW = NZ * ZR
NT = NZ // 2
SCALE = HD ** -0.5
MASKED = -1e30
RT = 128
NR = QW // RT
GROUPS = ((0, 1, 2), (3, 4))


def nt(a, b):
    return lax.dot_general(a, b, (((1,), (1,)), ((), ())), preferred_element_type=F32)


def tn(a, b):
    return lax.dot_general(a, b, (((0,), (0,)), ((), ())), preferred_element_type=F32)


def nn(a, b):
    return lax.dot_general(a, b, (((1,), (0,)), ((), ())), preferred_element_type=F32)


def kernel(order, q_in, do_in, o_in, k_in, v_in, dq_out, dk_out, dv_out,
           qv, dov, ov, kin, vin, pk, p1, g, gd, kv, q3, do3, delc, pl_, pb, db, m3, lse3, c3, lz,
           dqa, zs, zr_, dkv, ks1, kr1, ks2, kr2, tb, p8,
           sin, s1, r1, sz, rz, szd, rzd, sy, ry, sf, rf, sl, rl, sg, rg, sk, rk, s8, r8):
    s = lax.axis_index("section")
    c = lax.axis_index("ctx")
    y = c >> 4
    xh = (c >> 3) & 1
    z = c & 7
    me = (s, c)
    own = s == y

    def dev(s_, y_, x_, z_):
        return (s_, (y_ << 4) | (x_ << 3) | z_)

    def rc(src, dst, ssem, rsem, to):
        return pltpu.make_async_remote_copy(
            src_ref=src, dst_ref=dst, send_sem=ssem, recv_sem=rsem,
            device_id=to, device_id_type=MESH)

    def arrived(dst, rsem):
        rc(dst, dst, rsem, rsem, me).wait_recv()

    def up(v, n, mod):
        return (v + n) & (mod - 1)

    def dn(v, n, mod):
        return (v - n) & (mod - 1)

    sends = []

    def go(cp):
        cp.start()
        sends.append(cp)

    loads = []
    for i, (a, b) in enumerate(((q_in, qv), (do_in, dov), (o_in, ov), (k_in, kin), (v_in, vin))):
        cp = pltpu.make_async_copy(a, b, sin.at[i])
        cp.start()
        loads.append(cp)

    yr, yl, y2 = up(y, 1, NY), dn(y, 1, NY), up(y, 2, NY)
    bar = pltpu.get_barrier_semaphore()

    def greet(to):
        pl.semaphore_signal(bar, inc=1, device_id=to, device_id_type=MESH)

    count = 0
    for j in range(NZ):
        for k in range(NX):
            if (j, k) != (0, 0):
                greet(dev(s, y, up(xh, k, NX), up(z, j, NZ)))
                count += 1
    for t in (yr, yl):
        greet(dev(s, t, xh, z))
        count += 1
    for i in range(4):
        for k in range(NX):
            if (i, k) != (0, 0):
                greet(dev(up(s, i, NS), s, up(xh, k, NX), z))
                greet(dev(y, up(y, i, NY), up(xh, k, NX), z))
                count += 2

    @pl.when(jnp.logical_not(own))
    def _():
        greet(dev(s, s, xh, z))
        greet(dev(y, y, xh, z))

    for cp in loads:
        cp.wait()

    lane = lax.broadcasted_iota(jnp.int32, (QR, 128), 1)
    for t in range(NS):
        cols = slice(t * GF, (t + 1) * GF)
        qf = qv[0, :, cols].astype(F32)
        df = dov[0, :, cols].astype(F32)
        prod = df * ov[0, :, cols].astype(F32)
        both = jnp.concatenate([qf, df], axis=0).astype(BF16)
        tile = jnp.zeros((QR, 128), F32)
        for h in range(HG):
            pk[t, h] = both[:, h * HD:(h + 1) * HD]
            d = jnp.sum(prod[:, h * HD:(h + 1) * HD], axis=1, keepdims=True)
            tile = jnp.where(lane == h, d, tile)
        hi = tile.astype(BF16).astype(F32)
        mid = (tile - hi).astype(BF16).astype(F32)
        lo = tile - hi - mid
        pk[t, HG] = jnp.concatenate([hi + pltpu.roll(lo, QR, 1), mid], axis=0).astype(BF16)

    pl.semaphore_wait(bar, count + 2 - 2 * own.astype(jnp.int32))

    mine = xh * NY + y
    for k in range(NX):
        for i in range(NS):
            t = up(s, i, NS)
            cp = rc(pk.at[t], p1.at[mine], s1.at[i, k], r1.at[k, y], dev(t, s, up(xh, k, NX), z))
            if (i, k) == (0, 0):
                self_in = cp

                @pl.when(jnp.logical_not(own))
                def _():
                    cp.start()
            else:
                go(cp)

    @pl.when(own)
    def _():
        p1[mine] = pk[s]

    dyr, dyl = dev(s, yr, xh, z), dev(s, yl, xh, z)
    for h in range(HG):
        kv[y, h, 0] = kin[:, h * HD:(h + 1) * HD]
        kv[y, h, 1] = vin[:, h * HD:(h + 1) * HD]
        go(rc(kv.at[y, h], kv.at[y, h], sy.at[0, h], ry.at[0, h], dyr))
        go(rc(kv.at[y, h], kv.at[y, h], sy.at[1, h], ry.at[1, h], dyl))

    def kv_forward(h):
        arrived(kv.at[yl, h], ry.at[0, h])
        go(rc(kv.at[yl, h, 0], kv.at[yl, h, 0], sf.at[0, h], rf.at[0, h], dyr))
        arrived(kv.at[yr, h], ry.at[1, h])
        go(rc(kv.at[yr, h, 1], kv.at[yr, h, 1], sf.at[1, h], rf.at[1, h], dyl))

    def kv_ready(h):
        arrived(kv.at[y2, h, 0], rf.at[0, h])
        arrived(kv.at[y2, h, 1], rf.at[1, h])

    kcol = lax.broadcasted_iota(jnp.int32, (1, KV), 1)
    kblk = kcol // KR
    base = jnp.zeros((1, KV), jnp.int32)
    for b in range(NY):
        base = jnp.where(kblk == b, order[(b * NX + xh) * NZ + z], base)
    kpos = base * KR + kcol % KR
    first = NY * NX * NZ * KR - QW
    zrow = lax.broadcasted_iota(jnp.int32, (ZR, 1), 0)
    zpos = first + (((zrow // QR) % NY) * NX + zrow // (NY * QR)) * NZ * QR + zrow % QR

    for k in range(NX):
        for b in range(NY):
            slot = dn(xh, k, NX) * NY + b
            if k == 0:
                @pl.when(jnp.logical_not(own & (y == b)))
                def _():
                    arrived(p1.at[slot], r1.at[k, b])
            else:
                arrived(p1.at[slot], r1.at[k, b])
    zr, zl = up(z, 1, NZ), dn(z, 1, NZ)
    dzr, dzl = dev(s, y, xh, zr), dev(s, y, xh, zl)
    half = NB // 2

    def zref(d, t, h):
        src = dn(z, t, NZ) if d == 0 else up(z, t, NZ)
        return src, g.at[src, h]

    def zsend(d, t, h):
        _, ref = zref(d, t - 1, h)
        if t == NT:
            ref = ref.at[pl.ds(d * half, half)]
        go(rc(ref, ref, sz.at[d, t - 1, h], rz.at[d, t - 1, h], dzr if d == 0 else dzl))

    def zwait(d, t, h):
        _, ref = zref(d, t, h)
        if t == NT:
            ref = ref.at[pl.ds(d * half, half)]
        arrived(ref, rz.at[d, t - 1, h])

    def dsend(d, t):
        src, _ = zref(d, t - 1, 0)
        go(rc(gd.at[src], gd.at[src], szd.at[d, t - 1], rzd.at[d, t - 1], dzr if d == 0 else dzl))

    def dwait(d, t):
        src, _ = zref(d, t, 0)
        arrived(gd.at[src], rzd.at[d, t - 1])

    def delta_rows(zc):
        tile = gd[zc]
        for b in range(NB):
            piece = tile if b == 0 else pltpu.roll(tile, 128 - b * QR, 1)
            delc[pl.ds(pl.multiple_of(zc * ZR + b * QR, QR), QR)] = piece

    def chunks(t):
        return (z, up(z, NT, NZ)) if t == NT else (dn(z, t, NZ), up(z, t, NZ))

    def rowsof(zc):
        return pl.ds(pl.multiple_of(zc * ZR, ZR), ZR)

    def pair(ref, h, t):
        a, b = chunks(t)
        return jnp.concatenate([ref[h, rowsof(a)], ref[h, rowsof(b)]], axis=0)

    def put(ref, h, t, v):
        a, b = chunks(t)
        ref[h, rowsof(a)] = v[:ZR]
        ref[h, rowsof(b)] = v[ZR:]

    def score_tile(h, t):
        qs_, ds_ = [], []
        for zc in chunks(t):
            blk = g[zc, h].astype(F32).reshape(NB, 2, QR, HD)
            qc = blk[:, 0].reshape(ZR, HD).astype(BF16)
            dc = blk[:, 1].reshape(ZR, HD).astype(BF16)
            q3[h, rowsof(zc)] = qc
            do3[h, rowsof(zc)] = dc
            qs_.append(qc)
            ds_.append(dc)
        kh = kv[:, h, 0].reshape(KV, HD)
        sc = nt(jnp.concatenate(qs_, axis=0), kh) * SCALE
        a, b = chunks(t)
        qpos = jnp.concatenate([zpos + a * QR, zpos + b * QR], axis=0)
        sc = jnp.where(kpos <= qpos, sc, MASKED)
        m = jnp.max(sc, axis=1, keepdims=True)
        p = jnp.exp(sc - m)
        l = jnp.sum(p, axis=1, keepdims=True)
        put(pb, h, t, p.astype(BF16))
        put(m3, h, t, jnp.broadcast_to(m, (RT, 128)))
        put(lse3, h, t, jnp.broadcast_to(m + jnp.log(l), (RT, 128)))
        if t == NT:
            pl_[h] = p
        else:
            dprob(h, t, p, jnp.concatenate(ds_, axis=0))

    def dprob(h, t, p, dom):
        vh = kv[:, h, 1].reshape(KV, HD)
        a, b = chunks(t)
        dl = jnp.concatenate([delc[rowsof(a)], delc[rowsof(b)]], axis=0)[:, h:h + 1]
        put(db, h, t, (p * (nt(dom, vh) - dl) * SCALE).astype(BF16))

    def dprob_late(h):
        dprob(h, NT, pl_[h], pair(do3, h, NT))
        kh = kv[:, h, 0].reshape(KV, HD)
        dqa[h] = nn(db[h], kh).reshape(NZ, ZR, HD)

    lane2 = lax.broadcasted_iota(jnp.int32, (RT, 128), 1)

    def stats_send(gi):
        heads = GROUPS[gi]
        st = jnp.zeros((RT, 128), F32)
        for hi_, h in enumerate(heads):
            for rt in range(NR):
                st = jnp.where(lane2 == hi_ * NR + rt, lse3[h, rt * RT:(rt + 1) * RT], st)
        lz[gi, mz] = st.T[:16]
        for j in range(NZ):
            for k in range(NX):
                if (j, k) != (0, 0):
                    to = dev(s, y, up(xh, k, NX), up(z, j, NZ))
                    go(rc(lz.at[gi, mz], lz.at[gi, mz], sl.at[gi, k, j], rl.at[gi, k, j], to))

    mz = xh * NZ + z

    def stats_wait(gi):
        for j in range(NZ):
            for k in range(NX):
                if (j, k) != (0, 0):
                    f = dn(xh, k, NX) * NZ + dn(z, j, NZ)
                    arrived(lz.at[gi, f], rl.at[gi, k, j])
        mx = lz[gi, 0]
        for f in range(1, NX * NZ):
            mx = jnp.maximum(mx, lz[gi, f])
        tot = jnp.exp(lz[gi, 0] - mx)
        for f in range(1, NX * NZ):
            tot = tot + jnp.exp(lz[gi, f] - mx)
        lt = mx + jnp.log(tot)
        tt = jnp.concatenate([lt, jnp.zeros((112, 128), F32)], axis=0).T
        for hi_, h in enumerate(GROUPS[gi]):
            for rt in range(NR):
                rows = slice(rt * RT, (rt + 1) * RT)
                i = hi_ * NR + rt
                c3[h, rows] = jnp.exp(m3[h, rows] - jnp.broadcast_to(tt[:, i:i + 1], (RT, 128)))

    for h in range(HG):
        for b in range(NB):
            g[z, h, b] = p1[b, h]
    tile = jnp.zeros((QR, 128), F32)
    for b in range(NB):
        d2 = p1[b, HG].astype(F32)
        top = d2[:QR]
        d1 = jnp.where(lane < QR, top + d2[QR:] + pltpu.roll(top, 128 - QR, 1), 0.0)
        tile = tile + (d1 if b == 0 else pltpu.roll(d1, b * QR, 1))
    gd[z] = tile

    for h in range(HG):
        zsend(0, 1, h)
        zsend(1, 1, h)
    dsend(0, 1)
    dsend(1, 1)
    kv_forward(0)
    kv_forward(1)
    late = []
    for t in range(2, NT + 2):
        for h in range(HG):
            zwait(0, t - 1, h)
            zwait(1, t - 1, h)
            if t <= NT:
                zsend(0, t, h)
                zsend(1, t, h)
            if h == 0:
                dwait(0, t - 1)
                if t <= NT:
                    dwait(1, t - 1)
                    dsend(0, t)
                    if t < NT:
                        dsend(1, t)
                for zc in chunks(t - 1):
                    delta_rows(zc)
            if t == 2:
                if h + 2 < HG:
                    kv_forward(h + 2)
                kv_ready(h)
            score_tile(h, t - 1)
            if t == NT + 1:
                late.append(h)
                for gi, heads in enumerate(GROUPS):
                    if h == heads[-1]:
                        stats_send(gi)
                        for hh in late:
                            dprob_late(hh)
                        late = []

    HR = ZR // 2
    dz2r, dz2l = dev(s, y, xh, up(z, 2, NZ)), dev(s, y, xh, dn(z, 2, NZ))

    def zmsg(gi, d, kind):
        heads = GROUPS[gi]
        hs = pl.ds(heads[0], len(heads))
        a_, b_ = zs.at[d, kind, hs], zr_.at[d, kind, hs]
        if kind == 0:
            part = pl.ds(d * HR, HR)
            a_, b_ = zs.at[d, kind, hs, part], zr_.at[d, kind, hs, part]
        near, far = (dzr, dz2r) if d == 0 else (dzl, dz2l)
        return rc(a_, b_, sg.at[gi, d, kind], rg.at[gi, d, kind], far if kind in (0, 3) else near)

    def step(d, n):
        return up(z, n, NZ) if d == 0 else dn(z, n, NZ)

    def query_grads(gi):
        for h in GROUPS[gi]:
            dqa[h] = dqa[h] * c3[h].reshape(NZ, ZR, HD)
        for kind, n in ((0, 4), (1, 3), (2, 1)):
            for d in range(2):
                for h in GROUPS[gi]:
                    if kind == 0:
                        part = slice(d * HR, (d + 1) * HR)
                        zs[d, kind, h, part] = dqa[h, step(d, n), part].astype(BF16)
                    else:
                        zs[d, kind, h] = dqa[h, step(d, n)].astype(BF16)
                go(zmsg(gi, d, kind))

    def query_relay(gi):
        for d in range(2):
            zmsg(gi, d, 0).wait_recv()
            zmsg(gi, d, 1).wait_recv()
            part = slice(d * HR, (d + 1) * HR)
            rest = slice((1 - d) * HR, (2 - d) * HR)
            for h in GROUPS[gi]:
                acc = dqa[h, step(d, 2)] + zr_[d, 1, h].astype(F32)
                zs[d, 3, h, rest] = acc[rest].astype(BF16)
                zs[d, 3, h, part] = (acc[part] + zr_[d, 0, h, part].astype(F32)).astype(BF16)
            go(zmsg(gi, d, 3))

    def query_sum(gi):
        for d in range(2):
            zmsg(gi, d, 2).wait_recv()
            zmsg(gi, d, 3).wait_recv()
        for h in GROUPS[gi]:
            acc = dqa[h, z]
            for d in range(2):
                acc = acc + zr_[d, 2, h].astype(F32) + zr_[d, 3, h].astype(F32)
            tb[:, h] = acc.reshape(NB, QR, HD)

    def cache_grads(h):
        cc = c3[h]
        dkt = tn((q3[h].astype(F32) * cc).astype(BF16), db[h])
        dvt = tn((do3[h].astype(F32) * cc).astype(BF16), pb[h])
        for b in range(NY):
            dkv[h, b, 0] = dkt[:, b * KR:(b + 1) * KR].T
            dkv[h, b, 1] = dvt[:, b * KR:(b + 1) * KR].T
        ks1[h, 0, 0] = dkv[h, y2, 0].astype(BF16)
        ks1[h, 0, 1] = dkv[h, yr, 1].astype(BF16)
        ks1[h, 1, 0] = dkv[h, y2, 1].astype(BF16)
        ks1[h, 1, 1] = dkv[h, yl, 0].astype(BF16)
        go(rc(ks1.at[h, 0], kr1.at[h, 0], sk.at[0, 0, h], rk.at[0, 0, h], dyr))
        go(rc(ks1.at[h, 1], kr1.at[h, 1], sk.at[0, 1, h], rk.at[0, 1, h], dyl))

    def second_leg(h):
        arrived(kr1.at[h, 0], rk.at[0, 0, h])
        ks2[h, 0] = (dkv[h, yr, 0] + kr1[h, 0, 0].astype(F32)).astype(BF16)
        go(rc(ks2.at[h, 0], kr2.at[h, 0], sk.at[1, 0, h], rk.at[1, 0, h], dyr))
        arrived(kr1.at[h, 1], rk.at[0, 1, h])
        ks2[h, 1] = (dkv[h, yl, 1] + kr1[h, 1, 0].astype(F32)).astype(BF16)
        go(rc(ks2.at[h, 1], kr2.at[h, 1], sk.at[1, 1, h], rk.at[1, 1, h], dyl))

    def cache_out(h):
        arrived(kr2.at[h, 0], rk.at[1, 0, h])
        arrived(kr2.at[h, 1], rk.at[1, 1, h])
        cols = slice(h * HD, (h + 1) * HD)
        dk_out[:, cols] = (dkv[h, y, 0] + kr1[h, 1, 1].astype(F32) + kr2[h, 0].astype(F32)).astype(BF16)
        dv_out[:, cols] = (dkv[h, y, 1] + kr1[h, 0, 1].astype(F32) + kr2[h, 1].astype(F32)).astype(BF16)

    stats_wait(0)
    query_grads(0)
    cache_grads(0)
    cache_grads(1)
    cache_grads(2)
    second_leg(0)
    query_relay(0)
    stats_wait(1)
    query_grads(1)
    second_leg(1)
    cache_grads(3)
    second_leg(2)
    cache_grads(4)
    query_sum(0)
    query_relay(1)
    second_leg(3)
    second_leg(4)
    query_sum(1)

    for j in range(NY):
        for k in range(NX):
            ty, tx = up(y, j, NY), up(xh, k, NX)
            cp = rc(tb.at[tx * NY + ty], p8.at[k, s], s8.at[j, k], r8.at[k, s], dev(y, ty, tx, z))
            if (j, k) == (0, 0):
                self_out = cp

                @pl.when(jnp.logical_not(own))
                def _():
                    cp.start()
            else:
                go(cp)

    @pl.when(own)
    def _():
        p8[0, s] = tb[mine]

    for h in range(HG):
        cache_out(h)

    for k in range(NX):
        for b in range(NS):
            if k == 0:
                @pl.when(jnp.logical_not(own & (s == b)))
                def _():
                    arrived(p8.at[k, b], r8.at[k, b])
            else:
                arrived(p8.at[k, b], r8.at[k, b])
    for b in range(NS):
        for h in range(HG):
            col = b * GF + h * HD
            dq_out[0, :, col:col + HD] = (p8[0, b, h] + p8[1, b, h]).astype(BF16)

    @pl.when(jnp.logical_not(own))
    def _():
        self_in.wait_send()
        self_out.wait_send()

    for cp in sends:
        cp.wait_send()


def place(a, b, c, x, y, z):
    x[...] = a[...]
    y[...] = b[...]
    z[...] = c[...]


def local(block_order, queries, cache_keys, cache_values, attention_out, output_grad):
    dma = pltpu.SemaphoreType.DMA
    vm = pltpu.VMEM
    row = queries.shape
    scratch = [
        vm(row, BF16), vm(row, BF16), vm(row, BF16), vm((KR, GF), BF16), vm((KR, GF), BF16),
        vm((NS, HG + 1, 16, HD), BF16), vm((NB, HG + 1, 16, HD), BF16),
        vm((NZ, HG, NB, 16, HD), BF16), vm((NZ, QR, 128), F32),
        vm((NY, HG, 2, KR, HD), BF16), vm((HG, QW, HD), BF16), vm((HG, QW, HD), BF16), vm((QW, 128), F32),
        vm((HG, RT, KV), F32), vm((HG, QW, KV), BF16), vm((HG, QW, KV), BF16),
        vm((HG, QW, 128), F32), vm((HG, QW, 128), F32), vm((HG, QW, 128), F32),
        vm((2, NX * NZ, 16, 128), F32),
        vm((HG, NZ, ZR, HD), F32), vm((2, 4, HG, ZR, HD), BF16), vm((2, 4, HG, ZR, HD), BF16),
        vm((HG, NY, 2, KR, HD), F32),
        vm((HG, 2, 2, KR, HD), BF16), vm((HG, 2, 2, KR, HD), BF16),
        vm((HG, 2, KR, HD), BF16), vm((HG, 2, KR, HD), BF16),
        vm((NB, HG, QR, HD), F32), vm((NX, NS, HG, QR, HD), F32),
        dma((5,)), dma((NS, NX)), dma((NX, NY)),
        dma((2, NT, HG)), dma((2, NT, HG)), dma((2, NT)), dma((2, NT)),
        dma((2, HG)), dma((2, HG)), dma((2, HG)), dma((2, HG)),
        dma((2, NX, NZ)), dma((2, NX, NZ)), dma((2, 2, 4)), dma((2, 2, 4)),
        dma((2, 2, HG)), dma((2, 2, HG)), dma((NY, NX)), dma((NX, NS)),
    ]
    vspec = pl.BlockSpec(memory_space=pltpu.VMEM)
    hbm = pl.BlockSpec(memory_space=pl.ANY)
    dq, dk, dv = pl.pallas_call(
        kernel,
        out_shape=(
            jax.ShapeDtypeStruct((1, QR, NS * GF), BF16),
            jax.ShapeDtypeStruct((KR, GF), BF16),
            jax.ShapeDtypeStruct((KR, GF), BF16),
        ),
        in_specs=[pl.BlockSpec(memory_space=pltpu.SMEM)] + [hbm] * 5,
        out_specs=(vspec, vspec, vspec),
        scratch_shapes=scratch,
        compiler_params=pltpu.CompilerParams(
            collective_id=0, has_side_effects=True, vmem_limit_bytes=56 << 20),
    )(block_order, queries, output_grad, attention_out, cache_keys, cache_values)
    return pl.pallas_call(
        place,
        out_shape=tuple(jax.ShapeDtypeStruct(v.shape, v.dtype) for v in (dq, dk, dv)),
        in_specs=[vspec] * 3,
        out_specs=(vspec,) * 3,
    )(dq, dk, dv)


def solution(mesh):
    in_specs = (
        P(),
        P("section", "ctx", None),
        P("ctx", "section"),
        P("ctx", "section"),
        P("section", "ctx", None),
        P("section", "ctx", None),
    )
    out_specs = (P("section", "ctx", None), P("ctx", "section"), P("ctx", "section"))
    return jax.shard_map(local, mesh=mesh, in_specs=in_specs, out_specs=out_specs, check_vma=False)
```

```python
import jax
import jax.numpy as jnp
from jax import lax
from jax.experimental import pallas as pl
from jax.experimental.pallas import tpu as pltpu
from jax.sharding import PartitionSpec as P

MESH = pl.DeviceIdType.MESH
F32 = jnp.float32
BF16 = jnp.bfloat16

NS, NY, NX, NZ = 4, 4, 2, 8
HG, HD, GF = 5, 128, 640
KR = 128
KV = NY * KR
QR = 8
NB = NX * NY
ZR = NB * QR
QW = NZ * ZR
NT = NZ // 2
SCALE = HD ** -0.5
MASKED = -1e30
RT = 128
NR = QW // RT
PIECES = ((0, 2), (2, 3))
SR = 24


def nt(a, b):
    return lax.dot_general(a, b, (((1,), (1,)), ((), ())), preferred_element_type=F32)


def tn(a, b):
    return lax.dot_general(a, b, (((0,), (0,)), ((), ())), preferred_element_type=F32)


def nn(a, b):
    return lax.dot_general(a, b, (((1,), (0,)), ((), ())), preferred_element_type=F32)


def kernel(order, q_in, do_in, o_in, k_in, v_in, dq_out, dk_out, dv_out,
           qv, dov, ov, kin, vin, pk, p1, g, gd, kv, q3, do3, delc, pl_, pb, db, m3, lse3, c3, w3, lz, wt,
           dqa, zs, zr_, dkv, ks1, kr1, ks2, kr2, tb, p8,
           sin, s1, r1, sz, rz, szd, rzd, sy, ry, sf, rf, sl, rl, sg, rg, sk, rk, s8, r8):
    s = lax.axis_index("section")
    c = lax.axis_index("ctx")
    y = c >> 4
    xh = (c >> 3) & 1
    z = c & 7
    me = (s, c)
    own = s == y

    def dev(s_, y_, x_, z_):
        return (s_, (y_ << 4) | (x_ << 3) | z_)

    def rc(src, dst, ssem, rsem, to):
        return pltpu.make_async_remote_copy(
            src_ref=src, dst_ref=dst, send_sem=ssem, recv_sem=rsem,
            device_id=to, device_id_type=MESH)

    def arrived(dst, rsem):
        rc(dst, dst, rsem, rsem, me).wait_recv()

    def up(v, n, mod):
        return (v + n) & (mod - 1)

    def dn(v, n, mod):
        return (v - n) & (mod - 1)

    sends = []

    def go(cp):
        cp.start()
        sends.append(cp)

    loads = []
    for i, (a, b) in enumerate(((q_in, qv), (do_in, dov), (o_in, ov), (k_in, kin), (v_in, vin))):
        cp = pltpu.make_async_copy(a, b, sin.at[i])
        cp.start()
        loads.append(cp)

    yr, yl, y2 = up(y, 1, NY), dn(y, 1, NY), up(y, 2, NY)
    bar = pltpu.get_barrier_semaphore()

    def greet(to):
        pl.semaphore_signal(bar, inc=1, device_id=to, device_id_type=MESH)

    count = 0
    for j in range(NZ):
        for k in range(NX):
            if (j, k) != (0, 0):
                greet(dev(s, y, up(xh, k, NX), up(z, j, NZ)))
                count += 1
    for t in (yr, yl):
        greet(dev(s, t, xh, z))
        count += 1
    for i in range(4):
        for k in range(NX):
            if (i, k) != (0, 0):
                greet(dev(up(s, i, NS), s, up(xh, k, NX), z))
                greet(dev(y, up(y, i, NY), up(xh, k, NX), z))
                count += 2

    @pl.when(jnp.logical_not(own))
    def _():
        greet(dev(s, s, xh, z))
        greet(dev(y, y, xh, z))

    for cp in loads:
        cp.wait()

    lane = lax.broadcasted_iota(jnp.int32, (QR, 128), 1)
    for t in range(NS):
        cols = slice(t * GF, (t + 1) * GF)
        qf = qv[0, :, cols].astype(F32)
        df = dov[0, :, cols].astype(F32)
        prod = df * ov[0, :, cols].astype(F32)
        both = jnp.concatenate([qf, df], axis=0).astype(BF16)
        tile = jnp.zeros((QR, 128), F32)
        for h in range(HG):
            pk[t, h] = both[:, h * HD:(h + 1) * HD]
            d = jnp.sum(prod[:, h * HD:(h + 1) * HD], axis=1, keepdims=True)
            tile = jnp.where(lane == h, d, tile)
        hi = tile.astype(BF16).astype(F32)
        mid = (tile - hi).astype(BF16).astype(F32)
        lo = tile - hi - mid
        pk[t, HG] = jnp.concatenate([hi + pltpu.roll(lo, QR, 1), mid], axis=0).astype(BF16)

    pl.semaphore_wait(bar, count + 2 - 2 * own.astype(jnp.int32))

    mine = xh * NY + y
    for k in range(NX):
        for i in range(NS):
            t = up(s, i, NS)
            cp = rc(pk.at[t], p1.at[mine], s1.at[i, k], r1.at[k, y], dev(t, s, up(xh, k, NX), z))
            if (i, k) == (0, 0):
                self_in = cp

                @pl.when(jnp.logical_not(own))
                def _():
                    cp.start()
            else:
                go(cp)

    @pl.when(own)
    def _():
        p1[mine] = pk[s]

    dyr, dyl = dev(s, yr, xh, z), dev(s, yl, xh, z)
    for h in range(HG):
        kv[y, h, 0] = kin[:, h * HD:(h + 1) * HD]
        kv[y, h, 1] = vin[:, h * HD:(h + 1) * HD]
        for i, (h0, n) in enumerate(PIECES):
            if h == h0 + n - 1:
                ref = kv.at[y, pl.ds(h0, n)]
                go(rc(ref, ref, sy.at[0, i], ry.at[0, i], dyr))
                go(rc(ref, ref, sy.at[1, i], ry.at[1, i], dyl))

    def kv_forward(i):
        hs = pl.ds(*PIECES[i])
        arrived(kv.at[yl, hs], ry.at[0, i])
        go(rc(kv.at[yl, hs, 0], kv.at[yl, hs, 0], sf.at[0, i], rf.at[0, i], dyr))
        arrived(kv.at[yr, hs], ry.at[1, i])
        go(rc(kv.at[yr, hs, 1], kv.at[yr, hs, 1], sf.at[1, i], rf.at[1, i], dyl))

    def kv_ready(i):
        hs = pl.ds(*PIECES[i])
        arrived(kv.at[y2, hs, 0], rf.at[0, i])
        arrived(kv.at[y2, hs, 1], rf.at[1, i])

    kcol = lax.broadcasted_iota(jnp.int32, (1, KV), 1)
    kblk = kcol // KR
    base = jnp.zeros((1, KV), jnp.int32)
    for b in range(NY):
        base = jnp.where(kblk == b, order[(b * NX + xh) * NZ + z], base)
    kpos = base * KR + kcol % KR
    first = NY * NX * NZ * KR - QW
    zrow = lax.broadcasted_iota(jnp.int32, (ZR, 1), 0)
    zpos = first + (((zrow // QR) % NY) * NX + zrow // (NY * QR)) * NZ * QR + zrow % QR

    for k in range(NX):
        for b in range(NY):
            slot = dn(xh, k, NX) * NY + b
            if k == 0:
                @pl.when(jnp.logical_not(own & (y == b)))
                def _():
                    arrived(p1.at[slot], r1.at[k, b])
            else:
                arrived(p1.at[slot], r1.at[k, b])
    zr, zl = up(z, 1, NZ), dn(z, 1, NZ)
    dzr, dzl = dev(s, y, xh, zr), dev(s, y, xh, zl)
    half = NB // 2

    def zref(d, t, i, part):
        src = dn(z, t, NZ) if d == 0 else up(z, t, NZ)
        hs = pl.ds(*PIECES[i])
        return g.at[src, hs, pl.ds(d * half, half)] if part else g.at[src, hs]

    def zsend(d, t, i):
        ref = zref(d, t - 1, i, t == NT)
        go(rc(ref, ref, sz.at[d, t - 1, i], rz.at[d, t - 1, i], dzr if d == 0 else dzl))

    def zwait(d, t, i):
        arrived(zref(d, t, i, t == NT), rz.at[d, t - 1, i])

    def dsend(d, t):
        src = dn(z, t - 1, NZ) if d == 0 else up(z, t - 1, NZ)
        go(rc(gd.at[src], gd.at[src], szd.at[d, t - 1], rzd.at[d, t - 1], dzr if d == 0 else dzl))

    def dwait(d, t):
        src = dn(z, t, NZ) if d == 0 else up(z, t, NZ)
        arrived(gd.at[src], rzd.at[d, t - 1])

    def delta_rows(zc):
        tile = gd[zc]
        for b in range(NB):
            piece = tile if b == 0 else pltpu.roll(tile, 128 - b * QR, 1)
            delc[pl.ds(pl.multiple_of(zc * ZR + b * QR, QR), QR)] = piece

    def chunks(t):
        return (z, up(z, NT, NZ)) if t == NT else (dn(z, t, NZ), up(z, t, NZ))

    def rowsof(zc):
        return pl.ds(pl.multiple_of(zc * ZR, ZR), ZR)

    def pair(ref, h, t):
        a, b = chunks(t)
        return jnp.concatenate([ref[h, rowsof(a)], ref[h, rowsof(b)]], axis=0)

    def put(ref, h, t, v):
        a, b = chunks(t)
        ref[h, rowsof(a)] = v[:ZR]
        ref[h, rowsof(b)] = v[ZR:]

    def score_tile(h, t):
        qs_, ds_ = [], []
        for zc in chunks(t):
            blk = g[zc, h].astype(F32).reshape(NB, 2, QR, HD)
            qc = blk[:, 0].reshape(ZR, HD).astype(BF16)
            dc = blk[:, 1].reshape(ZR, HD).astype(BF16)
            q3[h, rowsof(zc)] = qc
            do3[h, rowsof(zc)] = dc
            qs_.append(qc)
            ds_.append(dc)
        kh = kv[:, h, 0].reshape(KV, HD)
        sc = nt(jnp.concatenate(qs_, axis=0), kh) * SCALE
        a, b = chunks(t)
        qpos = jnp.concatenate([zpos + a * QR, zpos + b * QR], axis=0)
        sc = jnp.where(kpos <= qpos, sc, MASKED)
        m = jnp.max(sc, axis=1, keepdims=True)
        p = jnp.exp(sc - m)
        l = jnp.sum(p, axis=1, keepdims=True)
        put(pb, h, t, p.astype(BF16))
        put(m3, h, t, jnp.broadcast_to(m, (RT, 128)))
        put(lse3, h, t, jnp.broadcast_to(m + jnp.log(l), (RT, 128)))
        if t == NT:
            pl_[h] = p
        else:
            dprob(h, t, p, jnp.concatenate(ds_, axis=0))

    def dprob(h, t, p, dom):
        vh = kv[:, h, 1].reshape(KV, HD)
        a, b = chunks(t)
        dl = jnp.concatenate([delc[rowsof(a)], delc[rowsof(b)]], axis=0)[:, h:h + 1]
        put(db, h, t, (p * (nt(dom, vh) - dl) * SCALE).astype(BF16))

    def dprob_late(h):
        dprob(h, NT, pl_[h], pair(do3, h, NT))
        kh = kv[:, h, 0].reshape(KV, HD)
        dqa[h] = (nn(db[h], kh) * jnp.exp(m3[h] - lse3[h])).reshape(NZ, ZR, HD)

    lane2 = lax.broadcasted_iota(jnp.int32, (RT, 128), 1)

    mz = xh * NZ + z

    def stats_send():
        st = jnp.zeros((RT, 128), F32)
        for h in range(HG):
            for rt in range(NR):
                st = jnp.where(lane2 == h * NR + rt, lse3[h, rt * RT:(rt + 1) * RT], st)
        lz[mz] = st.T[:SR]
        for j in range(NZ):
            for k in range(NX):
                if (j, k) != (0, 0):
                    to = dev(s, y, up(xh, k, NX), up(z, j, NZ))
                    go(rc(lz.at[mz], lz.at[mz], sl.at[k, j], rl.at[k, j], to))

    def stats_wait():
        for j in range(NZ):
            for k in range(NX):
                if (j, k) != (0, 0):
                    f = (up(xh, k, NX) << 3) | dn(z, j, NZ)
                    arrived(lz.at[f], rl.at[k, j])
        mx = lz[0]
        for f in range(1, NX * NZ):
            mx = jnp.maximum(mx, lz[f])
        tot = jnp.exp(lz[0] - mx)
        for f in range(1, NX * NZ):
            tot = tot + jnp.exp(lz[f] - mx)
        lt = mx + jnp.log(tot)
        pad = jnp.zeros((128 - SR, 128), F32)
        tt = jnp.concatenate([lt, pad], axis=0).T
        for h in range(HG):
            for rt in range(NR):
                rows = slice(rt * RT, (rt + 1) * RT)
                i = h * NR + rt
                col = jnp.broadcast_to(tt[:, i:i + 1], (RT, 128))
                c3[h, rows] = jnp.exp(m3[h, rows] - col)
                w3[h, rows] = jnp.exp(lse3[h, rows] - col)
        return lt, pad

    def weights(lt, pad):
        for i, n in enumerate((-2, -1, 1, 2)):
            f = (xh << 3) | up(z, n, NZ)
            wt[i] = jnp.concatenate([jnp.exp(lz[f] - lt), pad], axis=0).T

    lane3 = lax.broadcasted_iota(jnp.int32, (ZR, 128), 1)

    def weight(n, zc, h):
        i = {-2: 0, -1: 1, 1: 2, 2: 3}[n]
        v = wt[i, pl.ds(pl.multiple_of((zc & 1) * ZR, ZR), ZR)]
        v = jnp.where(lane3 == h * NR + (zc >> 1), v, 0.0)
        return jnp.sum(v, axis=1, keepdims=True)

    for h in range(HG):
        for b in range(NB):
            g[z, h, b] = p1[b, h]
    tile = jnp.zeros((QR, 128), F32)
    for b in range(NB):
        d2 = p1[b, HG].astype(F32)
        top = d2[:QR]
        d1 = jnp.where(lane < QR, top + d2[QR:] + pltpu.roll(top, 128 - QR, 1), 0.0)
        tile = tile + (d1 if b == 0 else pltpu.roll(d1, b * QR, 1))
    gd[z] = tile

    for i in range(2):
        zsend(0, 1, i)
        zsend(1, 1, i)
        if i == 0:
            dsend(0, 1)
            dsend(1, 1)
    kv_forward(0)
    for t in range(2, NT + 2):
        for i, (h0, n) in enumerate(PIECES):
            zwait(0, t - 1, i)
            zwait(1, t - 1, i)
            if t <= NT:
                zsend(0, t, i)
                zsend(1, t, i)
            if i == 0:
                dwait(0, t - 1)
                if t <= NT:
                    dwait(1, t - 1)
                    dsend(0, t)
                    if t < NT:
                        dsend(1, t)
                for zc in chunks(t - 1):
                    delta_rows(zc)
            if t == 2:
                if i == 0:
                    kv_forward(1)
                kv_ready(i)
            for h in range(h0, h0 + n):
                score_tile(h, t - 1)
    stats_send()

    HR = ZR // 2
    dz2r, dz2l = dev(s, y, xh, up(z, 2, NZ)), dev(s, y, xh, dn(z, 2, NZ))

    def zmsg(d, kind):
        a_, b_ = zs.at[d, kind], zr_.at[d, kind]
        if kind == 0:
            part = pl.ds(d * HR, HR)
            a_, b_ = zs.at[d, kind, :, part], zr_.at[d, kind, :, part]
        near, far = (dzr, dz2r) if d == 0 else (dzl, dz2l)
        return rc(a_, b_, sg.at[d, kind], rg.at[d, kind], far if kind in (0, 3) else near)

    def step(d, n):
        return up(z, n, NZ) if d == 0 else dn(z, n, NZ)

    def query_grads():
        for kind, n in ((1, 3), (0, 4), (2, 1)):
            for d in range(2):
                for h in range(HG):
                    if kind == 0:
                        part = slice(d * HR, (d + 1) * HR)
                        zs[d, kind, h, part] = dqa[h, step(d, n), part].astype(BF16)
                    else:
                        zs[d, kind, h] = dqa[h, step(d, n)].astype(BF16)
                go(zmsg(d, kind))

    def query_relay():
        for d in range(2):
            sign = 1 - 2 * d
            zmsg(d, 0).wait_recv()
            zmsg(d, 1).wait_recv()
            part = slice(d * HR, (d + 1) * HR)
            rest = slice((1 - d) * HR, (2 - d) * HR)
            to = step(d, 2)
            for h in range(HG):
                acc = dqa[h, to] * w3[h, rowsof(to)] + zr_[d, 1, h].astype(F32) * weight(-sign, to, h)
                far = zr_[d, 0, h, part].astype(F32) * weight(-2 * sign, to, h)[part]
                zs[d, 3, h, rest] = acc[rest].astype(BF16)
                zs[d, 3, h, part] = (acc[part] + far).astype(BF16)
            go(zmsg(d, 3))

    def query_sum():
        for d in range(2):
            zmsg(d, 2).wait_recv()
            zmsg(d, 3).wait_recv()
        for h in range(HG):
            acc = dqa[h, z] * w3[h, rowsof(z)]
            for d in range(2):
                acc = acc + zr_[d, 3, h].astype(F32)
                acc = acc + zr_[d, 2, h].astype(F32) * weight(2 * d - 1, z, h)
            tb[:, h] = acc.reshape(NB, QR, HD)

    def cache_grads(h):
        cc = c3[h]
        dkt = tn((q3[h].astype(F32) * cc).astype(BF16), db[h])
        dvt = tn((do3[h].astype(F32) * cc).astype(BF16), pb[h])
        for b in range(NY):
            dkv[h, b, 0] = dkt[:, b * KR:(b + 1) * KR].T
            dkv[h, b, 1] = dvt[:, b * KR:(b + 1) * KR].T
        ks1[h, 0, 0] = dkv[h, y2, 0].astype(BF16)
        ks1[h, 0, 1] = dkv[h, yr, 1].astype(BF16)
        ks1[h, 1, 0] = dkv[h, y2, 1].astype(BF16)
        ks1[h, 1, 1] = dkv[h, yl, 0].astype(BF16)
        go(rc(ks1.at[h, 0], kr1.at[h, 0], sk.at[0, 0, h], rk.at[0, 0, h], dyr))
        go(rc(ks1.at[h, 1], kr1.at[h, 1], sk.at[0, 1, h], rk.at[0, 1, h], dyl))

    def second_leg(h):
        arrived(kr1.at[h, 0], rk.at[0, 0, h])
        ks2[h, 0] = (dkv[h, yr, 0] + kr1[h, 0, 0].astype(F32)).astype(BF16)
        go(rc(ks2.at[h, 0], kr2.at[h, 0], sk.at[1, 0, h], rk.at[1, 0, h], dyr))
        arrived(kr1.at[h, 1], rk.at[0, 1, h])
        ks2[h, 1] = (dkv[h, yl, 1] + kr1[h, 1, 0].astype(F32)).astype(BF16)
        go(rc(ks2.at[h, 1], kr2.at[h, 1], sk.at[1, 1, h], rk.at[1, 1, h], dyl))

    def cache_out(h):
        arrived(kr2.at[h, 0], rk.at[1, 0, h])
        arrived(kr2.at[h, 1], rk.at[1, 1, h])
        cols = slice(h * HD, (h + 1) * HD)
        dk_out[:, cols] = (dkv[h, y, 0] + kr1[h, 1, 1].astype(F32) + kr2[h, 0].astype(F32)).astype(BF16)
        dv_out[:, cols] = (dkv[h, y, 1] + kr1[h, 0, 1].astype(F32) + kr2[h, 1].astype(F32)).astype(BF16)

    for h in range(HG):
        dprob_late(h)
    query_grads()
    stats = stats_wait()
    cache_grads(0)
    cache_grads(1)
    weights(*stats)
    query_relay()
    second_leg(0)
    cache_grads(2)
    second_leg(1)
    cache_grads(3)
    second_leg(2)
    cache_grads(4)
    second_leg(3)
    query_sum()

    for j in range(NY):
        for k in range(NX):
            ty, tx = up(y, j, NY), up(xh, k, NX)
            cp = rc(tb.at[tx * NY + ty], p8.at[k, s], s8.at[j, k], r8.at[k, s], dev(y, ty, tx, z))
            if (j, k) == (0, 0):
                self_out = cp

                @pl.when(jnp.logical_not(own))
                def _():
                    cp.start()
            else:
                go(cp)

    @pl.when(own)
    def _():
        p8[0, s] = tb[mine]

    second_leg(HG - 1)
    for h in range(HG):
        cache_out(h)

    for k in range(NX):
        for b in range(NS):
            if k == 0:
                @pl.when(jnp.logical_not(own & (s == b)))
                def _():
                    arrived(p8.at[k, b], r8.at[k, b])
            else:
                arrived(p8.at[k, b], r8.at[k, b])
    for b in range(NS):
        for h in range(HG):
            col = b * GF + h * HD
            dq_out[0, :, col:col + HD] = (p8[0, b, h] + p8[1, b, h]).astype(BF16)

    @pl.when(jnp.logical_not(own))
    def _():
        self_in.wait_send()
        self_out.wait_send()

    for cp in sends:
        cp.wait_send()


def place(a, b, c, x, y, z):
    x[...] = a[...]
    y[...] = b[...]
    z[...] = c[...]


def local(block_order, queries, cache_keys, cache_values, attention_out, output_grad):
    dma = pltpu.SemaphoreType.DMA
    vm = pltpu.VMEM
    row = queries.shape
    scratch = [
        vm(row, BF16), vm(row, BF16), vm(row, BF16), vm((KR, GF), BF16), vm((KR, GF), BF16),
        vm((NS, HG + 1, 16, HD), BF16), vm((NB, HG + 1, 16, HD), BF16),
        vm((NZ, HG, NB, 16, HD), BF16), vm((NZ, QR, 128), F32),
        vm((NY, HG, 2, KR, HD), BF16), vm((HG, QW, HD), BF16), vm((HG, QW, HD), BF16), vm((QW, 128), F32),
        vm((HG, RT, KV), F32), vm((HG, QW, KV), BF16), vm((HG, QW, KV), BF16),
        vm((HG, QW, 128), F32), vm((HG, QW, 128), F32), vm((HG, QW, 128), F32),
        vm((HG, QW, 128), F32), vm((NX * NZ, SR, 128), F32), vm((4, 128, 128), F32),
        vm((HG, NZ, ZR, HD), F32), vm((2, 4, HG, ZR, HD), BF16), vm((2, 4, HG, ZR, HD), BF16),
        vm((HG, NY, 2, KR, HD), F32),
        vm((HG, 2, 2, KR, HD), BF16), vm((HG, 2, 2, KR, HD), BF16),
        vm((HG, 2, KR, HD), BF16), vm((HG, 2, KR, HD), BF16),
        vm((NB, HG, QR, HD), F32), vm((NX, NS, HG, QR, HD), F32),
        dma((5,)), dma((NS, NX)), dma((NX, NY)),
        dma((2, NT, 2)), dma((2, NT, 2)), dma((2, NT)), dma((2, NT)),
        dma((2, 2)), dma((2, 2)), dma((2, 2)), dma((2, 2)),
        dma((NX, NZ)), dma((NX, NZ)), dma((2, 4)), dma((2, 4)),
        dma((2, 2, HG)), dma((2, 2, HG)), dma((NY, NX)), dma((NX, NS)),
    ]
    vspec = pl.BlockSpec(memory_space=pltpu.VMEM)
    hbm = pl.BlockSpec(memory_space=pl.ANY)
    dq, dk, dv = pl.pallas_call(
        kernel,
        out_shape=(
            jax.ShapeDtypeStruct((1, QR, NS * GF), BF16),
            jax.ShapeDtypeStruct((KR, GF), BF16),
            jax.ShapeDtypeStruct((KR, GF), BF16),
        ),
        in_specs=[pl.BlockSpec(memory_space=pltpu.SMEM)] + [hbm] * 5,
        out_specs=(vspec, vspec, vspec),
        scratch_shapes=scratch,
        compiler_params=pltpu.CompilerParams(
            collective_id=0, has_side_effects=True, vmem_limit_bytes=56 << 20),
    )(block_order, queries, output_grad, attention_out, cache_keys, cache_values)
    return pl.pallas_call(
        place,
        out_shape=tuple(jax.ShapeDtypeStruct(v.shape, v.dtype) for v in (dq, dk, dv)),
        in_specs=[vspec] * 3,
        out_specs=(vspec,) * 3,
    )(dq, dk, dv)


def solution(mesh):
    in_specs = (
        P(),
        P("section", "ctx", None),
        P("ctx", "section"),
        P("ctx", "section"),
        P("section", "ctx", None),
        P("section", "ctx", None),
    )
    out_specs = (P("section", "ctx", None), P("ctx", "section"), P("ctx", "section"))
    return jax.shard_map(local, mesh=mesh, in_specs=in_specs, out_specs=out_specs, check_vma=False)
```

```python
import jax
import jax.numpy as jnp
from jax import lax
from jax.experimental import pallas as pl
from jax.experimental.pallas import tpu as pltpu
from jax.sharding import PartitionSpec as P

MESH = pl.DeviceIdType.MESH
F32 = jnp.float32
BF16 = jnp.bfloat16

NS, NY, NX, NZ = 4, 4, 2, 8
HG, HD, GF = 5, 128, 640
KR = 128
KV = NY * KR
QR = 8
NB = NX * NY
ZR = NB * QR
QW = NZ * ZR
NT = NZ // 2
SCALE = HD ** -0.5
MASKED = -1e30
RT = 128
NR = QW // RT
PIECES = ((0, 2), (2, 3))
SR = 24


def nt(a, b):
    return lax.dot_general(a, b, (((1,), (1,)), ((), ())), preferred_element_type=F32)


def tn(a, b):
    return lax.dot_general(a, b, (((0,), (0,)), ((), ())), preferred_element_type=F32)


def nn(a, b):
    return lax.dot_general(a, b, (((1,), (0,)), ((), ())), preferred_element_type=F32)


def kernel(order, q_in, do_in, o_in, k_in, v_in, dq_out, dk_out, dv_out,
           qv, dov, ov, kin, vin, pk, p1, g, gd, kv, q3, do3, delc, pl_, pb, db, m3, lse3, c3, w3, lx, lz, wt,
           dqa, zs, zr_, dkv, ks1, kr1, ks2, kr2, tb, p8,
           sin, s1, r1, sz, rz, szd, rzd, sy, ry, sf, rf, sl, rl, sx, rx, sg, rg, sk, rk, s8, r8):
    s = lax.axis_index("section")
    c = lax.axis_index("ctx")
    y = c >> 4
    xh = (c >> 3) & 1
    z = c & 7
    me = (s, c)
    own = s == y

    def dev(s_, y_, x_, z_):
        return (s_, (y_ << 4) | (x_ << 3) | z_)

    def rc(src, dst, ssem, rsem, to):
        return pltpu.make_async_remote_copy(
            src_ref=src, dst_ref=dst, send_sem=ssem, recv_sem=rsem,
            device_id=to, device_id_type=MESH)

    def arrived(dst, rsem):
        rc(dst, dst, rsem, rsem, me).wait_recv()

    def up(v, n, mod):
        return (v + n) & (mod - 1)

    def dn(v, n, mod):
        return (v - n) & (mod - 1)

    sends = []

    def go(cp):
        cp.start()
        sends.append(cp)

    loads = []
    for i, (a, b) in enumerate(((q_in, qv), (do_in, dov), (o_in, ov), (k_in, kin), (v_in, vin))):
        cp = pltpu.make_async_copy(a, b, sin.at[i])
        cp.start()
        loads.append(cp)

    yr, yl, y2 = up(y, 1, NY), dn(y, 1, NY), up(y, 2, NY)
    bar = pltpu.get_barrier_semaphore()

    def greet(to):
        pl.semaphore_signal(bar, inc=1, device_id=to, device_id_type=MESH)

    count = 0
    for j in range(1, NZ):
        greet(dev(s, y, xh, up(z, j, NZ)))
        count += 1
    for t in (dev(s, yr, xh, z), dev(s, yl, xh, z), dev(s, y, up(xh, 1, NX), z)):
        greet(t)
        count += 1
    for i in range(4):
        for k in range(NX):
            if (i, k) != (0, 0):
                greet(dev(up(s, i, NS), s, up(xh, k, NX), z))
                greet(dev(y, up(y, i, NY), up(xh, k, NX), z))
                count += 2

    @pl.when(jnp.logical_not(own))
    def _():
        greet(dev(s, s, xh, z))
        greet(dev(y, y, xh, z))

    for cp in loads:
        cp.wait()

    lane = lax.broadcasted_iota(jnp.int32, (QR, 128), 1)
    for t in range(NS):
        cols = slice(t * GF, (t + 1) * GF)
        qf = qv[0, :, cols].astype(F32)
        df = dov[0, :, cols].astype(F32)
        prod = df * ov[0, :, cols].astype(F32)
        both = jnp.concatenate([qf, df], axis=0).astype(BF16)
        tile = jnp.zeros((QR, 128), F32)
        for h in range(HG):
            pk[t, h] = both[:, h * HD:(h + 1) * HD]
            d = jnp.sum(prod[:, h * HD:(h + 1) * HD], axis=1, keepdims=True)
            tile = jnp.where(lane == h, d, tile)
        hi = tile.astype(BF16).astype(F32)
        mid = (tile - hi).astype(BF16).astype(F32)
        lo = tile - hi - mid
        pk[t, HG] = jnp.concatenate([hi + pltpu.roll(lo, QR, 1), mid], axis=0).astype(BF16)

    pl.semaphore_wait(bar, count + 2 - 2 * own.astype(jnp.int32))

    mine = xh * NY + y
    for k in range(NX):
        for i in range(NS):
            t = up(s, i, NS)
            cp = rc(pk.at[t], p1.at[mine], s1.at[i, k], r1.at[k, y], dev(t, s, up(xh, k, NX), z))
            if (i, k) == (0, 0):
                self_in = cp

                @pl.when(jnp.logical_not(own))
                def _():
                    cp.start()
            else:
                go(cp)

    @pl.when(own)
    def _():
        p1[mine] = pk[s]

    dyr, dyl = dev(s, yr, xh, z), dev(s, yl, xh, z)
    for h in range(HG):
        kv[y, h, 0] = kin[:, h * HD:(h + 1) * HD]
        kv[y, h, 1] = vin[:, h * HD:(h + 1) * HD]
        for i, (h0, n) in enumerate(PIECES):
            if h == h0 + n - 1:
                ref = kv.at[y, pl.ds(h0, n)]
                go(rc(ref, ref, sy.at[0, i], ry.at[0, i], dyr))
                go(rc(ref, ref, sy.at[1, i], ry.at[1, i], dyl))

    def kv_forward(i):
        hs = pl.ds(*PIECES[i])
        arrived(kv.at[yl, hs], ry.at[0, i])
        go(rc(kv.at[yl, hs, 0], kv.at[yl, hs, 0], sf.at[0, i], rf.at[0, i], dyr))
        arrived(kv.at[yr, hs], ry.at[1, i])
        go(rc(kv.at[yr, hs, 1], kv.at[yr, hs, 1], sf.at[1, i], rf.at[1, i], dyl))

    def kv_ready(i):
        hs = pl.ds(*PIECES[i])
        arrived(kv.at[y2, hs, 0], rf.at[0, i])
        arrived(kv.at[y2, hs, 1], rf.at[1, i])

    kcol = lax.broadcasted_iota(jnp.int32, (1, KV), 1)
    kblk = kcol // KR
    base = jnp.zeros((1, KV), jnp.int32)
    for b in range(NY):
        base = jnp.where(kblk == b, order[(b * NX + xh) * NZ + z], base)
    kpos = base * KR + kcol % KR
    first = NY * NX * NZ * KR - QW
    zrow = lax.broadcasted_iota(jnp.int32, (ZR, 1), 0)
    zpos = first + (((zrow // QR) % NY) * NX + zrow // (NY * QR)) * NZ * QR + zrow % QR

    for k in range(NX):
        for b in range(NY):
            slot = dn(xh, k, NX) * NY + b
            if k == 0:
                @pl.when(jnp.logical_not(own & (y == b)))
                def _():
                    arrived(p1.at[slot], r1.at[k, b])
            else:
                arrived(p1.at[slot], r1.at[k, b])
    zr, zl = up(z, 1, NZ), dn(z, 1, NZ)
    dzr, dzl = dev(s, y, xh, zr), dev(s, y, xh, zl)
    dz2r, dz2l = dev(s, y, xh, up(z, 2, NZ)), dev(s, y, xh, dn(z, 2, NZ))
    half = NB // 2

    def zref(d, t, i, part):
        src = dn(z, t, NZ) if d == 0 else up(z, t, NZ)
        hs = pl.ds(*PIECES[i])
        return g.at[src, hs, pl.ds(d * half, half)] if part else g.at[src, hs]

    def zsend(d, t, i):
        last = t == NT
        ref = zref(d, 2 if last else t - 1, i, last)
        to = (dz2r if d == 0 else dz2l) if last else (dzr if d == 0 else dzl)
        go(rc(ref, ref, sz.at[d, t - 1, i], rz.at[d, t - 1, i], to))

    def zwait(d, t, i):
        arrived(zref(d, t, i, t == NT), rz.at[d, t - 1, i])

    def dsend(d, t):
        n = 2 if t == NT else t - 1
        ref = gd.at[dn(z, n, NZ) if d == 0 else up(z, n, NZ)]
        to = dz2r if t == NT else (dzr if d == 0 else dzl)
        go(rc(ref, ref, szd.at[d, t - 1], rzd.at[d, t - 1], to))

    def dwait(d, t):
        arrived(gd.at[dn(z, t, NZ) if d == 0 else up(z, t, NZ)], rzd.at[d, t - 1])

    def delta_rows(zc):
        tile = gd[zc]
        for b in range(NB):
            piece = tile if b == 0 else pltpu.roll(tile, 128 - b * QR, 1)
            delc[pl.ds(pl.multiple_of(zc * ZR + b * QR, QR), QR)] = piece

    def chunks(t):
        return (z, up(z, NT, NZ)) if t == NT else (dn(z, t, NZ), up(z, t, NZ))

    def rowsof(zc):
        return pl.ds(pl.multiple_of(zc * ZR, ZR), ZR)

    def pair(ref, h, t):
        a, b = chunks(t)
        return jnp.concatenate([ref[h, rowsof(a)], ref[h, rowsof(b)]], axis=0)

    def put(ref, h, t, v):
        a, b = chunks(t)
        ref[h, rowsof(a)] = v[:ZR]
        ref[h, rowsof(b)] = v[ZR:]

    def score_tile(h, t):
        qs_, ds_ = [], []
        for zc in chunks(t):
            blk = g[zc, h].astype(F32).reshape(NB, 2, QR, HD)
            qc = blk[:, 0].reshape(ZR, HD).astype(BF16)
            dc = blk[:, 1].reshape(ZR, HD).astype(BF16)
            q3[h, rowsof(zc)] = qc
            do3[h, rowsof(zc)] = dc
            qs_.append(qc)
            ds_.append(dc)
        kh = kv[:, h, 0].reshape(KV, HD)
        sc = nt(jnp.concatenate(qs_, axis=0), kh) * SCALE
        a, b = chunks(t)
        qpos = jnp.concatenate([zpos + a * QR, zpos + b * QR], axis=0)
        sc = jnp.where(kpos <= qpos, sc, MASKED)
        m = jnp.max(sc, axis=1, keepdims=True)
        p = jnp.exp(sc - m)
        l = jnp.sum(p, axis=1, keepdims=True)
        put(pb, h, t, p.astype(BF16))
        put(m3, h, t, jnp.broadcast_to(m, (RT, 128)))
        put(lse3, h, t, jnp.broadcast_to(m + jnp.log(l), (RT, 128)))
        if t == NT:
            pl_[h] = p
        else:
            dprob(h, t, p, jnp.concatenate(ds_, axis=0))

    def dprob(h, t, p, dom):
        vh = kv[:, h, 1].reshape(KV, HD)
        a, b = chunks(t)
        dl = jnp.concatenate([delc[rowsof(a)], delc[rowsof(b)]], axis=0)[:, h:h + 1]
        put(db, h, t, (p * (nt(dom, vh) - dl) * SCALE).astype(BF16))

    def dprob_late(h):
        dprob(h, NT, pl_[h], pair(do3, h, NT))
        kh = kv[:, h, 0].reshape(KV, HD)
        dqa[h] = nn(db[h], kh).reshape(NZ, ZR, HD)

    lane2 = lax.broadcasted_iota(jnp.int32, (RT, 128), 1)

    def columns(rows_):
        pad = jnp.zeros((128 - SR, 128), F32)
        return jnp.concatenate([rows_, pad], axis=0).T

    def stats_send():
        st = jnp.zeros((RT, 128), F32)
        for h in range(HG):
            for rt in range(NR):
                st = jnp.where(lane2 == h * NR + rt, lse3[h, rt * RT:(rt + 1) * RT], st)
        lx[0] = st.T[:SR]
        go(rc(lx.at[0], lx.at[1], sx.at[0], rx.at[0], dev(s, y, up(xh, 1, NX), z)))

    def stats_pair():
        arrived(lx.at[1], rx.at[0])
        a, b = lx[0], lx[1]
        mx = jnp.maximum(a, b)
        both = mx + jnp.log(jnp.exp(a - mx) + jnp.exp(b - mx))
        lz[z] = both
        for j in range(1, NZ):
            go(rc(lz.at[z], lz.at[z], sl.at[j], rl.at[j], dev(s, y, xh, up(z, j, NZ))))
        tt = columns(both)
        for h in range(HG):
            for rt in range(NR):
                i = h * NR + rt
                lse3[h, rt * RT:(rt + 1) * RT] = jnp.broadcast_to(tt[:, i:i + 1], (RT, 128))

    def stats_wait():
        for j in range(1, NZ):
            f = dn(z, j, NZ)
            arrived(lz.at[f], rl.at[j])
        mx = lz[0]
        for f in range(1, NZ):
            mx = jnp.maximum(mx, lz[f])
        tot = jnp.exp(lz[0] - mx)
        for f in range(1, NZ):
            tot = tot + jnp.exp(lz[f] - mx)
        lt = mx + jnp.log(tot)
        tt = columns(lt)
        for h in range(HG):
            for rt in range(NR):
                rows = slice(rt * RT, (rt + 1) * RT)
                i = h * NR + rt
                col = jnp.broadcast_to(tt[:, i:i + 1], (RT, 128))
                c3[h, rows] = jnp.exp(m3[h, rows] - col)
                w3[h, rows] = jnp.exp(lse3[h, rows] - col)
        return lt

    def weights(lt):
        for i, n in enumerate((-2, -1, 1, 2)):
            wt[i] = columns(jnp.exp(lz[up(z, n, NZ)] - lt))

    lane3 = lax.broadcasted_iota(jnp.int32, (ZR, 128), 1)

    def weight(n, zc, h):
        i = {-2: 0, -1: 1, 1: 2, 2: 3}[n]
        v = wt[i, pl.ds(pl.multiple_of((zc & 1) * ZR, ZR), ZR)]
        v = jnp.where(lane3 == h * NR + (zc >> 1), v, 0.0)
        return jnp.sum(v, axis=1, keepdims=True)

    for h in range(HG):
        for b in range(NB):
            g[z, h, b] = p1[b, h]
    tile = jnp.zeros((QR, 128), F32)
    for b in range(NB):
        d2 = p1[b, HG].astype(F32)
        top = d2[:QR]
        d1 = jnp.where(lane < QR, top + d2[QR:] + pltpu.roll(top, 128 - QR, 1), 0.0)
        tile = tile + (d1 if b == 0 else pltpu.roll(d1, b * QR, 1))
    gd[z] = tile

    for i in range(2):
        zsend(0, 1, i)
        zsend(1, 1, i)
        if i == 0:
            dsend(0, 1)
            dsend(1, 1)
    kv_forward(0)
    for t in range(2, NT + 2):
        for i, (h0, n) in enumerate(PIECES):
            zwait(0, t - 1, i)
            zwait(1, t - 1, i)
            for n_ in (t, t + 1):
                if n_ == t < NT or n_ == NT == t + 1:
                    zsend(0, n_, i)
                    zsend(1, n_, i)
            if i == 0:
                dwait(0, t - 1)
                if t <= NT:
                    dwait(1, t - 1)
                if t < NT:
                    dsend(0, t)
                    dsend(1, t)
                if t == NT - 1:
                    dsend(0, NT)
                for zc in chunks(t - 1):
                    delta_rows(zc)
            if t == 2:
                if i == 0:
                    kv_forward(1)
                kv_ready(i)
            for h in range(h0, h0 + n):
                score_tile(h, t - 1)
    stats_send()

    HR = ZR // 2

    def zmsg(d, kind):
        a_, b_ = zs.at[d, kind], zr_.at[d, kind]
        if kind == 0:
            part = pl.ds(d * HR, HR)
            a_, b_ = zs.at[d, kind, :, part], zr_.at[d, kind, :, part]
        near, far = (dzr, dz2r) if d == 0 else (dzl, dz2l)
        return rc(a_, b_, sg.at[d, kind], rg.at[d, kind], far if kind in (0, 3) else near)

    def step(d, n):
        return up(z, n, NZ) if d == 0 else dn(z, n, NZ)

    def query_grads():
        for h in range(HG):
            dqa[h] = dqa[h] * jnp.exp(m3[h] - lse3[h]).reshape(NZ, ZR, HD)
        for kind, n in ((1, 3), (0, 4), (2, 1)):
            for d in range(2):
                for h in range(HG):
                    if kind == 0:
                        part = slice(d * HR, (d + 1) * HR)
                        zs[d, kind, h, part] = dqa[h, step(d, n), part].astype(BF16)
                    else:
                        zs[d, kind, h] = dqa[h, step(d, n)].astype(BF16)
                go(zmsg(d, kind))

    def query_relay():
        for d in range(2):
            sign = 1 - 2 * d
            zmsg(d, 0).wait_recv()
            zmsg(d, 1).wait_recv()
            part = slice(d * HR, (d + 1) * HR)
            rest = slice((1 - d) * HR, (2 - d) * HR)
            to = step(d, 2)
            for h in range(HG):
                acc = dqa[h, to] * w3[h, rowsof(to)] + zr_[d, 1, h].astype(F32) * weight(-sign, to, h)
                far = zr_[d, 0, h, part].astype(F32) * weight(-2 * sign, to, h)[part]
                zs[d, 3, h, rest] = acc[rest].astype(BF16)
                zs[d, 3, h, part] = (acc[part] + far).astype(BF16)
            go(zmsg(d, 3))

    def query_sum():
        for d in range(2):
            zmsg(d, 2).wait_recv()
            zmsg(d, 3).wait_recv()
        for h in range(HG):
            acc = dqa[h, z] * w3[h, rowsof(z)]
            for d in range(2):
                acc = acc + zr_[d, 3, h].astype(F32)
                acc = acc + zr_[d, 2, h].astype(F32) * weight(2 * d - 1, z, h)
            tb[:, h] = acc.reshape(NB, QR, HD)

    def cache_grads(h):
        cc = c3[h]
        dkt = tn((q3[h].astype(F32) * cc).astype(BF16), db[h])
        dvt = tn((do3[h].astype(F32) * cc).astype(BF16), pb[h])
        for b in range(NY):
            dkv[h, b, 0] = dkt[:, b * KR:(b + 1) * KR].T
            dkv[h, b, 1] = dvt[:, b * KR:(b + 1) * KR].T
        ks1[h, 0, 0] = dkv[h, y2, 0].astype(BF16)
        ks1[h, 0, 1] = dkv[h, yr, 1].astype(BF16)
        ks1[h, 1, 0] = dkv[h, y2, 1].astype(BF16)
        ks1[h, 1, 1] = dkv[h, yl, 0].astype(BF16)
        go(leg(h, 0, 0, dyr))
        go(leg(h, 1, 0, dyl))

    def leg(h, d, i, to):
        return rc(ks1.at[h, d, i], kr1.at[h, d, i], sk.at[i, d, h], rk.at[i, d, h], to)

    def near_blocks(h):
        go(leg(h, 0, 1, dyr))
        go(leg(h, 1, 1, dyl))

    def second_leg(h):
        arrived(kr1.at[h, 0, 0], rk.at[0, 0, h])
        ks2[h, 0] = (dkv[h, yr, 0] + kr1[h, 0, 0].astype(F32)).astype(BF16)
        go(rc(ks2.at[h, 0], kr2.at[h, 0], sk.at[2, 0, h], rk.at[2, 0, h], dyr))
        arrived(kr1.at[h, 1, 0], rk.at[0, 1, h])
        ks2[h, 1] = (dkv[h, yl, 1] + kr1[h, 1, 0].astype(F32)).astype(BF16)
        go(rc(ks2.at[h, 1], kr2.at[h, 1], sk.at[2, 1, h], rk.at[2, 1, h], dyl))

    def cache_out(h):
        arrived(kr1.at[h, 0, 1], rk.at[1, 0, h])
        arrived(kr1.at[h, 1, 1], rk.at[1, 1, h])
        arrived(kr2.at[h, 0], rk.at[2, 0, h])
        arrived(kr2.at[h, 1], rk.at[2, 1, h])
        cols = slice(h * HD, (h + 1) * HD)
        dk_out[:, cols] = (dkv[h, y, 0] + kr1[h, 1, 1].astype(F32) + kr2[h, 0].astype(F32)).astype(BF16)
        dv_out[:, cols] = (dkv[h, y, 1] + kr1[h, 0, 1].astype(F32) + kr2[h, 1].astype(F32)).astype(BF16)

    for h in range(HG):
        dprob_late(h)
    stats_pair()
    query_grads()
    total = stats_wait()
    for h in range(HG):
        cache_grads(h)
        if h > 0:
            near_blocks(h - 1)
    near_blocks(HG - 1)
    weights(total)
    query_relay()
    second_leg(0)
    second_leg(1)
    second_leg(2)
    query_sum()

    for j in range(NY):
        for k in range(NX):
            ty, tx = up(y, j, NY), up(xh, k, NX)
            cp = rc(tb.at[tx * NY + ty], p8.at[k, s], s8.at[j, k], r8.at[k, s], dev(y, ty, tx, z))
            if (j, k) == (0, 0):
                self_out = cp

                @pl.when(jnp.logical_not(own))
                def _():
                    cp.start()
            else:
                go(cp)

    @pl.when(own)
    def _():
        p8[0, s] = tb[mine]

    second_leg(3)
    second_leg(4)
    for h in range(HG):
        cache_out(h)

    for k in range(NX):
        for b in range(NS):
            if k == 0:
                @pl.when(jnp.logical_not(own & (s == b)))
                def _():
                    arrived(p8.at[k, b], r8.at[k, b])
            else:
                arrived(p8.at[k, b], r8.at[k, b])
    for b in range(NS):
        for h in range(HG):
            col = b * GF + h * HD
            dq_out[0, :, col:col + HD] = (p8[0, b, h] + p8[1, b, h]).astype(BF16)

    @pl.when(jnp.logical_not(own))
    def _():
        self_in.wait_send()
        self_out.wait_send()

    for cp in sends:
        cp.wait_send()


def place(a, b, c, x, y, z):
    x[...] = a[...]
    y[...] = b[...]
    z[...] = c[...]


def local(block_order, queries, cache_keys, cache_values, attention_out, output_grad):
    dma = pltpu.SemaphoreType.DMA
    vm = pltpu.VMEM
    row = queries.shape
    scratch = [
        vm(row, BF16), vm(row, BF16), vm(row, BF16), vm((KR, GF), BF16), vm((KR, GF), BF16),
        vm((NS, HG + 1, 16, HD), BF16), vm((NB, HG + 1, 16, HD), BF16),
        vm((NZ, HG, NB, 16, HD), BF16), vm((NZ, QR, 128), F32),
        vm((NY, HG, 2, KR, HD), BF16), vm((HG, QW, HD), BF16), vm((HG, QW, HD), BF16), vm((QW, 128), F32),
        vm((HG, RT, KV), F32), vm((HG, QW, KV), BF16), vm((HG, QW, KV), BF16),
        vm((HG, QW, 128), F32), vm((HG, QW, 128), F32), vm((HG, QW, 128), F32),
        vm((HG, QW, 128), F32), vm((2, SR, 128), F32), vm((NZ, SR, 128), F32), vm((4, 128, 128), F32),
        vm((HG, NZ, ZR, HD), F32), vm((2, 4, HG, ZR, HD), BF16), vm((2, 4, HG, ZR, HD), BF16),
        vm((HG, NY, 2, KR, HD), F32),
        vm((HG, 2, 2, KR, HD), BF16), vm((HG, 2, 2, KR, HD), BF16),
        vm((HG, 2, KR, HD), BF16), vm((HG, 2, KR, HD), BF16),
        vm((NB, HG, QR, HD), F32), vm((NX, NS, HG, QR, HD), F32),
        dma((5,)), dma((NS, NX)), dma((NX, NY)),
        dma((2, NT, 2)), dma((2, NT, 2)), dma((2, NT)), dma((2, NT)),
        dma((2, 2)), dma((2, 2)), dma((2, 2)), dma((2, 2)),
        dma((NZ,)), dma((NZ,)), dma((1,)), dma((1,)), dma((2, 4)), dma((2, 4)),
        dma((3, 2, HG)), dma((3, 2, HG)), dma((NY, NX)), dma((NX, NS)),
    ]
    vspec = pl.BlockSpec(memory_space=pltpu.VMEM)
    hbm = pl.BlockSpec(memory_space=pl.ANY)
    dq, dk, dv = pl.pallas_call(
        kernel,
        out_shape=(
            jax.ShapeDtypeStruct((1, QR, NS * GF), BF16),
            jax.ShapeDtypeStruct((KR, GF), BF16),
            jax.ShapeDtypeStruct((KR, GF), BF16),
        ),
        in_specs=[pl.BlockSpec(memory_space=pltpu.SMEM)] + [hbm] * 5,
        out_specs=(vspec, vspec, vspec),
        scratch_shapes=scratch,
        compiler_params=pltpu.CompilerParams(
            collective_id=0, has_side_effects=True, vmem_limit_bytes=56 << 20),
    )(block_order, queries, output_grad, attention_out, cache_keys, cache_values)
    return pl.pallas_call(
        place,
        out_shape=tuple(jax.ShapeDtypeStruct(v.shape, v.dtype) for v in (dq, dk, dv)),
        in_specs=[vspec] * 3,
        out_specs=(vspec,) * 3,
    )(dq, dk, dv)


def solution(mesh):
    in_specs = (
        P(),
        P("section", "ctx", None),
        P("ctx", "section"),
        P("ctx", "section"),
        P("section", "ctx", None),
        P("section", "ctx", None),
    )
    out_specs = (P("section", "ctx", None), P("ctx", "section"), P("ctx", "section"))
    return jax.shard_map(local, mesh=mesh, in_specs=in_specs, out_specs=out_specs, check_vma=False)
```

```python
import jax
import jax.numpy as jnp
from jax import lax
from jax.experimental import pallas as pl
from jax.experimental.pallas import tpu as pltpu
from jax.sharding import PartitionSpec as P

MESH = pl.DeviceIdType.MESH
F32 = jnp.float32
BF16 = jnp.bfloat16

NS, NY, NX, NZ = 4, 4, 2, 8
HG, HD, GF = 5, 128, 640
KR = 128
KV = NY * KR
QR = 8
NB = NX * NY
ZR = NB * QR
QW = NZ * ZR
NT = NZ // 2
SCALE = HD ** -0.5
MASKED = -1e30
RT = 128
NR = QW // RT
PIECES = ((0, 2), (2, 3))
SROWS = (8, 16)


def nt(a, b):
    return lax.dot_general(a, b, (((1,), (1,)), ((), ())), preferred_element_type=F32)


def tn(a, b):
    return lax.dot_general(a, b, (((0,), (0,)), ((), ())), preferred_element_type=F32)


def nn(a, b):
    return lax.dot_general(a, b, (((1,), (0,)), ((), ())), preferred_element_type=F32)


def kernel(order, q_in, do_in, o_in, k_in, v_in, dq_out, dk_out, dv_out,
           qv, dov, ov, kin, vin, pk, p1, g, gd, kv, q3, do3, delc, pl_, pb, db, m3, lse3, c3, lx, lz, wt,
           dqa, zs, zr_, dkv, ks1, kr1, ks2, kr2, tb, p8,
           sin, s1, r1, sz, rz, szd, rzd, sy, ry, sf, rf, sl, rl, sx, rx, sg, rg, sk, rk, s8, r8):
    s = lax.axis_index("section")
    c = lax.axis_index("ctx")
    y = c >> 4
    xh = (c >> 3) & 1
    z = c & 7
    me = (s, c)
    own = s == y

    def dev(s_, y_, x_, z_):
        return (s_, (y_ << 4) | (x_ << 3) | z_)

    def rc(src, dst, ssem, rsem, to):
        return pltpu.make_async_remote_copy(
            src_ref=src, dst_ref=dst, send_sem=ssem, recv_sem=rsem,
            device_id=to, device_id_type=MESH)

    def arrived(dst, rsem):
        rc(dst, dst, rsem, rsem, me).wait_recv()

    def up(v, n, mod):
        return (v + n) & (mod - 1)

    def dn(v, n, mod):
        return (v - n) & (mod - 1)

    sends = []

    def go(cp):
        cp.start()
        sends.append(cp)

    def settle(count_):
        for cp in sends[:count_]:
            cp.wait_send()
        del sends[:count_]

    loads = []
    for i, (a, b) in enumerate(((q_in, qv), (do_in, dov), (o_in, ov), (k_in, kin), (v_in, vin))):
        cp = pltpu.make_async_copy(a, b, sin.at[i])
        cp.start()
        loads.append(cp)

    yr, yl, y2 = up(y, 1, NY), dn(y, 1, NY), up(y, 2, NY)
    bar = pltpu.get_barrier_semaphore()

    def greet(to):
        pl.semaphore_signal(bar, inc=1, device_id=to, device_id_type=MESH)

    count = 0
    for j in range(1, NZ):
        greet(dev(s, y, xh, up(z, j, NZ)))
        count += 1
    for t in (dev(s, yr, xh, z), dev(s, yl, xh, z), dev(s, y, up(xh, 1, NX), z)):
        greet(t)
        count += 1
    for i in range(4):
        for k in range(NX):
            if (i, k) != (0, 0):
                greet(dev(up(s, i, NS), s, up(xh, k, NX), z))
                greet(dev(y, up(y, i, NY), up(xh, k, NX), z))
                count += 2

    @pl.when(jnp.logical_not(own))
    def _():
        greet(dev(s, s, xh, z))
        greet(dev(y, y, xh, z))

    for cp in loads:
        cp.wait()

    lane = lax.broadcasted_iota(jnp.int32, (QR, 128), 1)
    for t in range(NS):
        cols = slice(t * GF, (t + 1) * GF)
        qf = qv[0, :, cols].astype(F32)
        df = dov[0, :, cols].astype(F32)
        prod = df * ov[0, :, cols].astype(F32)
        both = jnp.concatenate([qf, df], axis=0).astype(BF16)
        tile = jnp.zeros((QR, 128), F32)
        for h in range(HG):
            pk[t, h] = both[:, h * HD:(h + 1) * HD]
            d = jnp.sum(prod[:, h * HD:(h + 1) * HD], axis=1, keepdims=True)
            tile = jnp.where(lane == h, d, tile)
        hi = tile.astype(BF16).astype(F32)
        mid = (tile - hi).astype(BF16).astype(F32)
        lo = tile - hi - mid
        pk[t, HG] = jnp.concatenate([hi + pltpu.roll(lo, QR, 1), mid], axis=0).astype(BF16)

    pl.semaphore_wait(bar, count + 2 - 2 * own.astype(jnp.int32))

    mine = xh * NY + y
    for k in range(NX):
        for i in range(NS):
            t = up(s, i, NS)
            cp = rc(pk.at[t], p1.at[mine], s1.at[i, k], r1.at[k, y], dev(t, s, up(xh, k, NX), z))
            if (i, k) == (0, 0):
                self_in = cp

                @pl.when(jnp.logical_not(own))
                def _():
                    cp.start()
            else:
                go(cp)

    @pl.when(own)
    def _():
        p1[mine] = pk[s]

    dyr, dyl = dev(s, yr, xh, z), dev(s, yl, xh, z)
    for h in range(HG):
        kv[y, h, 0] = kin[:, h * HD:(h + 1) * HD]
        kv[y, h, 1] = vin[:, h * HD:(h + 1) * HD]
        for i, (h0, n) in enumerate(PIECES):
            if h == h0 + n - 1:
                ref = kv.at[y, pl.ds(h0, n)]
                go(rc(ref, ref, sy.at[0, i], ry.at[0, i], dyr))
                go(rc(ref, ref, sy.at[1, i], ry.at[1, i], dyl))

    def kv_forward(i):
        hs = pl.ds(*PIECES[i])
        arrived(kv.at[yl, hs], ry.at[0, i])
        go(rc(kv.at[yl, hs, 0], kv.at[yl, hs, 0], sf.at[0, i], rf.at[0, i], dyr))
        arrived(kv.at[yr, hs], ry.at[1, i])
        go(rc(kv.at[yr, hs, 1], kv.at[yr, hs, 1], sf.at[1, i], rf.at[1, i], dyl))

    def kv_ready(i):
        hs = pl.ds(*PIECES[i])
        arrived(kv.at[y2, hs, 0], rf.at[0, i])
        arrived(kv.at[y2, hs, 1], rf.at[1, i])

    kcol = lax.broadcasted_iota(jnp.int32, (1, KV), 1)
    kblk = kcol // KR
    base = jnp.zeros((1, KV), jnp.int32)
    for b in range(NY):
        base = jnp.where(kblk == b, order[(b * NX + xh) * NZ + z], base)
    kpos = base * KR + kcol % KR
    first = NY * NX * NZ * KR - QW
    zrow = lax.broadcasted_iota(jnp.int32, (ZR, 1), 0)
    zpos = first + (((zrow // QR) % NY) * NX + zrow // (NY * QR)) * NZ * QR + zrow % QR

    for k in range(NX):
        for b in range(NY):
            slot = dn(xh, k, NX) * NY + b
            if k == 0:
                @pl.when(jnp.logical_not(own & (y == b)))
                def _():
                    arrived(p1.at[slot], r1.at[k, b])
            else:
                arrived(p1.at[slot], r1.at[k, b])
    zr, zl = up(z, 1, NZ), dn(z, 1, NZ)
    dzr, dzl = dev(s, y, xh, zr), dev(s, y, xh, zl)
    dz2r, dz2l = dev(s, y, xh, up(z, 2, NZ)), dev(s, y, xh, dn(z, 2, NZ))
    half = NB // 2

    def zref(d, t, i, part):
        src = dn(z, t, NZ) if d == 0 else up(z, t, NZ)
        hs = pl.ds(*PIECES[i])
        return g.at[src, hs, pl.ds(d * half, half)] if part else g.at[src, hs]

    def zsend(d, t, i):
        last = t == NT
        ref = zref(d, 2 if last else t - 1, i, last)
        to = (dz2r if d == 0 else dz2l) if last else (dzr if d == 0 else dzl)
        go(rc(ref, ref, sz.at[d, t - 1, i], rz.at[d, t - 1, i], to))

    def zwait(d, t, i):
        arrived(zref(d, t, i, t == NT), rz.at[d, t - 1, i])

    def dsend(d, t):
        n = 2 if t == NT else t - 1
        ref = gd.at[dn(z, n, NZ) if d == 0 else up(z, n, NZ)]
        to = dz2r if t == NT else (dzr if d == 0 else dzl)
        go(rc(ref, ref, szd.at[d, t - 1], rzd.at[d, t - 1], to))

    def dwait(d, t):
        arrived(gd.at[dn(z, t, NZ) if d == 0 else up(z, t, NZ)], rzd.at[d, t - 1])

    def delta_rows(zc):
        tile = gd[zc]
        for b in range(NB):
            piece = tile if b == 0 else pltpu.roll(tile, 128 - b * QR, 1)
            delc[pl.ds(pl.multiple_of(zc * ZR + b * QR, QR), QR)] = piece

    def chunks(t):
        return (z, up(z, NT, NZ)) if t == NT else (dn(z, t, NZ), up(z, t, NZ))

    def rowsof(zc):
        return pl.ds(pl.multiple_of(zc * ZR, ZR), ZR)

    def pair(ref, h, t):
        a, b = chunks(t)
        return jnp.concatenate([ref[h, rowsof(a)], ref[h, rowsof(b)]], axis=0)

    def put(ref, h, t, v):
        a, b = chunks(t)
        ref[h, rowsof(a)] = v[:ZR]
        ref[h, rowsof(b)] = v[ZR:]

    def score_tile(h, t):
        qs_, ds_ = [], []
        for zc in chunks(t):
            blk = g[zc, h].astype(F32).reshape(NB, 2, QR, HD)
            qc = blk[:, 0].reshape(ZR, HD).astype(BF16)
            dc = blk[:, 1].reshape(ZR, HD).astype(BF16)
            q3[h, rowsof(zc)] = qc
            do3[h, rowsof(zc)] = dc
            qs_.append(qc)
            ds_.append(dc)
        kh = kv[:, h, 0].reshape(KV, HD)
        sc = nt(jnp.concatenate(qs_, axis=0), kh) * SCALE
        a, b = chunks(t)
        qpos = jnp.concatenate([zpos + a * QR, zpos + b * QR], axis=0)
        sc = jnp.where(kpos <= qpos, sc, MASKED)
        m = jnp.max(sc, axis=1, keepdims=True)
        p = jnp.exp(sc - m)
        l = jnp.sum(p, axis=1, keepdims=True)
        put(pb, h, t, p.astype(BF16))
        put(m3, h, t, jnp.broadcast_to(m, (RT, 128)))
        put(lse3, h, t, jnp.broadcast_to(m + jnp.log(l), (RT, 128)))
        if t == NT:
            pl_[h] = p
        else:
            dprob(h, t, p, jnp.concatenate(ds_, axis=0))

    def dprob(h, t, p, dom):
        vh = kv[:, h, 1].reshape(KV, HD)
        a, b = chunks(t)
        dl = jnp.concatenate([delc[rowsof(a)], delc[rowsof(b)]], axis=0)[:, h:h + 1]
        put(db, h, t, (p * (nt(dom, vh) - dl) * SCALE).astype(BF16))

    def dprob_late(h):
        dprob(h, NT, pl_[h], pair(do3, h, NT))
        kh = kv[:, h, 0].reshape(KV, HD)
        dqa[h] = nn(db[h], kh).reshape(NZ, ZR, HD)

    lane2 = lax.broadcasted_iota(jnp.int32, (RT, 128), 1)

    def columns(rows_):
        pad = jnp.zeros((128 - rows_.shape[0], 128), F32)
        return jnp.concatenate([rows_, pad], axis=0).T

    def heads_of(i):
        return range(PIECES[i][0], PIECES[i][0] + PIECES[i][1])

    def stats_send(i):
        st = jnp.zeros((RT, 128), F32)
        for j, h in enumerate(heads_of(i)):
            for rt in range(NR):
                st = jnp.where(lane2 == j * NR + rt, lse3[h, rt * RT:(rt + 1) * RT], st)
        sr = pl.ds(0, SROWS[i])
        lx[i, 0, sr] = st.T[:SROWS[i]]
        go(rc(lx.at[i, 0, sr], lx.at[i, 1, sr], sx.at[i], rx.at[i], dev(s, y, up(xh, 1, NX), z)))

    def stats_pair(i):
        sr = pl.ds(0, SROWS[i])
        arrived(lx.at[i, 1, sr], rx.at[i])
        a, b = lx[i, 0, sr], lx[i, 1, sr]
        mx = jnp.maximum(a, b)
        both = mx + jnp.log(jnp.exp(a - mx) + jnp.exp(b - mx))
        lz[i, z, sr] = both
        for j in range(1, NZ):
            ref = lz.at[i, z, sr]
            go(rc(ref, ref, sl.at[i, j], rl.at[i, j], dev(s, y, xh, up(z, j, NZ))))
        tt = columns(both)
        for j, h in enumerate(heads_of(i)):
            for rt in range(NR):
                k = j * NR + rt
                lse3[h, rt * RT:(rt + 1) * RT] = jnp.broadcast_to(tt[:, k:k + 1], (RT, 128))

    def stats_wait(i):
        sr = pl.ds(0, SROWS[i])
        for j in range(1, NZ):
            arrived(lz.at[i, dn(z, j, NZ), sr], rl.at[i, j])
        mx = lz[i, 0, sr]
        for f in range(1, NZ):
            mx = jnp.maximum(mx, lz[i, f, sr])
        tot = jnp.exp(lz[i, 0, sr] - mx)
        for f in range(1, NZ):
            tot = tot + jnp.exp(lz[i, f, sr] - mx)
        lt = mx + jnp.log(tot)
        tt = columns(lt)
        for j, h in enumerate(heads_of(i)):
            for rt in range(NR):
                rows = slice(rt * RT, (rt + 1) * RT)
                k = j * NR + rt
                col = jnp.broadcast_to(tt[:, k:k + 1], (RT, 128))
                c3[h, rows] = jnp.exp(m3[h, rows] - col)
        return lt

    def weights(i, lt):
        sr = pl.ds(0, SROWS[i])
        for k, n in enumerate((-2, -1, 0, 1, 2)):
            wt[i, k] = columns(jnp.exp(lz[i, up(z, n, NZ), sr] - lt))

    lane3 = lax.broadcasted_iota(jnp.int32, (ZR, 128), 1)

    def weight(n, zc, h):
        i = 0 if h < PIECES[1][0] else 1
        v = wt[i, n + 2, pl.ds(pl.multiple_of((zc & 1) * ZR, ZR), ZR)]
        v = jnp.where(lane3 == (h - PIECES[i][0]) * NR + (zc >> 1), v, 0.0)
        return jnp.sum(v, axis=1, keepdims=True)

    for h in range(HG):
        for b in range(NB):
            g[z, h, b] = p1[b, h]
    tile = jnp.zeros((QR, 128), F32)
    for b in range(NB):
        d2 = p1[b, HG].astype(F32)
        top = d2[:QR]
        d1 = jnp.where(lane < QR, top + d2[QR:] + pltpu.roll(top, 128 - QR, 1), 0.0)
        tile = tile + (d1 if b == 0 else pltpu.roll(d1, b * QR, 1))
    gd[z] = tile

    for i in range(2):
        zsend(0, 1, i)
        zsend(1, 1, i)
        if i == 0:
            dsend(0, 1)
            dsend(1, 1)
    kv_forward(0)
    for t in range(2, NT + 2):
        for i, (h0, n) in enumerate(PIECES):
            zwait(0, t - 1, i)
            zwait(1, t - 1, i)
            for n_ in (t, t + 1):
                if n_ == t < NT or n_ == NT == t + 1:
                    zsend(0, n_, i)
                    zsend(1, n_, i)
            if i == 0:
                dwait(0, t - 1)
                if t <= NT:
                    dwait(1, t - 1)
                if t < NT:
                    dsend(0, t)
                    dsend(1, t)
                if t == NT - 1:
                    dsend(0, NT)
                for zc in chunks(t - 1):
                    delta_rows(zc)
            if t == 2:
                if i == 0:
                    kv_forward(1)
                kv_ready(i)
            for h in range(h0, h0 + n):
                score_tile(h, t - 1)
            if t == NT + 1:
                if i == 0:
                    ring_sends = len(sends)
                stats_send(i)

    HR = ZR // 2

    def zmsg(d, kind, i):
        hs = pl.ds(*PIECES[i])
        a_, b_ = zs.at[d, kind, hs], zr_.at[d, kind, hs]
        if kind == 0:
            part = pl.ds(d * HR, HR)
            a_, b_ = zs.at[d, kind, hs, part], zr_.at[d, kind, hs, part]
        near, far = (dzr, dz2r) if d == 0 else (dzl, dz2l)
        return rc(a_, b_, sg.at[d, kind, i], rg.at[d, kind, i], far if kind in (0, 3) else near)

    def step(d, n):
        return up(z, n, NZ) if d == 0 else dn(z, n, NZ)

    def query_scale(i):
        for h in heads_of(i):
            dqa[h] = dqa[h] * jnp.exp(m3[h] - lse3[h]).reshape(NZ, ZR, HD)

    def query_send(i, kind, n):
        for d in range(2):
            for h in heads_of(i):
                if kind == 0:
                    part = slice(d * HR, (d + 1) * HR)
                    zs[d, kind, h, part] = dqa[h, step(d, n), part].astype(BF16)
                else:
                    zs[d, kind, h] = dqa[h, step(d, n)].astype(BF16)
            go(zmsg(d, kind, i))

    def query_relay(i):
        for d in range(2):
            sign = 1 - 2 * d
            zmsg(d, 0, i).wait_recv()
            zmsg(d, 1, i).wait_recv()
            part = slice(d * HR, (d + 1) * HR)
            rest = slice((1 - d) * HR, (2 - d) * HR)
            to = step(d, 2)
            for h in heads_of(i):
                acc = dqa[h, to] * weight(0, to, h) + zr_[d, 1, h].astype(F32) * weight(-sign, to, h)
                far = zr_[d, 0, h, part].astype(F32) * weight(-2 * sign, to, h)[part]
                zs[d, 3, h, rest] = acc[rest].astype(BF16)
                zs[d, 3, h, part] = (acc[part] + far).astype(BF16)
            go(zmsg(d, 3, i))

    def query_sum(i):
        for d in range(2):
            zmsg(d, 2, i).wait_recv()
            zmsg(d, 3, i).wait_recv()
        for h in heads_of(i):
            acc = dqa[h, z] * weight(0, z, h)
            for d in range(2):
                acc = acc + zr_[d, 3, h].astype(F32)
                acc = acc + zr_[d, 2, h].astype(F32) * weight(2 * d - 1, z, h)
            tb[:, h] = acc.reshape(NB, QR, HD)

    def cache_grads(h):
        cc = c3[h]
        dkt = tn((q3[h].astype(F32) * cc).astype(BF16), db[h])
        dvt = tn((do3[h].astype(F32) * cc).astype(BF16), pb[h])
        for b in range(NY):
            dkv[h, b, 0] = dkt[:, b * KR:(b + 1) * KR].T
            dkv[h, b, 1] = dvt[:, b * KR:(b + 1) * KR].T
        ks1[h, 0, 0] = dkv[h, y2, 0].astype(BF16)
        ks1[h, 0, 1] = dkv[h, yr, 1].astype(BF16)
        ks1[h, 1, 0] = dkv[h, y2, 1].astype(BF16)
        ks1[h, 1, 1] = dkv[h, yl, 0].astype(BF16)
        go(leg(h, 0, 0, dyr))
        go(leg(h, 1, 0, dyl))

    def leg(h, d, i, to):
        return rc(ks1.at[h, d, i], kr1.at[h, d, i], sk.at[i, d, h], rk.at[i, d, h], to)

    def near_blocks(h):
        go(leg(h, 0, 1, dyr))
        go(leg(h, 1, 1, dyl))

    def second_leg(h):
        arrived(kr1.at[h, 0, 0], rk.at[0, 0, h])
        ks2[h, 0] = (dkv[h, yr, 0] + kr1[h, 0, 0].astype(F32)).astype(BF16)
        go(rc(ks2.at[h, 0], kr2.at[h, 0], sk.at[2, 0, h], rk.at[2, 0, h], dyr))
        arrived(kr1.at[h, 1, 0], rk.at[0, 1, h])
        ks2[h, 1] = (dkv[h, yl, 1] + kr1[h, 1, 0].astype(F32)).astype(BF16)
        go(rc(ks2.at[h, 1], kr2.at[h, 1], sk.at[2, 1, h], rk.at[2, 1, h], dyl))

    def cache_out(h):
        arrived(kr1.at[h, 0, 1], rk.at[1, 0, h])
        arrived(kr1.at[h, 1, 1], rk.at[1, 1, h])
        arrived(kr2.at[h, 0], rk.at[2, 0, h])
        arrived(kr2.at[h, 1], rk.at[2, 1, h])
        cols = slice(h * HD, (h + 1) * HD)
        dk_out[:, cols] = (dkv[h, y, 0] + kr1[h, 1, 1].astype(F32) + kr2[h, 0].astype(F32)).astype(BF16)
        dv_out[:, cols] = (dkv[h, y, 1] + kr1[h, 0, 1].astype(F32) + kr2[h, 1].astype(F32)).astype(BF16)

    dprob_late(0)
    settle(ring_sends)
    stats_pair(0)
    for h in heads_of(0):
        if h > 0:
            dprob_late(h)
    query_scale(0)
    query_send(0, 1, 3)
    query_send(0, 0, 4)
    stats_pair(1)
    for h in heads_of(1):
        dprob_late(h)
    query_scale(1)
    query_send(1, 1, 3)
    query_send(1, 0, 4)
    early = len(sends)
    query_send(0, 2, 1)
    query_send(1, 2, 1)
    total = stats_wait(0)
    cache_grads(0)
    weights(0, total)
    query_relay(0)
    near_blocks(0)
    cache_grads(1)
    near_blocks(1)
    total = stats_wait(1)
    cache_grads(2)
    near_blocks(2)
    weights(1, total)
    query_relay(1)
    cache_grads(3)
    near_blocks(3)
    cache_grads(4)
    near_blocks(4)
    settle(early)
    second_leg(0)
    query_sum(0)
    second_leg(1)
    second_leg(2)
    query_sum(1)

    for j in range(NY):
        for k in range(NX):
            ty, tx = up(y, j, NY), up(xh, k, NX)
            cp = rc(tb.at[tx * NY + ty], p8.at[k, s], s8.at[j, k], r8.at[k, s], dev(y, ty, tx, z))
            if (j, k) == (0, 0):
                self_out = cp

                @pl.when(jnp.logical_not(own))
                def _():
                    cp.start()
            else:
                go(cp)

    @pl.when(own)
    def _():
        p8[0, s] = tb[mine]

    second_leg(3)
    second_leg(4)
    for h in range(HG):
        cache_out(h)

    for k in range(NX):
        for b in range(NS):
            if k == 0:
                @pl.when(jnp.logical_not(own & (s == b)))
                def _():
                    arrived(p8.at[k, b], r8.at[k, b])
            else:
                arrived(p8.at[k, b], r8.at[k, b])
    for b in range(NS):
        for h in range(HG):
            col = b * GF + h * HD
            dq_out[0, :, col:col + HD] = (p8[0, b, h] + p8[1, b, h]).astype(BF16)

    @pl.when(jnp.logical_not(own))
    def _():
        self_in.wait_send()
        self_out.wait_send()

    for cp in sends:
        cp.wait_send()


def place(a, b, c, x, y, z):
    x[...] = a[...]
    y[...] = b[...]
    z[...] = c[...]


def local(block_order, queries, cache_keys, cache_values, attention_out, output_grad):
    dma = pltpu.SemaphoreType.DMA
    vm = pltpu.VMEM
    row = queries.shape
    scratch = [
        vm(row, BF16), vm(row, BF16), vm(row, BF16), vm((KR, GF), BF16), vm((KR, GF), BF16),
        vm((NS, HG + 1, 16, HD), BF16), vm((NB, HG + 1, 16, HD), BF16),
        vm((NZ, HG, NB, 16, HD), BF16), vm((NZ, QR, 128), F32),
        vm((NY, HG, 2, KR, HD), BF16), vm((HG, QW, HD), BF16), vm((HG, QW, HD), BF16), vm((QW, 128), F32),
        vm((HG, RT, KV), F32), vm((HG, QW, KV), BF16), vm((HG, QW, KV), BF16),
        vm((HG, QW, 128), F32), vm((HG, QW, 128), F32), vm((HG, QW, 128), F32),
        vm((2, 2, 16, 128), F32), vm((2, NZ, 16, 128), F32), vm((2, 5, 128, 128), F32),
        vm((HG, NZ, ZR, HD), F32), vm((2, 4, HG, ZR, HD), BF16), vm((2, 4, HG, ZR, HD), BF16),
        vm((HG, NY, 2, KR, HD), F32),
        vm((HG, 2, 2, KR, HD), BF16), vm((HG, 2, 2, KR, HD), BF16),
        vm((HG, 2, KR, HD), BF16), vm((HG, 2, KR, HD), BF16),
        vm((NB, HG, QR, HD), F32), vm((NX, NS, HG, QR, HD), F32),
        dma((5,)), dma((NS, NX)), dma((NX, NY)),
        dma((2, NT, 2)), dma((2, NT, 2)), dma((2, NT)), dma((2, NT)),
        dma((2, 2)), dma((2, 2)), dma((2, 2)), dma((2, 2)),
        dma((2, NZ)), dma((2, NZ)), dma((2,)), dma((2,)), dma((2, 4, 2)), dma((2, 4, 2)),
        dma((3, 2, HG)), dma((3, 2, HG)), dma((NY, NX)), dma((NX, NS)),
    ]
    vspec = pl.BlockSpec(memory_space=pltpu.VMEM)
    hbm = pl.BlockSpec(memory_space=pl.ANY)
    dq, dk, dv = pl.pallas_call(
        kernel,
        out_shape=(
            jax.ShapeDtypeStruct((1, QR, NS * GF), BF16),
            jax.ShapeDtypeStruct((KR, GF), BF16),
            jax.ShapeDtypeStruct((KR, GF), BF16),
        ),
        in_specs=[pl.BlockSpec(memory_space=pltpu.SMEM)] + [hbm] * 5,
        out_specs=(vspec, vspec, vspec),
        scratch_shapes=scratch,
        compiler_params=pltpu.CompilerParams(
            collective_id=0, has_side_effects=True, vmem_limit_bytes=56 << 20),
    )(block_order, queries, output_grad, attention_out, cache_keys, cache_values)
    return pl.pallas_call(
        place,
        out_shape=tuple(jax.ShapeDtypeStruct(v.shape, v.dtype) for v in (dq, dk, dv)),
        in_specs=[vspec] * 3,
        out_specs=(vspec,) * 3,
    )(dq, dk, dv)


def solution(mesh):
    in_specs = (
        P(),
        P("section", "ctx", None),
        P("ctx", "section"),
        P("ctx", "section"),
        P("section", "ctx", None),
        P("section", "ctx", None),
    )
    out_specs = (P("section", "ctx", None), P("ctx", "section"), P("ctx", "section"))
    return jax.shard_map(local, mesh=mesh, in_specs=in_specs, out_specs=out_specs, check_vma=False)
```

```python
import jax
import jax.numpy as jnp
from jax import lax
from jax.experimental import pallas as pl
from jax.experimental.pallas import tpu as pltpu
from jax.sharding import PartitionSpec as P

MESH = pl.DeviceIdType.MESH
F32 = jnp.float32
BF16 = jnp.bfloat16

NS, NY, NX, NZ = 4, 4, 2, 8
HG, HD, GF = 5, 128, 640
KR = 128
KV = NY * KR
QR = 8
NB = NX * NY
ZR = NB * QR
QW = NZ * ZR
NT = NZ // 2
SCALE = HD ** -0.5
MASKED = -1e30
RT = 128
NR = QW // RT
PIECES = ((0, 2), (2, 3))
SROWS = (8, 16)


def nt(a, b):
    return lax.dot_general(a, b, (((1,), (1,)), ((), ())), preferred_element_type=F32)


def tn(a, b):
    return lax.dot_general(a, b, (((0,), (0,)), ((), ())), preferred_element_type=F32)


def nn(a, b):
    return lax.dot_general(a, b, (((1,), (0,)), ((), ())), preferred_element_type=F32)


def kernel(order, q_in, do_in, o_in, k_in, v_in, dq_out, dk_out, dv_out,
           qv, dov, ov, kin, vin, pk, p1, g, gd, kv, q3, do3, delc, pl_, pb, db, m3, lse3, c3, lx, lz, wt,
           dqa, zs, zr_, dkv, ks1, kr1, ks2, kr2, tb, p8,
           sin, s1, r1, sz, rz, szd, rzd, sy, ry, sf, rf, sl, rl, sx, rx, sg, rg, sk, rk, s8, r8):
    s = lax.axis_index("section")
    c = lax.axis_index("ctx")
    y = c >> 4
    xh = (c >> 3) & 1
    z = c & 7
    me = (s, c)
    own = s == y

    def dev(s_, y_, x_, z_):
        return (s_, (y_ << 4) | (x_ << 3) | z_)

    def rc(src, dst, ssem, rsem, to):
        return pltpu.make_async_remote_copy(
            src_ref=src, dst_ref=dst, send_sem=ssem, recv_sem=rsem,
            device_id=to, device_id_type=MESH)

    def arrived(dst, rsem):
        rc(dst, dst, rsem, rsem, me).wait_recv()

    def up(v, n, mod):
        return (v + n) & (mod - 1)

    def dn(v, n, mod):
        return (v - n) & (mod - 1)

    sends = []

    def go(cp):
        cp.start()
        sends.append(cp)

    def settle(count_):
        for cp in sends[:count_]:
            cp.wait_send()
        del sends[:count_]

    loads = []
    for i, (a, b) in enumerate(((q_in, qv), (do_in, dov), (o_in, ov), (k_in, kin), (v_in, vin))):
        cp = pltpu.make_async_copy(a, b, sin.at[i])
        cp.start()
        loads.append(cp)

    yr, yl, y2 = up(y, 1, NY), dn(y, 1, NY), up(y, 2, NY)
    bar = pltpu.get_barrier_semaphore()

    def greet(to):
        pl.semaphore_signal(bar, inc=1, device_id=to, device_id_type=MESH)

    count = 0
    for j in range(1, NZ):
        greet(dev(s, y, xh, up(z, j, NZ)))
        count += 1
    for t in (dev(s, yr, xh, z), dev(s, yl, xh, z), dev(s, y, up(xh, 1, NX), z)):
        greet(t)
        count += 1
    for i in range(4):
        for k in range(NX):
            if (i, k) != (0, 0):
                greet(dev(up(s, i, NS), s, up(xh, k, NX), z))
                greet(dev(y, up(y, i, NY), up(xh, k, NX), z))
                count += 2

    @pl.when(jnp.logical_not(own))
    def _():
        greet(dev(s, s, xh, z))
        greet(dev(y, y, xh, z))

    for cp in loads:
        cp.wait()

    lane = lax.broadcasted_iota(jnp.int32, (QR, 128), 1)
    for t in range(NS):
        cols = slice(t * GF, (t + 1) * GF)
        qf = qv[0, :, cols].astype(F32)
        df = dov[0, :, cols].astype(F32)
        prod = df * ov[0, :, cols].astype(F32)
        both = jnp.concatenate([qf, df], axis=0).astype(BF16)
        tile = jnp.zeros((QR, 128), F32)
        for h in range(HG):
            pk[t, h] = both[:, h * HD:(h + 1) * HD]
            d = jnp.sum(prod[:, h * HD:(h + 1) * HD], axis=1, keepdims=True)
            tile = jnp.where(lane == h, d, tile)
        hi = tile.astype(BF16).astype(F32)
        mid = (tile - hi).astype(BF16).astype(F32)
        lo = tile - hi - mid
        pk[t, HG] = jnp.concatenate([hi + pltpu.roll(lo, QR, 1), mid], axis=0).astype(BF16)

    pl.semaphore_wait(bar, count + 2 - 2 * own.astype(jnp.int32))

    mine = xh * NY + y
    for k in range(NX):
        for i in range(NS):
            t = up(s, i, NS)
            cp = rc(pk.at[t], p1.at[mine], s1.at[i, k], r1.at[k, y], dev(t, s, up(xh, k, NX), z))
            if (i, k) == (0, 0):
                self_in = cp

                @pl.when(jnp.logical_not(own))
                def _():
                    cp.start()
            else:
                go(cp)

    @pl.when(own)
    def _():
        p1[mine] = pk[s]

    dyr, dyl = dev(s, yr, xh, z), dev(s, yl, xh, z)
    for h in range(HG):
        kv[y, h, 0] = kin[:, h * HD:(h + 1) * HD]
        kv[y, h, 1] = vin[:, h * HD:(h + 1) * HD]
        for i, (h0, n) in enumerate(PIECES):
            if h == h0 + n - 1:
                ref = kv.at[y, pl.ds(h0, n)]
                go(rc(ref, ref, sy.at[0, i], ry.at[0, i], dyr))
                go(rc(ref, ref, sy.at[1, i], ry.at[1, i], dyl))

    def kv_forward(i):
        hs = pl.ds(*PIECES[i])
        arrived(kv.at[yl, hs], ry.at[0, i])
        go(rc(kv.at[yl, hs, 0], kv.at[yl, hs, 0], sf.at[0, i], rf.at[0, i], dyr))
        arrived(kv.at[yr, hs], ry.at[1, i])
        go(rc(kv.at[yr, hs, 1], kv.at[yr, hs, 1], sf.at[1, i], rf.at[1, i], dyl))

    def kv_ready(i):
        hs = pl.ds(*PIECES[i])
        arrived(kv.at[y2, hs, 0], rf.at[0, i])
        arrived(kv.at[y2, hs, 1], rf.at[1, i])

    kcol = lax.broadcasted_iota(jnp.int32, (1, KV), 1)
    kblk = kcol // KR
    base = jnp.zeros((1, KV), jnp.int32)
    for b in range(NY):
        base = jnp.where(kblk == b, order[(b * NX + xh) * NZ + z], base)
    kpos = base * KR + kcol % KR
    first = NY * NX * NZ * KR - QW
    zrow = lax.broadcasted_iota(jnp.int32, (ZR, 1), 0)
    zpos = first + (((zrow // QR) % NY) * NX + zrow // (NY * QR)) * NZ * QR + zrow % QR

    for k in range(NX):
        for b in range(NY):
            slot = dn(xh, k, NX) * NY + b
            if k == 0:
                @pl.when(jnp.logical_not(own & (y == b)))
                def _():
                    arrived(p1.at[slot], r1.at[k, b])
            else:
                arrived(p1.at[slot], r1.at[k, b])
    zr, zl = up(z, 1, NZ), dn(z, 1, NZ)
    dzr, dzl = dev(s, y, xh, zr), dev(s, y, xh, zl)
    dz2r, dz2l = dev(s, y, xh, up(z, 2, NZ)), dev(s, y, xh, dn(z, 2, NZ))
    half = NB // 2

    def zref(d, t, i, part):
        src = dn(z, t, NZ) if d == 0 else up(z, t, NZ)
        hs = pl.ds(*PIECES[i])
        return g.at[src, hs, pl.ds(d * half, half)] if part else g.at[src, hs]

    def zsend(d, t, i):
        last = t == NT
        ref = zref(d, 2 if last else t - 1, i, last)
        to = (dz2r if d == 0 else dz2l) if last else (dzr if d == 0 else dzl)
        go(rc(ref, ref, sz.at[d, t - 1, i], rz.at[d, t - 1, i], to))

    def zwait(d, t, i):
        arrived(zref(d, t, i, t == NT), rz.at[d, t - 1, i])

    def dsend(d, t):
        n = 2 if t == NT else t - 1
        ref = gd.at[dn(z, n, NZ) if d == 0 else up(z, n, NZ)]
        to = dz2r if t == NT else (dzr if d == 0 else dzl)
        go(rc(ref, ref, szd.at[d, t - 1], rzd.at[d, t - 1], to))

    def dwait(d, t):
        arrived(gd.at[dn(z, t, NZ) if d == 0 else up(z, t, NZ)], rzd.at[d, t - 1])

    def delta_rows(zc):
        tile = gd[zc]
        for b in range(NB):
            piece = tile if b == 0 else pltpu.roll(tile, 128 - b * QR, 1)
            delc[pl.ds(pl.multiple_of(zc * ZR + b * QR, QR), QR)] = piece

    def chunks(t):
        return (z, up(z, NT, NZ)) if t == NT else (dn(z, t, NZ), up(z, t, NZ))

    def rowsof(zc):
        return pl.ds(pl.multiple_of(zc * ZR, ZR), ZR)

    def pair(ref, h, t):
        a, b = chunks(t)
        return jnp.concatenate([ref[h, rowsof(a)], ref[h, rowsof(b)]], axis=0)

    def put(ref, h, t, v):
        a, b = chunks(t)
        ref[h, rowsof(a)] = v[:ZR]
        ref[h, rowsof(b)] = v[ZR:]

    def score_tile(h, t):
        qs_, ds_ = [], []
        for zc in chunks(t):
            blk = g[zc, h].astype(F32).reshape(NB, 2, QR, HD)
            qc = blk[:, 0].reshape(ZR, HD).astype(BF16)
            dc = blk[:, 1].reshape(ZR, HD).astype(BF16)
            q3[h, rowsof(zc)] = qc
            do3[h, rowsof(zc)] = dc
            qs_.append(qc)
            ds_.append(dc)
        kh = kv[:, h, 0].reshape(KV, HD)
        sc = nt(jnp.concatenate(qs_, axis=0), kh) * SCALE
        a, b = chunks(t)
        qpos = jnp.concatenate([zpos + a * QR, zpos + b * QR], axis=0)
        sc = jnp.where(kpos <= qpos, sc, MASKED)
        m = jnp.max(sc, axis=1, keepdims=True)
        p = jnp.exp(sc - m)
        l = jnp.sum(p, axis=1, keepdims=True)
        put(pb, h, t, p.astype(BF16))
        put(m3, h, t, jnp.broadcast_to(m, (RT, 128)))
        put(lse3, h, t, jnp.broadcast_to(m + jnp.log(l), (RT, 128)))
        if t == NT:
            pl_[h] = p
        else:
            dprob(h, t, p, jnp.concatenate(ds_, axis=0))

    def dprob(h, t, p, dom):
        vh = kv[:, h, 1].reshape(KV, HD)
        a, b = chunks(t)
        dl = jnp.concatenate([delc[rowsof(a)], delc[rowsof(b)]], axis=0)[:, h:h + 1]
        put(db, h, t, (p * (nt(dom, vh) - dl) * SCALE).astype(BF16))

    def dprob_late(h):
        dprob(h, NT, pl_[h], pair(do3, h, NT))
        kh = kv[:, h, 0].reshape(KV, HD)
        dqa[h] = nn(db[h], kh).reshape(NZ, ZR, HD)

    lane2 = lax.broadcasted_iota(jnp.int32, (RT, 128), 1)

    def columns(rows_):
        pad = jnp.zeros((128 - rows_.shape[0], 128), F32)
        return jnp.concatenate([rows_, pad], axis=0).T

    def heads_of(i):
        return range(PIECES[i][0], PIECES[i][0] + PIECES[i][1])

    def stats_send(i):
        st = jnp.zeros((RT, 128), F32)
        for j, h in enumerate(heads_of(i)):
            for rt in range(NR):
                st = jnp.where(lane2 == j * NR + rt, lse3[h, rt * RT:(rt + 1) * RT], st)
        sr = pl.ds(0, SROWS[i])
        lx[i, 0, sr] = st.T[:SROWS[i]]
        go(rc(lx.at[i, 0, sr], lx.at[i, 1, sr], sx.at[i], rx.at[i], dev(s, y, up(xh, 1, NX), z)))

    def stats_pair(i):
        sr = pl.ds(0, SROWS[i])
        arrived(lx.at[i, 1, sr], rx.at[i])
        a, b = lx[i, 0, sr], lx[i, 1, sr]
        mx = jnp.maximum(a, b)
        both = mx + jnp.log(jnp.exp(a - mx) + jnp.exp(b - mx))
        lz[i, z, sr] = both
        for j in range(1, NZ):
            ref = lz.at[i, z, sr]
            go(rc(ref, ref, sl.at[i, j], rl.at[i, j], dev(s, y, xh, up(z, j, NZ))))
        tt = columns(both)
        for j, h in enumerate(heads_of(i)):
            for rt in range(NR):
                k = j * NR + rt
                lse3[h, rt * RT:(rt + 1) * RT] = jnp.broadcast_to(tt[:, k:k + 1], (RT, 128))

    def stats_wait(i):
        sr = pl.ds(0, SROWS[i])
        for j in range(1, NZ):
            arrived(lz.at[i, dn(z, j, NZ), sr], rl.at[i, j])
        mx = lz[i, 0, sr]
        for f in range(1, NZ):
            mx = jnp.maximum(mx, lz[i, f, sr])
        tot = jnp.exp(lz[i, 0, sr] - mx)
        for f in range(1, NZ):
            tot = tot + jnp.exp(lz[i, f, sr] - mx)
        lt = mx + jnp.log(tot)
        tt = columns(lt)
        for j, h in enumerate(heads_of(i)):
            for rt in range(NR):
                rows = slice(rt * RT, (rt + 1) * RT)
                k = j * NR + rt
                col = jnp.broadcast_to(tt[:, k:k + 1], (RT, 128))
                c3[h, rows] = jnp.exp(m3[h, rows] - col)
        return lt

    def weights(i, lt):
        sr = pl.ds(0, SROWS[i])
        for k, n in enumerate((-2, -1, 0, 1, 2)):
            wt[i, k] = columns(jnp.exp(lz[i, up(z, n, NZ), sr] - lt))

    lane3 = lax.broadcasted_iota(jnp.int32, (ZR, 128), 1)

    def weight(n, zc, h):
        i = 0 if h < PIECES[1][0] else 1
        v = wt[i, n + 2, pl.ds(pl.multiple_of((zc & 1) * ZR, ZR), ZR)]
        v = jnp.where(lane3 == (h - PIECES[i][0]) * NR + (zc >> 1), v, 0.0)
        return jnp.sum(v, axis=1, keepdims=True)

    for h in range(HG):
        for b in range(NB):
            g[z, h, b] = p1[b, h]
    tile = jnp.zeros((QR, 128), F32)
    for b in range(NB):
        d2 = p1[b, HG].astype(F32)
        top = d2[:QR]
        d1 = jnp.where(lane < QR, top + d2[QR:] + pltpu.roll(top, 128 - QR, 1), 0.0)
        tile = tile + (d1 if b == 0 else pltpu.roll(d1, b * QR, 1))
    gd[z] = tile

    for i in range(2):
        zsend(0, 1, i)
        zsend(1, 1, i)
        if i == 0:
            dsend(0, 1)
            dsend(1, 1)
    kv_forward(0)
    def score_piece(t, i):
        if t == 1:
            kv_ready(i)
        if i == 0:
            for zc in chunks(t):
                delta_rows(zc)
        for h in heads_of(i):
            score_tile(h, t)

    pending = []
    for t in range(2, NT + 2):
        for i in range(2):
            for d in range(2):
                zwait(d, t - 1, i)
                for n_ in (t, t + 1):
                    if n_ == t < NT or n_ == NT == t + 1:
                        zsend(d, n_, i)
            if i == 0:
                dwait(0, t - 1)
                if t <= NT:
                    dwait(1, t - 1)
                if t < NT:
                    dsend(0, t)
                    dsend(1, t)
                if t == NT - 1:
                    dsend(0, NT)
                if t == 2:
                    kv_forward(1)
            pending.append((t - 1, i))
            while len(pending) > (2 if (t, i) < (NT - 1, 1) else 0):
                score_piece(*pending.pop(0))
            if t == NT + 1:
                if i == 0:
                    ring_sends = len(sends)
                stats_send(i)

    HR = ZR // 2

    def zmsg(d, kind, i):
        hs = pl.ds(*PIECES[i])
        a_, b_ = zs.at[d, kind, hs], zr_.at[d, kind, hs]
        if kind == 0:
            part = pl.ds(d * HR, HR)
            a_, b_ = zs.at[d, kind, hs, part], zr_.at[d, kind, hs, part]
        near, far = (dzr, dz2r) if d == 0 else (dzl, dz2l)
        return rc(a_, b_, sg.at[d, kind, i], rg.at[d, kind, i], far if kind in (0, 3) else near)

    def step(d, n):
        return up(z, n, NZ) if d == 0 else dn(z, n, NZ)

    def query_scale(i):
        for h in heads_of(i):
            dqa[h] = dqa[h] * jnp.exp(m3[h] - lse3[h]).reshape(NZ, ZR, HD)

    def query_send(i, kind, n):
        for d in range(2):
            for h in heads_of(i):
                if kind == 0:
                    part = slice(d * HR, (d + 1) * HR)
                    zs[d, kind, h, part] = dqa[h, step(d, n), part].astype(BF16)
                else:
                    zs[d, kind, h] = dqa[h, step(d, n)].astype(BF16)
            go(zmsg(d, kind, i))

    def query_relay(i):
        for d in range(2):
            sign = 1 - 2 * d
            zmsg(d, 0, i).wait_recv()
            zmsg(d, 1, i).wait_recv()
            part = slice(d * HR, (d + 1) * HR)
            rest = slice((1 - d) * HR, (2 - d) * HR)
            to = step(d, 2)
            for h in heads_of(i):
                acc = dqa[h, to] * weight(0, to, h) + zr_[d, 1, h].astype(F32) * weight(-sign, to, h)
                far = zr_[d, 0, h, part].astype(F32) * weight(-2 * sign, to, h)[part]
                zs[d, 3, h, rest] = acc[rest].astype(BF16)
                zs[d, 3, h, part] = (acc[part] + far).astype(BF16)
            go(zmsg(d, 3, i))

    def query_sum(i):
        for d in range(2):
            zmsg(d, 2, i).wait_recv()
            zmsg(d, 3, i).wait_recv()
        for h in heads_of(i):
            acc = dqa[h, z] * weight(0, z, h)
            for d in range(2):
                acc = acc + zr_[d, 3, h].astype(F32)
                acc = acc + zr_[d, 2, h].astype(F32) * weight(2 * d - 1, z, h)
            tb[:, h] = acc.reshape(NB, QR, HD)

    def cache_grads(h):
        cc = c3[h]
        dkt = tn((q3[h].astype(F32) * cc).astype(BF16), db[h])
        dvt = tn((do3[h].astype(F32) * cc).astype(BF16), pb[h])
        for b in range(NY):
            dkv[h, b, 0] = dkt[:, b * KR:(b + 1) * KR].T
            dkv[h, b, 1] = dvt[:, b * KR:(b + 1) * KR].T
        ks1[h, 0, 0] = dkv[h, y2, 0].astype(BF16)
        ks1[h, 0, 1] = dkv[h, yr, 1].astype(BF16)
        ks1[h, 1, 0] = dkv[h, y2, 1].astype(BF16)
        ks1[h, 1, 1] = dkv[h, yl, 0].astype(BF16)
        go(leg(h, 0, 0, dyr))
        go(leg(h, 1, 0, dyl))

    def leg(h, d, i, to):
        return rc(ks1.at[h, d, i], kr1.at[h, d, i], sk.at[i, d, h], rk.at[i, d, h], to)

    def near_blocks(h):
        go(leg(h, 0, 1, dyr))
        go(leg(h, 1, 1, dyl))

    def second_leg(h):
        arrived(kr1.at[h, 0, 0], rk.at[0, 0, h])
        ks2[h, 0] = (dkv[h, yr, 0] + kr1[h, 0, 0].astype(F32)).astype(BF16)
        go(rc(ks2.at[h, 0], kr2.at[h, 0], sk.at[2, 0, h], rk.at[2, 0, h], dyr))
        arrived(kr1.at[h, 1, 0], rk.at[0, 1, h])
        ks2[h, 1] = (dkv[h, yl, 1] + kr1[h, 1, 0].astype(F32)).astype(BF16)
        go(rc(ks2.at[h, 1], kr2.at[h, 1], sk.at[2, 1, h], rk.at[2, 1, h], dyl))

    def cache_out(h):
        arrived(kr1.at[h, 0, 1], rk.at[1, 0, h])
        arrived(kr1.at[h, 1, 1], rk.at[1, 1, h])
        arrived(kr2.at[h, 0], rk.at[2, 0, h])
        arrived(kr2.at[h, 1], rk.at[2, 1, h])
        cols = slice(h * HD, (h + 1) * HD)
        dk_out[:, cols] = (dkv[h, y, 0] + kr1[h, 1, 1].astype(F32) + kr2[h, 0].astype(F32)).astype(BF16)
        dv_out[:, cols] = (dkv[h, y, 1] + kr1[h, 0, 1].astype(F32) + kr2[h, 1].astype(F32)).astype(BF16)

    dprob_late(0)
    settle(ring_sends)
    stats_pair(0)
    for h in heads_of(0):
        if h > 0:
            dprob_late(h)
    query_scale(0)
    query_send(0, 1, 3)
    query_send(0, 0, 4)
    stats_pair(1)
    for h in heads_of(1):
        dprob_late(h)
    query_scale(1)
    query_send(1, 1, 3)
    query_send(1, 0, 4)
    early = len(sends)
    query_send(0, 2, 1)
    query_send(1, 2, 1)
    total = stats_wait(0)
    cache_grads(0)
    weights(0, total)
    query_relay(0)
    near_blocks(0)
    cache_grads(1)
    near_blocks(1)
    total = stats_wait(1)
    cache_grads(2)
    near_blocks(2)
    weights(1, total)
    query_relay(1)
    cache_grads(3)
    near_blocks(3)
    cache_grads(4)
    near_blocks(4)
    settle(early)
    second_leg(0)
    query_sum(0)
    second_leg(1)
    second_leg(2)
    query_sum(1)

    for j in range(NY):
        for k in range(NX):
            ty, tx = up(y, j, NY), up(xh, k, NX)
            cp = rc(tb.at[tx * NY + ty], p8.at[k, s], s8.at[j, k], r8.at[k, s], dev(y, ty, tx, z))
            if (j, k) == (0, 0):
                self_out = cp

                @pl.when(jnp.logical_not(own))
                def _():
                    cp.start()
            else:
                go(cp)

    @pl.when(own)
    def _():
        p8[0, s] = tb[mine]

    second_leg(3)
    second_leg(4)
    for h in range(HG):
        cache_out(h)

    for k in range(NX):
        for b in range(NS):
            if k == 0:
                @pl.when(jnp.logical_not(own & (s == b)))
                def _():
                    arrived(p8.at[k, b], r8.at[k, b])
            else:
                arrived(p8.at[k, b], r8.at[k, b])
    for b in range(NS):
        for h in range(HG):
            col = b * GF + h * HD
            dq_out[0, :, col:col + HD] = (p8[0, b, h] + p8[1, b, h]).astype(BF16)

    @pl.when(jnp.logical_not(own))
    def _():
        self_in.wait_send()
        self_out.wait_send()

    for cp in sends:
        cp.wait_send()


def place(a, b, c, x, y, z):
    x[...] = a[...]
    y[...] = b[...]
    z[...] = c[...]


def local(block_order, queries, cache_keys, cache_values, attention_out, output_grad):
    dma = pltpu.SemaphoreType.DMA
    vm = pltpu.VMEM
    row = queries.shape
    scratch = [
        vm(row, BF16), vm(row, BF16), vm(row, BF16), vm((KR, GF), BF16), vm((KR, GF), BF16),
        vm((NS, HG + 1, 16, HD), BF16), vm((NB, HG + 1, 16, HD), BF16),
        vm((NZ, HG, NB, 16, HD), BF16), vm((NZ, QR, 128), F32),
        vm((NY, HG, 2, KR, HD), BF16), vm((HG, QW, HD), BF16), vm((HG, QW, HD), BF16), vm((QW, 128), F32),
        vm((HG, RT, KV), F32), vm((HG, QW, KV), BF16), vm((HG, QW, KV), BF16),
        vm((HG, QW, 128), F32), vm((HG, QW, 128), F32), vm((HG, QW, 128), F32),
        vm((2, 2, 16, 128), F32), vm((2, NZ, 16, 128), F32), vm((2, 5, 128, 128), F32),
        vm((HG, NZ, ZR, HD), F32), vm((2, 4, HG, ZR, HD), BF16), vm((2, 4, HG, ZR, HD), BF16),
        vm((HG, NY, 2, KR, HD), F32),
        vm((HG, 2, 2, KR, HD), BF16), vm((HG, 2, 2, KR, HD), BF16),
        vm((HG, 2, KR, HD), BF16), vm((HG, 2, KR, HD), BF16),
        vm((NB, HG, QR, HD), F32), vm((NX, NS, HG, QR, HD), F32),
        dma((5,)), dma((NS, NX)), dma((NX, NY)),
        dma((2, NT, 2)), dma((2, NT, 2)), dma((2, NT)), dma((2, NT)),
        dma((2, 2)), dma((2, 2)), dma((2, 2)), dma((2, 2)),
        dma((2, NZ)), dma((2, NZ)), dma((2,)), dma((2,)), dma((2, 4, 2)), dma((2, 4, 2)),
        dma((3, 2, HG)), dma((3, 2, HG)), dma((NY, NX)), dma((NX, NS)),
    ]
    vspec = pl.BlockSpec(memory_space=pltpu.VMEM)
    hbm = pl.BlockSpec(memory_space=pl.ANY)
    dq, dk, dv = pl.pallas_call(
        kernel,
        out_shape=(
            jax.ShapeDtypeStruct((1, QR, NS * GF), BF16),
            jax.ShapeDtypeStruct((KR, GF), BF16),
            jax.ShapeDtypeStruct((KR, GF), BF16),
        ),
        in_specs=[pl.BlockSpec(memory_space=pltpu.SMEM)] + [hbm] * 5,
        out_specs=(vspec, vspec, vspec),
        scratch_shapes=scratch,
        compiler_params=pltpu.CompilerParams(
            collective_id=0, has_side_effects=True, vmem_limit_bytes=56 << 20),
    )(block_order, queries, output_grad, attention_out, cache_keys, cache_values)
    return pl.pallas_call(
        place,
        out_shape=tuple(jax.ShapeDtypeStruct(v.shape, v.dtype) for v in (dq, dk, dv)),
        in_specs=[vspec] * 3,
        out_specs=(vspec,) * 3,
    )(dq, dk, dv)


def solution(mesh):
    in_specs = (
        P(),
        P("section", "ctx", None),
        P("ctx", "section"),
        P("ctx", "section"),
        P("section", "ctx", None),
        P("section", "ctx", None),
    )
    out_specs = (P("section", "ctx", None), P("ctx", "section"), P("ctx", "section"))
    return jax.shard_map(local, mesh=mesh, in_specs=in_specs, out_specs=out_specs, check_vma=False)
```

```python
import jax
import jax.numpy as jnp
from jax import lax
from jax.experimental import pallas as pl
from jax.experimental.pallas import tpu as pltpu
from jax.sharding import PartitionSpec as P

MESH = pl.DeviceIdType.MESH
F32 = jnp.float32
BF16 = jnp.bfloat16

NS, NY, NX, NZ = 4, 4, 2, 8
HG, HD, GF = 5, 128, 640
KR = 128
KV = NY * KR
QR = 8
NB = NX * NY
ZR = NB * QR
QW = NZ * ZR
NT = NZ // 2
SCALE = HD ** -0.5
MASKED = -1e30
RT = 128
NR = QW // RT
PIECES = ((0, 2), (2, 3))
SROWS = (8, 16)


def nt(a, b):
    return lax.dot_general(a, b, (((1,), (1,)), ((), ())), preferred_element_type=F32)


def tn(a, b):
    return lax.dot_general(a, b, (((0,), (0,)), ((), ())), preferred_element_type=F32)


def nn(a, b):
    return lax.dot_general(a, b, (((1,), (0,)), ((), ())), preferred_element_type=F32)


def kernel(order, q_in, do_in, o_in, k_in, v_in, dq_out, dk_out, dv_out,
           qv, dov, ov, kin, vin, pk, p1, g, gd, kv, q3, do3, delc, pl_, pb, db, m3, lse3, c3, lx, lz, wt,
           dqa, zs, zr_, dkv, ks1, kr1, ks2, kr2, tb, p8,
           sin, s1, r1, sz, rz, szd, rzd, sy, ry, sf, rf, sl, rl, sx, rx, sg, rg, sk, rk, s8, r8):
    s = lax.axis_index("section")
    c = lax.axis_index("ctx")
    y = c >> 4
    xh = (c >> 3) & 1
    z = c & 7
    me = (s, c)
    own = s == y

    def dev(s_, y_, x_, z_):
        return (s_, (y_ << 4) | (x_ << 3) | z_)

    def rc(src, dst, ssem, rsem, to):
        return pltpu.make_async_remote_copy(
            src_ref=src, dst_ref=dst, send_sem=ssem, recv_sem=rsem,
            device_id=to, device_id_type=MESH)

    def arrived(dst, rsem):
        rc(dst, dst, rsem, rsem, me).wait_recv()

    def up(v, n, mod):
        return (v + n) & (mod - 1)

    def dn(v, n, mod):
        return (v - n) & (mod - 1)

    sends = []

    def go(cp):
        cp.start()
        sends.append(cp)

    def settle(count_):
        for cp in sends[:count_]:
            cp.wait_send()
        del sends[:count_]

    loads = []
    for i, (a, b) in enumerate(((q_in, qv), (do_in, dov), (o_in, ov), (k_in, kin), (v_in, vin))):
        cp = pltpu.make_async_copy(a, b, sin.at[i])
        cp.start()
        loads.append(cp)

    yr, yl, y2 = up(y, 1, NY), dn(y, 1, NY), up(y, 2, NY)
    bar = pltpu.get_barrier_semaphore()

    def greet(to):
        pl.semaphore_signal(bar, inc=1, device_id=to, device_id_type=MESH)

    count = 0
    for j in range(1, NZ):
        greet(dev(s, y, xh, up(z, j, NZ)))
        count += 1
    for t in (dev(s, yr, xh, z), dev(s, yl, xh, z), dev(s, y, up(xh, 1, NX), z)):
        greet(t)
        count += 1
    for i in range(4):
        for k in range(NX):
            if (i, k) != (0, 0):
                greet(dev(up(s, i, NS), s, up(xh, k, NX), z))
                greet(dev(y, up(y, i, NY), up(xh, k, NX), z))
                count += 2

    @pl.when(jnp.logical_not(own))
    def _():
        greet(dev(s, s, xh, z))
        greet(dev(y, y, xh, z))

    for cp in loads:
        cp.wait()

    lane = lax.broadcasted_iota(jnp.int32, (QR, 128), 1)
    for t in range(NS):
        cols = slice(t * GF, (t + 1) * GF)
        qf = qv[0, :, cols].astype(F32)
        df = dov[0, :, cols].astype(F32)
        prod = df * ov[0, :, cols].astype(F32)
        both = jnp.concatenate([qf, df], axis=0).astype(BF16)
        tile = jnp.zeros((QR, 128), F32)
        for h in range(HG):
            pk[t, h] = both[:, h * HD:(h + 1) * HD]
            d = jnp.sum(prod[:, h * HD:(h + 1) * HD], axis=1, keepdims=True)
            tile = jnp.where(lane == h, d, tile)
        hi = tile.astype(BF16).astype(F32)
        mid = (tile - hi).astype(BF16).astype(F32)
        lo = tile - hi - mid
        pk[t, HG] = jnp.concatenate([hi + pltpu.roll(lo, QR, 1), mid], axis=0).astype(BF16)

    pl.semaphore_wait(bar, count + 2 - 2 * own.astype(jnp.int32))

    mine = xh * NY + y
    for k in range(NX):
        for i in range(NS):
            t = up(s, i, NS)
            cp = rc(pk.at[t], p1.at[mine], s1.at[i, k], r1.at[k, y], dev(t, s, up(xh, k, NX), z))
            if (i, k) == (0, 0):
                self_in = cp

                @pl.when(jnp.logical_not(own))
                def _():
                    cp.start()
            else:
                go(cp)

    @pl.when(own)
    def _():
        p1[mine] = pk[s]

    dyr, dyl = dev(s, yr, xh, z), dev(s, yl, xh, z)

    def kv_send(i):
        ref = kv.at[y, pl.ds(*PIECES[i])]
        go(rc(ref, ref, sy.at[0, i], ry.at[0, i], dyr))
        go(rc(ref, ref, sy.at[1, i], ry.at[1, i], dyl))

    for h in range(HG):
        kv[y, h, 0] = kin[:, h * HD:(h + 1) * HD]
        kv[y, h, 1] = vin[:, h * HD:(h + 1) * HD]
        if h == PIECES[0][1] - 1:
            kv_send(0)

    def kv_forward(i):
        hs = pl.ds(*PIECES[i])
        arrived(kv.at[yl, hs], ry.at[0, i])
        go(rc(kv.at[yl, hs, 0], kv.at[yl, hs, 0], sf.at[0, i], rf.at[0, i], dyr))
        arrived(kv.at[yr, hs], ry.at[1, i])
        go(rc(kv.at[yr, hs, 1], kv.at[yr, hs, 1], sf.at[1, i], rf.at[1, i], dyl))

    def kv_ready(i):
        hs = pl.ds(*PIECES[i])
        arrived(kv.at[y2, hs, 0], rf.at[0, i])
        arrived(kv.at[y2, hs, 1], rf.at[1, i])

    kcol = lax.broadcasted_iota(jnp.int32, (1, KV), 1)
    kblk = kcol // KR
    base = jnp.zeros((1, KV), jnp.int32)
    for b in range(NY):
        base = jnp.where(kblk == b, order[(b * NX + xh) * NZ + z], base)
    kpos = base * KR + kcol % KR
    first = NY * NX * NZ * KR - QW
    zrow = lax.broadcasted_iota(jnp.int32, (ZR, 1), 0)
    zpos = first + (((zrow // QR) % NY) * NX + zrow // (NY * QR)) * NZ * QR + zrow % QR

    for k in range(NX):
        for b in range(NY):
            slot = dn(xh, k, NX) * NY + b
            if k == 0:
                @pl.when(jnp.logical_not(own & (y == b)))
                def _():
                    arrived(p1.at[slot], r1.at[k, b])
            else:
                arrived(p1.at[slot], r1.at[k, b])
    zr, zl = up(z, 1, NZ), dn(z, 1, NZ)
    dzr, dzl = dev(s, y, xh, zr), dev(s, y, xh, zl)
    dz2r, dz2l = dev(s, y, xh, up(z, 2, NZ)), dev(s, y, xh, dn(z, 2, NZ))
    half = NB // 2

    def zref(d, t, i, part):
        src = dn(z, t, NZ) if d == 0 else up(z, t, NZ)
        hs = pl.ds(*PIECES[i])
        return g.at[src, hs, pl.ds(d * half, half)] if part else g.at[src, hs]

    def zsend(d, t, i):
        last = t == NT
        ref = zref(d, 2 if last else t - 1, i, last)
        to = (dz2r if d == 0 else dz2l) if last else (dzr if d == 0 else dzl)
        go(rc(ref, ref, sz.at[d, t - 1, i], rz.at[d, t - 1, i], to))

    def zwait(d, t, i):
        arrived(zref(d, t, i, t == NT), rz.at[d, t - 1, i])

    def dsend(d, t):
        n = 2 if t == NT else t - 1
        ref = gd.at[dn(z, n, NZ) if d == 0 else up(z, n, NZ)]
        to = dz2r if t == NT else (dzr if d == 0 else dzl)
        go(rc(ref, ref, szd.at[d, t - 1], rzd.at[d, t - 1], to))

    def dwait(d, t):
        arrived(gd.at[dn(z, t, NZ) if d == 0 else up(z, t, NZ)], rzd.at[d, t - 1])

    def delta_rows(zc):
        tile = gd[zc]
        for b in range(NB):
            piece = tile if b == 0 else pltpu.roll(tile, 128 - b * QR, 1)
            delc[pl.ds(pl.multiple_of(zc * ZR + b * QR, QR), QR)] = piece

    def chunks(t):
        return (z, up(z, NT, NZ)) if t == NT else (dn(z, t, NZ), up(z, t, NZ))

    def rowsof(zc):
        return pl.ds(pl.multiple_of(zc * ZR, ZR), ZR)

    def pair(ref, h, t):
        a, b = chunks(t)
        return jnp.concatenate([ref[h, rowsof(a)], ref[h, rowsof(b)]], axis=0)

    def put(ref, h, t, v):
        a, b = chunks(t)
        ref[h, rowsof(a)] = v[:ZR]
        ref[h, rowsof(b)] = v[ZR:]

    def score_tile(h, t):
        qs_, ds_ = [], []
        for zc in chunks(t):
            blk = g[zc, h].astype(F32).reshape(NB, 2, QR, HD)
            qc = blk[:, 0].reshape(ZR, HD).astype(BF16)
            dc = blk[:, 1].reshape(ZR, HD).astype(BF16)
            q3[h, rowsof(zc)] = qc
            do3[h, rowsof(zc)] = dc
            qs_.append(qc)
            ds_.append(dc)
        kh = kv[:, h, 0].reshape(KV, HD)
        sc = nt(jnp.concatenate(qs_, axis=0), kh) * SCALE
        a, b = chunks(t)
        qpos = jnp.concatenate([zpos + a * QR, zpos + b * QR], axis=0)
        sc = jnp.where(kpos <= qpos, sc, MASKED)
        m = jnp.max(sc, axis=1, keepdims=True)
        p = jnp.exp(sc - m)
        l = jnp.sum(p, axis=1, keepdims=True)
        put(pb, h, t, p.astype(BF16))
        put(m3, h, t, jnp.broadcast_to(m, (RT, 128)))
        put(lse3, h, t, jnp.broadcast_to(m + jnp.log(l), (RT, 128)))
        if t == NT:
            pl_[h] = p
        else:
            dprob(h, t, p, jnp.concatenate(ds_, axis=0))

    def dprob(h, t, p, dom):
        vh = kv[:, h, 1].reshape(KV, HD)
        a, b = chunks(t)
        dl = jnp.concatenate([delc[rowsof(a)], delc[rowsof(b)]], axis=0)[:, h:h + 1]
        put(db, h, t, (p * (nt(dom, vh) - dl) * SCALE).astype(BF16))

    def dprob_late(h):
        dprob(h, NT, pl_[h], pair(do3, h, NT))
        kh = kv[:, h, 0].reshape(KV, HD)
        dqa[h] = nn(db[h], kh).reshape(NZ, ZR, HD)

    lane2 = lax.broadcasted_iota(jnp.int32, (RT, 128), 1)

    def columns(rows_):
        pad = jnp.zeros((128 - rows_.shape[0], 128), F32)
        return jnp.concatenate([rows_, pad], axis=0).T

    def heads_of(i):
        return range(PIECES[i][0], PIECES[i][0] + PIECES[i][1])

    def stats_send(i):
        st = jnp.zeros((RT, 128), F32)
        for j, h in enumerate(heads_of(i)):
            for rt in range(NR):
                st = jnp.where(lane2 == j * NR + rt, lse3[h, rt * RT:(rt + 1) * RT], st)
        sr = pl.ds(0, SROWS[i])
        lx[i, 0, sr] = st.T[:SROWS[i]]
        go(rc(lx.at[i, 0, sr], lx.at[i, 1, sr], sx.at[i], rx.at[i], dev(s, y, up(xh, 1, NX), z)))

    def stats_pair(i):
        sr = pl.ds(0, SROWS[i])
        arrived(lx.at[i, 1, sr], rx.at[i])
        a, b = lx[i, 0, sr], lx[i, 1, sr]
        mx = jnp.maximum(a, b)
        both = mx + jnp.log(jnp.exp(a - mx) + jnp.exp(b - mx))
        lz[i, z, sr] = both
        for j in range(1, NZ):
            ref = lz.at[i, z, sr]
            go(rc(ref, ref, sl.at[i, j], rl.at[i, j], dev(s, y, xh, up(z, j, NZ))))
        tt = columns(both)
        for j, h in enumerate(heads_of(i)):
            for rt in range(NR):
                k = j * NR + rt
                lse3[h, rt * RT:(rt + 1) * RT] = jnp.broadcast_to(tt[:, k:k + 1], (RT, 128))

    def stats_wait(i):
        sr = pl.ds(0, SROWS[i])
        for j in range(1, NZ):
            arrived(lz.at[i, dn(z, j, NZ), sr], rl.at[i, j])
        mx = lz[i, 0, sr]
        for f in range(1, NZ):
            mx = jnp.maximum(mx, lz[i, f, sr])
        tot = jnp.exp(lz[i, 0, sr] - mx)
        for f in range(1, NZ):
            tot = tot + jnp.exp(lz[i, f, sr] - mx)
        lt = mx + jnp.log(tot)
        tt = columns(lt)
        for j, h in enumerate(heads_of(i)):
            for rt in range(NR):
                rows = slice(rt * RT, (rt + 1) * RT)
                k = j * NR + rt
                col = jnp.broadcast_to(tt[:, k:k + 1], (RT, 128))
                c3[h, rows] = jnp.exp(m3[h, rows] - col)
        return lt

    def weights(i, lt):
        sr = pl.ds(0, SROWS[i])
        for k, n in enumerate((-2, -1, 0, 1, 2)):
            wt[i, k] = columns(jnp.exp(lz[i, up(z, n, NZ), sr] - lt))

    lane3 = lax.broadcasted_iota(jnp.int32, (ZR, 128), 1)

    def weight(n, zc, h):
        i = 0 if h < PIECES[1][0] else 1
        v = wt[i, n + 2, pl.ds(pl.multiple_of((zc & 1) * ZR, ZR), ZR)]
        v = jnp.where(lane3 == (h - PIECES[i][0]) * NR + (zc >> 1), v, 0.0)
        return jnp.sum(v, axis=1, keepdims=True)

    for h in range(HG):
        for b in range(NB):
            g[z, h, b] = p1[b, h]
    tile = jnp.zeros((QR, 128), F32)
    for b in range(NB):
        d2 = p1[b, HG].astype(F32)
        top = d2[:QR]
        d1 = jnp.where(lane < QR, top + d2[QR:] + pltpu.roll(top, 128 - QR, 1), 0.0)
        tile = tile + (d1 if b == 0 else pltpu.roll(d1, b * QR, 1))
    gd[z] = tile

    for i in range(2):
        zsend(0, 1, i)
        zsend(1, 1, i)
        if i == 0:
            dsend(0, 1)
            dsend(1, 1)
    kv_send(1)
    kv_forward(0)
    def score_piece(t, i):
        if t == 1:
            kv_ready(i)
        if i == 0:
            for zc in chunks(t):
                delta_rows(zc)
        for h in heads_of(i):
            score_tile(h, t)

    pending = []
    for t in range(2, NT + 2):
        for i in range(2):
            for d in range(2):
                zwait(d, t - 1, i)
                for n_ in (t, t + 1):
                    if n_ == t < NT or n_ == NT == t + 1:
                        zsend(d, n_, i)
            if i == 0:
                dwait(0, t - 1)
                if t <= NT:
                    dwait(1, t - 1)
                if t < NT:
                    dsend(0, t)
                    dsend(1, t)
                if t == NT - 1:
                    dsend(0, NT)
                if t == 2:
                    kv_forward(1)
            pending.append((t - 1, i))
            while len(pending) > (2 if (t, i) < (NT - 1, 1) else 0):
                score_piece(*pending.pop(0))
            if t == NT + 1:
                if i == 0:
                    ring_sends = len(sends)
                stats_send(i)

    HR = ZR // 2

    def zmsg(d, kind, i):
        hs = pl.ds(*PIECES[i])
        a_, b_ = zs.at[d, kind, hs], zr_.at[d, kind, hs]
        if kind == 0:
            part = pl.ds(d * HR, HR)
            a_, b_ = zs.at[d, kind, hs, part], zr_.at[d, kind, hs, part]
        near, far = (dzr, dz2r) if d == 0 else (dzl, dz2l)
        return rc(a_, b_, sg.at[d, kind, i], rg.at[d, kind, i], far if kind in (0, 3) else near)

    def step(d, n):
        return up(z, n, NZ) if d == 0 else dn(z, n, NZ)

    def query_scale(i):
        for h in heads_of(i):
            dqa[h] = dqa[h] * jnp.exp(m3[h] - lse3[h]).reshape(NZ, ZR, HD)

    def query_send(i, kind, n):
        for d in range(2):
            for h in heads_of(i):
                if kind == 0:
                    part = slice(d * HR, (d + 1) * HR)
                    zs[d, kind, h, part] = dqa[h, step(d, n), part].astype(BF16)
                else:
                    zs[d, kind, h] = dqa[h, step(d, n)].astype(BF16)
            go(zmsg(d, kind, i))

    def query_relay(i):
        for d in range(2):
            sign = 1 - 2 * d
            zmsg(d, 0, i).wait_recv()
            zmsg(d, 1, i).wait_recv()
            part = slice(d * HR, (d + 1) * HR)
            rest = slice((1 - d) * HR, (2 - d) * HR)
            to = step(d, 2)
            for h in heads_of(i):
                acc = dqa[h, to] * weight(0, to, h) + zr_[d, 1, h].astype(F32) * weight(-sign, to, h)
                far = zr_[d, 0, h, part].astype(F32) * weight(-2 * sign, to, h)[part]
                zs[d, 3, h, rest] = acc[rest].astype(BF16)
                zs[d, 3, h, part] = (acc[part] + far).astype(BF16)
            go(zmsg(d, 3, i))

    def query_sum(i):
        for d in range(2):
            zmsg(d, 2, i).wait_recv()
            zmsg(d, 3, i).wait_recv()
        for h in heads_of(i):
            acc = dqa[h, z] * weight(0, z, h)
            for d in range(2):
                acc = acc + zr_[d, 3, h].astype(F32)
                acc = acc + zr_[d, 2, h].astype(F32) * weight(2 * d - 1, z, h)
            tb[:, h] = acc.reshape(NB, QR, HD)

    def cache_grads(h):
        cc = c3[h]
        dkt = tn((q3[h].astype(F32) * cc).astype(BF16), db[h])
        dvt = tn((do3[h].astype(F32) * cc).astype(BF16), pb[h])
        for b in range(NY):
            dkv[h, b, 0] = dkt[:, b * KR:(b + 1) * KR].T
            dkv[h, b, 1] = dvt[:, b * KR:(b + 1) * KR].T
        ks1[h, 0, 0] = dkv[h, y2, 0].astype(BF16)
        ks1[h, 0, 1] = dkv[h, yr, 1].astype(BF16)
        ks1[h, 1, 0] = dkv[h, y2, 1].astype(BF16)
        ks1[h, 1, 1] = dkv[h, yl, 0].astype(BF16)
        go(leg(h, 0, 0, dyr))
        go(leg(h, 1, 0, dyl))

    def leg(h, d, i, to):
        return rc(ks1.at[h, d, i], kr1.at[h, d, i], sk.at[i, d, h], rk.at[i, d, h], to)

    def near_blocks(h):
        go(leg(h, 0, 1, dyr))
        go(leg(h, 1, 1, dyl))

    def second_leg(h):
        arrived(kr1.at[h, 0, 0], rk.at[0, 0, h])
        ks2[h, 0] = (dkv[h, yr, 0] + kr1[h, 0, 0].astype(F32)).astype(BF16)
        go(rc(ks2.at[h, 0], kr2.at[h, 0], sk.at[2, 0, h], rk.at[2, 0, h], dyr))
        arrived(kr1.at[h, 1, 0], rk.at[0, 1, h])
        ks2[h, 1] = (dkv[h, yl, 1] + kr1[h, 1, 0].astype(F32)).astype(BF16)
        go(rc(ks2.at[h, 1], kr2.at[h, 1], sk.at[2, 1, h], rk.at[2, 1, h], dyl))

    def cache_out(h):
        arrived(kr1.at[h, 0, 1], rk.at[1, 0, h])
        arrived(kr1.at[h, 1, 1], rk.at[1, 1, h])
        arrived(kr2.at[h, 0], rk.at[2, 0, h])
        arrived(kr2.at[h, 1], rk.at[2, 1, h])
        cols = slice(h * HD, (h + 1) * HD)
        dk_out[:, cols] = (dkv[h, y, 0] + kr1[h, 1, 1].astype(F32) + kr2[h, 0].astype(F32)).astype(BF16)
        dv_out[:, cols] = (dkv[h, y, 1] + kr1[h, 0, 1].astype(F32) + kr2[h, 1].astype(F32)).astype(BF16)

    dprob_late(0)
    settle(ring_sends)
    stats_pair(0)
    for h in heads_of(0):
        if h > 0:
            dprob_late(h)
    query_scale(0)
    query_send(0, 1, 3)
    query_send(0, 0, 4)
    stats_pair(1)
    for h in heads_of(1):
        dprob_late(h)
    query_scale(1)
    query_send(1, 1, 3)
    query_send(1, 0, 4)
    early = len(sends)
    query_send(0, 2, 1)
    query_send(1, 2, 1)
    total = stats_wait(0)
    cache_grads(0)
    weights(0, total)
    query_relay(0)
    near_blocks(0)
    cache_grads(1)
    near_blocks(1)
    total = stats_wait(1)
    cache_grads(2)
    weights(1, total)
    query_relay(1)
    near_blocks(2)
    cache_grads(3)
    cache_grads(4)
    near_blocks(3)
    near_blocks(4)
    settle(early)
    second_leg(0)
    query_sum(0)
    second_leg(1)
    second_leg(2)
    query_sum(1)

    for j in range(NY):
        for k in range(NX):
            ty, tx = up(y, j, NY), up(xh, k, NX)
            cp = rc(tb.at[tx * NY + ty], p8.at[k, s], s8.at[j, k], r8.at[k, s], dev(y, ty, tx, z))
            if (j, k) == (0, 0):
                self_out = cp

                @pl.when(jnp.logical_not(own))
                def _():
                    cp.start()
            else:
                go(cp)

    @pl.when(own)
    def _():
        p8[0, s] = tb[mine]

    second_leg(3)
    second_leg(4)
    for h in range(HG):
        cache_out(h)

    for k in range(NX):
        for b in range(NS):
            if k == 0:
                @pl.when(jnp.logical_not(own & (s == b)))
                def _():
                    arrived(p8.at[k, b], r8.at[k, b])
            else:
                arrived(p8.at[k, b], r8.at[k, b])
    for b in range(NS):
        for h in range(HG):
            col = b * GF + h * HD
            dq_out[0, :, col:col + HD] = (p8[0, b, h] + p8[1, b, h]).astype(BF16)

    @pl.when(jnp.logical_not(own))
    def _():
        self_in.wait_send()
        self_out.wait_send()

    for cp in sends:
        cp.wait_send()


def place(a, b, c, x, y, z):
    x[...] = a[...]
    y[...] = b[...]
    z[...] = c[...]


def local(block_order, queries, cache_keys, cache_values, attention_out, output_grad):
    dma = pltpu.SemaphoreType.DMA
    vm = pltpu.VMEM
    row = queries.shape
    scratch = [
        vm(row, BF16), vm(row, BF16), vm(row, BF16), vm((KR, GF), BF16), vm((KR, GF), BF16),
        vm((NS, HG + 1, 16, HD), BF16), vm((NB, HG + 1, 16, HD), BF16),
        vm((NZ, HG, NB, 16, HD), BF16), vm((NZ, QR, 128), F32),
        vm((NY, HG, 2, KR, HD), BF16), vm((HG, QW, HD), BF16), vm((HG, QW, HD), BF16), vm((QW, 128), F32),
        vm((HG, RT, KV), F32), vm((HG, QW, KV), BF16), vm((HG, QW, KV), BF16),
        vm((HG, QW, 128), F32), vm((HG, QW, 128), F32), vm((HG, QW, 128), F32),
        vm((2, 2, 16, 128), F32), vm((2, NZ, 16, 128), F32), vm((2, 5, 128, 128), F32),
        vm((HG, NZ, ZR, HD), F32), vm((2, 4, HG, ZR, HD), BF16), vm((2, 4, HG, ZR, HD), BF16),
        vm((HG, NY, 2, KR, HD), F32),
        vm((HG, 2, 2, KR, HD), BF16), vm((HG, 2, 2, KR, HD), BF16),
        vm((HG, 2, KR, HD), BF16), vm((HG, 2, KR, HD), BF16),
        vm((NB, HG, QR, HD), F32), vm((NX, NS, HG, QR, HD), F32),
        dma((5,)), dma((NS, NX)), dma((NX, NY)),
        dma((2, NT, 2)), dma((2, NT, 2)), dma((2, NT)), dma((2, NT)),
        dma((2, 2)), dma((2, 2)), dma((2, 2)), dma((2, 2)),
        dma((2, NZ)), dma((2, NZ)), dma((2,)), dma((2,)), dma((2, 4, 2)), dma((2, 4, 2)),
        dma((3, 2, HG)), dma((3, 2, HG)), dma((NY, NX)), dma((NX, NS)),
    ]
    vspec = pl.BlockSpec(memory_space=pltpu.VMEM)
    hbm = pl.BlockSpec(memory_space=pl.ANY)
    dq, dk, dv = pl.pallas_call(
        kernel,
        out_shape=(
            jax.ShapeDtypeStruct((1, QR, NS * GF), BF16),
            jax.ShapeDtypeStruct((KR, GF), BF16),
            jax.ShapeDtypeStruct((KR, GF), BF16),
        ),
        in_specs=[pl.BlockSpec(memory_space=pltpu.SMEM)] + [hbm] * 5,
        out_specs=(vspec, vspec, vspec),
        scratch_shapes=scratch,
        compiler_params=pltpu.CompilerParams(
            collective_id=0, has_side_effects=True, vmem_limit_bytes=56 << 20),
    )(block_order, queries, output_grad, attention_out, cache_keys, cache_values)
    return pl.pallas_call(
        place,
        out_shape=tuple(jax.ShapeDtypeStruct(v.shape, v.dtype) for v in (dq, dk, dv)),
        in_specs=[vspec] * 3,
        out_specs=(vspec,) * 3,
    )(dq, dk, dv)


def solution(mesh):
    in_specs = (
        P(),
        P("section", "ctx", None),
        P("ctx", "section"),
        P("ctx", "section"),
        P("section", "ctx", None),
        P("section", "ctx", None),
    )
    out_specs = (P("section", "ctx", None), P("ctx", "section"), P("ctx", "section"))
    return jax.shard_map(local, mesh=mesh, in_specs=in_specs, out_specs=out_specs, check_vma=False)
```

```python
import jax
import jax.numpy as jnp
from jax import lax
from jax.experimental import pallas as pl
from jax.experimental.pallas import tpu as pltpu
from jax.sharding import PartitionSpec as P

MESH = pl.DeviceIdType.MESH
F32 = jnp.float32
BF16 = jnp.bfloat16

NS, NY, NX, NZ = 4, 4, 2, 8
HG, HD, GF = 5, 128, 640
KR = 128
KV = NY * KR
QR = 8
NB = NX * NY
ZR = NB * QR
QW = NZ * ZR
NT = NZ // 2
SCALE = HD ** -0.5
MASKED = -1e30
RT = 128
NR = QW // RT
PIECES = ((0, 2), (2, 3))
SROWS = (8, 16)


def nt(a, b):
    return lax.dot_general(a, b, (((1,), (1,)), ((), ())), preferred_element_type=F32)


def tn(a, b):
    return lax.dot_general(a, b, (((0,), (0,)), ((), ())), preferred_element_type=F32)


def nn(a, b):
    return lax.dot_general(a, b, (((1,), (0,)), ((), ())), preferred_element_type=F32)


def kernel(order, q_in, do_in, o_in, k_in, v_in, dq_out, dk_out, dv_out,
           qv, dov, ov, kin, vin, pk, p1, g, gd, kv, q3, do3, delc, pl_, pb, db, m3, lse3, c3, lx, lz, wt,
           dqa, zs, zr_, dkv, ks1, kr1, ks2, kr2, tb, p8,
           sin, s1, r1, sz, rz, szd, rzd, sy, ry, sf, rf, sl, rl, sx, rx, sg, rg, sk, rk, s8, r8):
    s = lax.axis_index("section")
    c = lax.axis_index("ctx")
    y = c >> 4
    xh = (c >> 3) & 1
    z = c & 7
    me = (s, c)
    own = s == y

    def dev(s_, y_, x_, z_):
        return (s_, (y_ << 4) | (x_ << 3) | z_)

    def rc(src, dst, ssem, rsem, to):
        return pltpu.make_async_remote_copy(
            src_ref=src, dst_ref=dst, send_sem=ssem, recv_sem=rsem,
            device_id=to, device_id_type=MESH)

    def arrived(dst, rsem):
        rc(dst, dst, rsem, rsem, me).wait_recv()

    def up(v, n, mod):
        return (v + n) & (mod - 1)

    def dn(v, n, mod):
        return (v - n) & (mod - 1)

    sends = []

    def go(cp):
        cp.start()
        sends.append(cp)

    def settle(count_):
        for cp in sends[:count_]:
            cp.wait_send()
        del sends[:count_]

    loads = []
    for i, (a, b) in enumerate(((q_in, qv), (do_in, dov), (o_in, ov), (k_in, kin), (v_in, vin))):
        cp = pltpu.make_async_copy(a, b, sin.at[i])
        cp.start()
        loads.append(cp)

    yr, yl, y2 = up(y, 1, NY), dn(y, 1, NY), up(y, 2, NY)
    bar = pltpu.get_barrier_semaphore()

    def greet(to):
        pl.semaphore_signal(bar, inc=1, device_id=to, device_id_type=MESH)

    count = 0
    for j in range(1, NZ):
        greet(dev(s, y, xh, up(z, j, NZ)))
        count += 1
    for t in (dev(s, yr, xh, z), dev(s, yl, xh, z), dev(s, y, up(xh, 1, NX), z)):
        greet(t)
        count += 1
    for i in range(4):
        for k in range(NX):
            if (i, k) != (0, 0):
                greet(dev(up(s, i, NS), s, up(xh, k, NX), z))
                greet(dev(y, up(y, i, NY), up(xh, k, NX), z))
                count += 2

    @pl.when(jnp.logical_not(own))
    def _():
        greet(dev(s, s, xh, z))
        greet(dev(y, y, xh, z))

    for cp in loads:
        cp.wait()

    lane = lax.broadcasted_iota(jnp.int32, (QR, 128), 1)
    for t in range(NS):
        cols = slice(t * GF, (t + 1) * GF)
        qf = qv[0, :, cols].astype(F32)
        df = dov[0, :, cols].astype(F32)
        prod = df * ov[0, :, cols].astype(F32)
        both = jnp.concatenate([qf, df], axis=0).astype(BF16)
        tile = jnp.zeros((QR, 128), F32)
        for h in range(HG):
            pk[t, h] = both[:, h * HD:(h + 1) * HD]
            d = jnp.sum(prod[:, h * HD:(h + 1) * HD], axis=1, keepdims=True)
            tile = jnp.where(lane == h, d, tile)
        hi = tile.astype(BF16).astype(F32)
        mid = (tile - hi).astype(BF16).astype(F32)
        lo = tile - hi - mid
        pk[t, HG] = jnp.concatenate([hi + pltpu.roll(lo, QR, 1), mid], axis=0).astype(BF16)

    pl.semaphore_wait(bar, count + 2 - 2 * own.astype(jnp.int32))

    mine = xh * NY + y
    for k in range(NX):
        for i in range(NS):
            t = up(s, i, NS)
            cp = rc(pk.at[t], p1.at[mine], s1.at[i, k], r1.at[k, y], dev(t, s, up(xh, k, NX), z))
            if (i, k) == (0, 0):
                self_in = cp

                @pl.when(jnp.logical_not(own))
                def _():
                    cp.start()
            else:
                go(cp)

    @pl.when(own)
    def _():
        p1[mine] = pk[s]

    dyr, dyl = dev(s, yr, xh, z), dev(s, yl, xh, z)

    def kv_send(i):
        ref = kv.at[y, pl.ds(*PIECES[i])]
        go(rc(ref, ref, sy.at[0, i], ry.at[0, i], dyr))
        go(rc(ref, ref, sy.at[1, i], ry.at[1, i], dyl))

    for h in range(HG):
        kv[y, h, 0] = kin[:, h * HD:(h + 1) * HD]
        kv[y, h, 1] = vin[:, h * HD:(h + 1) * HD]
        if h == PIECES[0][1] - 1:
            kv_send(0)

    def kv_forward(i):
        hs = pl.ds(*PIECES[i])
        arrived(kv.at[yl, hs], ry.at[0, i])
        go(rc(kv.at[yl, hs, 0], kv.at[yl, hs, 0], sf.at[0, i], rf.at[0, i], dyr))
        arrived(kv.at[yr, hs], ry.at[1, i])
        go(rc(kv.at[yr, hs, 1], kv.at[yr, hs, 1], sf.at[1, i], rf.at[1, i], dyl))

    def kv_ready(i):
        hs = pl.ds(*PIECES[i])
        arrived(kv.at[y2, hs, 0], rf.at[0, i])
        arrived(kv.at[y2, hs, 1], rf.at[1, i])

    kcol = lax.broadcasted_iota(jnp.int32, (1, KV), 1)
    kblk = kcol // KR
    base = jnp.zeros((1, KV), jnp.int32)
    for b in range(NY):
        base = jnp.where(kblk == b, order[(b * NX + xh) * NZ + z], base)
    kpos = base * KR + kcol % KR
    first = NY * NX * NZ * KR - QW
    zrow = lax.broadcasted_iota(jnp.int32, (ZR, 1), 0)
    zpos = first + (((zrow // QR) % NY) * NX + zrow // (NY * QR)) * NZ * QR + zrow % QR

    for k in range(NX):
        for b in range(NY):
            slot = dn(xh, k, NX) * NY + b
            if k == 0:
                @pl.when(jnp.logical_not(own & (y == b)))
                def _():
                    arrived(p1.at[slot], r1.at[k, b])
            else:
                arrived(p1.at[slot], r1.at[k, b])
    zr, zl = up(z, 1, NZ), dn(z, 1, NZ)
    dzr, dzl = dev(s, y, xh, zr), dev(s, y, xh, zl)
    dz2r, dz2l = dev(s, y, xh, up(z, 2, NZ)), dev(s, y, xh, dn(z, 2, NZ))
    half = NB // 2

    def zref(d, t, i, part):
        src = dn(z, t, NZ) if d == 0 else up(z, t, NZ)
        hs = pl.ds(*PIECES[i])
        return g.at[src, hs, pl.ds(d * half, half)] if part else g.at[src, hs]

    def zsend(d, t, i):
        last = t == NT
        ref = zref(d, 2 if last else t - 1, i, last)
        to = (dz2r if d == 0 else dz2l) if last else (dzr if d == 0 else dzl)
        go(rc(ref, ref, sz.at[d, t - 1, i], rz.at[d, t - 1, i], to))

    def zwait(d, t, i):
        arrived(zref(d, t, i, t == NT), rz.at[d, t - 1, i])

    def dsend(d, t):
        n = 2 if t == NT else t - 1
        ref = gd.at[dn(z, n, NZ) if d == 0 else up(z, n, NZ)]
        to = dz2r if t == NT else (dzr if d == 0 else dzl)
        go(rc(ref, ref, szd.at[d, t - 1], rzd.at[d, t - 1], to))

    def dwait(d, t):
        arrived(gd.at[dn(z, t, NZ) if d == 0 else up(z, t, NZ)], rzd.at[d, t - 1])

    def delta_rows(zc):
        tile = gd[zc]
        for b in range(NB):
            piece = tile if b == 0 else pltpu.roll(tile, 128 - b * QR, 1)
            delc[pl.ds(pl.multiple_of(zc * ZR + b * QR, QR), QR)] = piece

    def chunks(t):
        return (z, up(z, NT, NZ)) if t == NT else (dn(z, t, NZ), up(z, t, NZ))

    def rowsof(zc):
        return pl.ds(pl.multiple_of(zc * ZR, ZR), ZR)

    def pair(ref, h, t):
        a, b = chunks(t)
        return jnp.concatenate([ref[h, rowsof(a)], ref[h, rowsof(b)]], axis=0)

    def put(ref, h, t, v):
        a, b = chunks(t)
        ref[h, rowsof(a)] = v[:ZR]
        ref[h, rowsof(b)] = v[ZR:]

    def score_tile(h, t):
        qs_, ds_ = [], []
        for zc in chunks(t):
            blk = g[zc, h].astype(F32).reshape(NB, 2, QR, HD)
            qc = blk[:, 0].reshape(ZR, HD).astype(BF16)
            dc = blk[:, 1].reshape(ZR, HD).astype(BF16)
            q3[h, rowsof(zc)] = qc
            do3[h, rowsof(zc)] = dc
            qs_.append(qc)
            ds_.append(dc)
        kh = kv[:, h, 0].reshape(KV, HD)
        sc = nt(jnp.concatenate(qs_, axis=0), kh) * SCALE
        a, b = chunks(t)
        qpos = jnp.concatenate([zpos + a * QR, zpos + b * QR], axis=0)
        sc = jnp.where(kpos <= qpos, sc, MASKED)
        m = jnp.max(sc, axis=1, keepdims=True)
        p = jnp.exp(sc - m)
        l = jnp.sum(p, axis=1, keepdims=True)
        put(pb, h, t, p.astype(BF16))
        put(m3, h, t, jnp.broadcast_to(m, (RT, 128)))
        put(lse3, h, t, jnp.broadcast_to(m + jnp.log(l), (RT, 128)))
        if t == NT:
            pl_[h] = p
        else:
            dprob(h, t, p, jnp.concatenate(ds_, axis=0))

    def dprob(h, t, p, dom):
        vh = kv[:, h, 1].reshape(KV, HD)
        a, b = chunks(t)
        dl = jnp.concatenate([delc[rowsof(a)], delc[rowsof(b)]], axis=0)[:, h:h + 1]
        put(db, h, t, (p * (nt(dom, vh) - dl) * SCALE).astype(BF16))

    def dprob_late(h):
        dprob(h, NT, pl_[h], pair(do3, h, NT))
        kh = kv[:, h, 0].reshape(KV, HD)
        dqa[h] = nn(db[h], kh).reshape(NZ, ZR, HD)

    lane2 = lax.broadcasted_iota(jnp.int32, (RT, 128), 1)

    def columns(rows_):
        pad = jnp.zeros((128 - rows_.shape[0], 128), F32)
        return jnp.concatenate([rows_, pad], axis=0).T

    def heads_of(i):
        return range(PIECES[i][0], PIECES[i][0] + PIECES[i][1])

    def stats_send(i):
        st = jnp.zeros((RT, 128), F32)
        for j, h in enumerate(heads_of(i)):
            for rt in range(NR):
                st = jnp.where(lane2 == j * NR + rt, lse3[h, rt * RT:(rt + 1) * RT], st)
        sr = pl.ds(0, SROWS[i])
        lx[i, 0, sr] = st.T[:SROWS[i]]
        go(rc(lx.at[i, 0, sr], lx.at[i, 1, sr], sx.at[i], rx.at[i], dev(s, y, up(xh, 1, NX), z)))

    def stats_pair(i):
        sr = pl.ds(0, SROWS[i])
        arrived(lx.at[i, 1, sr], rx.at[i])
        a, b = lx[i, 0, sr], lx[i, 1, sr]
        mx = jnp.maximum(a, b)
        both = mx + jnp.log(jnp.exp(a - mx) + jnp.exp(b - mx))
        lz[i, z, sr] = both
        for j in range(1, NZ):
            ref = lz.at[i, z, sr]
            go(rc(ref, ref, sl.at[i, j], rl.at[i, j], dev(s, y, xh, up(z, j, NZ))))
        tt = columns(both)
        for j, h in enumerate(heads_of(i)):
            for rt in range(NR):
                k = j * NR + rt
                lse3[h, rt * RT:(rt + 1) * RT] = jnp.broadcast_to(tt[:, k:k + 1], (RT, 128))

    def stats_wait(i):
        sr = pl.ds(0, SROWS[i])
        for j in range(1, NZ):
            arrived(lz.at[i, dn(z, j, NZ), sr], rl.at[i, j])
        mx = lz[i, 0, sr]
        for f in range(1, NZ):
            mx = jnp.maximum(mx, lz[i, f, sr])
        tot = jnp.exp(lz[i, 0, sr] - mx)
        for f in range(1, NZ):
            tot = tot + jnp.exp(lz[i, f, sr] - mx)
        lt = mx + jnp.log(tot)
        tt = columns(lt)
        for j, h in enumerate(heads_of(i)):
            for rt in range(NR):
                rows = slice(rt * RT, (rt + 1) * RT)
                k = j * NR + rt
                col = jnp.broadcast_to(tt[:, k:k + 1], (RT, 128))
                c3[h, rows] = jnp.exp(m3[h, rows] - col)
        return lt

    def weights(i, lt):
        sr = pl.ds(0, SROWS[i])
        for k, n in enumerate((-2, -1, 0, 1, 2)):
            wt[i, k] = columns(jnp.exp(lz[i, up(z, n, NZ), sr] - lt))

    lane3 = lax.broadcasted_iota(jnp.int32, (ZR, 128), 1)

    def weight(n, zc, h):
        i = 0 if h < PIECES[1][0] else 1
        v = wt[i, n + 2, pl.ds(pl.multiple_of((zc & 1) * ZR, ZR), ZR)]
        v = jnp.where(lane3 == (h - PIECES[i][0]) * NR + (zc >> 1), v, 0.0)
        return jnp.sum(v, axis=1, keepdims=True)

    for h in range(HG):
        for b in range(NB):
            g[z, h, b] = p1[b, h]
    tile = jnp.zeros((QR, 128), F32)
    for b in range(NB):
        d2 = p1[b, HG].astype(F32)
        top = d2[:QR]
        d1 = jnp.where(lane < QR, top + d2[QR:] + pltpu.roll(top, 128 - QR, 1), 0.0)
        tile = tile + (d1 if b == 0 else pltpu.roll(d1, b * QR, 1))
    gd[z] = tile

    for i in range(2):
        zsend(0, 1, i)
        zsend(1, 1, i)
        if i == 0:
            dsend(0, 1)
            dsend(1, 1)
    kv_send(1)
    kv_forward(0)
    def score_piece(t, i):
        if t == 1:
            kv_ready(i)
        if i == 0:
            for zc in chunks(t):
                delta_rows(zc)
        for h in heads_of(i):
            score_tile(h, t)

    pending = []
    for t in range(2, NT + 2):
        for i in range(2):
            for d in range(2):
                zwait(d, t - 1, i)
                for n_ in (t, t + 1):
                    if n_ == t < NT or n_ == NT == t + 1:
                        zsend(d, n_, i)
            if i == 0:
                dwait(0, t - 1)
                if t <= NT:
                    dwait(1, t - 1)
                if t < NT:
                    dsend(0, t)
                    dsend(1, t)
                if t == NT - 1:
                    dsend(0, NT)
                if t == 2:
                    kv_forward(1)
            pending.append((t - 1, i))
            while len(pending) > (2 if (t, i) < (NT - 1, 1) else 0):
                score_piece(*pending.pop(0))
            if t == NT + 1:
                if i == 0:
                    ring_sends = len(sends)
                stats_send(i)

    HR = ZR // 2

    def zmsg(d, kind, i):
        hs = pl.ds(*PIECES[i])
        a_, b_ = zs.at[d, kind, hs], zr_.at[d, kind, hs]
        if kind == 0:
            part = pl.ds(d * HR, HR)
            a_, b_ = zs.at[d, kind, hs, part], zr_.at[d, kind, hs, part]
        near, far = (dzr, dz2r) if d == 0 else (dzl, dz2l)
        return rc(a_, b_, sg.at[d, kind, i], rg.at[d, kind, i], far if kind in (0, 3) else near)

    def step(d, n):
        return up(z, n, NZ) if d == 0 else dn(z, n, NZ)

    def query_scale(i):
        for h in heads_of(i):
            dqa[h] = dqa[h] * jnp.exp(m3[h] - lse3[h]).reshape(NZ, ZR, HD)

    def query_send(i, kind, n):
        for d in range(2):
            for h in heads_of(i):
                if kind == 0:
                    part = slice(d * HR, (d + 1) * HR)
                    zs[d, kind, h, part] = dqa[h, step(d, n), part].astype(BF16)
                else:
                    zs[d, kind, h] = dqa[h, step(d, n)].astype(BF16)
            go(zmsg(d, kind, i))

    def query_relay(i):
        for d in range(2):
            sign = 1 - 2 * d
            zmsg(d, 0, i).wait_recv()
            zmsg(d, 1, i).wait_recv()
            part = slice(d * HR, (d + 1) * HR)
            rest = slice((1 - d) * HR, (2 - d) * HR)
            to = step(d, 2)
            for h in heads_of(i):
                acc = dqa[h, to] * weight(0, to, h) + zr_[d, 1, h].astype(F32) * weight(-sign, to, h)
                far = zr_[d, 0, h, part].astype(F32) * weight(-2 * sign, to, h)[part]
                zs[d, 3, h, rest] = acc[rest].astype(BF16)
                zs[d, 3, h, part] = (acc[part] + far).astype(BF16)
            go(zmsg(d, 3, i))

    def query_sum(i):
        for d in range(2):
            zmsg(d, 2, i).wait_recv()
            zmsg(d, 3, i).wait_recv()
        for h in heads_of(i):
            acc = dqa[h, z] * weight(0, z, h)
            for d in range(2):
                acc = acc + zr_[d, 3, h].astype(F32)
                acc = acc + zr_[d, 2, h].astype(F32) * weight(2 * d - 1, z, h)
            tb[:, h] = acc.reshape(NB, QR, HD)

    def cache_grads(h):
        cc = c3[h]
        dkt = tn((q3[h].astype(F32) * cc).astype(BF16), db[h])
        dvt = tn((do3[h].astype(F32) * cc).astype(BF16), pb[h])
        for b in range(NY):
            dkv[h, b, 0] = dkt[:, b * KR:(b + 1) * KR].T
            dkv[h, b, 1] = dvt[:, b * KR:(b + 1) * KR].T
        ks1[h, 0, 0] = dkv[h, y2, 0].astype(BF16)
        ks1[h, 0, 1] = dkv[h, yr, 1].astype(BF16)
        ks1[h, 1, 0] = dkv[h, y2, 1].astype(BF16)
        ks1[h, 1, 1] = dkv[h, yl, 0].astype(BF16)
        go(leg(h, 0, 0, dyr))
        go(leg(h, 1, 0, dyl))

    def leg(h, d, i, to):
        return rc(ks1.at[h, d, i], kr1.at[h, d, i], sk.at[i, d, h], rk.at[i, d, h], to)

    def near_blocks(h):
        go(leg(h, 0, 1, dyr))
        go(leg(h, 1, 1, dyl))

    def second_leg(h):
        arrived(kr1.at[h, 0, 0], rk.at[0, 0, h])
        ks2[h, 0] = (dkv[h, yr, 0] + kr1[h, 0, 0].astype(F32)).astype(BF16)
        go(rc(ks2.at[h, 0], kr2.at[h, 0], sk.at[2, 0, h], rk.at[2, 0, h], dyr))
        arrived(kr1.at[h, 1, 0], rk.at[0, 1, h])
        ks2[h, 1] = (dkv[h, yl, 1] + kr1[h, 1, 0].astype(F32)).astype(BF16)
        go(rc(ks2.at[h, 1], kr2.at[h, 1], sk.at[2, 1, h], rk.at[2, 1, h], dyl))

    def cache_out(h):
        arrived(kr1.at[h, 0, 1], rk.at[1, 0, h])
        arrived(kr1.at[h, 1, 1], rk.at[1, 1, h])
        arrived(kr2.at[h, 0], rk.at[2, 0, h])
        arrived(kr2.at[h, 1], rk.at[2, 1, h])
        cols = slice(h * HD, (h + 1) * HD)
        dk_out[:, cols] = (dkv[h, y, 0] + kr1[h, 1, 1].astype(F32) + kr2[h, 0].astype(F32)).astype(BF16)
        dv_out[:, cols] = (dkv[h, y, 1] + kr1[h, 0, 1].astype(F32) + kr2[h, 1].astype(F32)).astype(BF16)

    dprob_late(0)
    settle(ring_sends)
    stats_pair(0)
    for h in heads_of(0):
        if h > 0:
            dprob_late(h)
    query_scale(0)
    query_send(0, 1, 3)
    query_send(0, 0, 4)
    stats_pair(1)
    for h in heads_of(1):
        dprob_late(h)
    query_scale(1)
    query_send(1, 1, 3)
    query_send(1, 0, 4)
    early = len(sends)
    query_send(0, 2, 1)
    query_send(1, 2, 1)
    total = stats_wait(0)
    cache_grads(0)
    weights(0, total)
    query_relay(0)
    near_blocks(0)
    cache_grads(1)
    near_blocks(1)
    total = stats_wait(1)
    cache_grads(2)
    weights(1, total)
    query_relay(1)
    near_blocks(2)
    cache_grads(3)
    cache_grads(4)
    second_leg(0)
    near_blocks(3)
    second_leg(1)
    near_blocks(4)
    query_sum(0)
    settle(early)
    second_leg(2)
    query_sum(1)

    for j in range(NY):
        for k in range(NX):
            ty, tx = up(y, j, NY), up(xh, k, NX)
            cp = rc(tb.at[tx * NY + ty], p8.at[k, s], s8.at[j, k], r8.at[k, s], dev(y, ty, tx, z))
            if (j, k) == (0, 0):
                self_out = cp

                @pl.when(jnp.logical_not(own))
                def _():
                    cp.start()
            else:
                go(cp)

    @pl.when(own)
    def _():
        p8[0, s] = tb[mine]

    second_leg(3)
    second_leg(4)
    for h in range(HG):
        cache_out(h)

    for k in range(NX):
        for b in range(NS):
            if k == 0:
                @pl.when(jnp.logical_not(own & (s == b)))
                def _():
                    arrived(p8.at[k, b], r8.at[k, b])
            else:
                arrived(p8.at[k, b], r8.at[k, b])
    for b in range(NS):
        for h in range(HG):
            col = b * GF + h * HD
            dq_out[0, :, col:col + HD] = (p8[0, b, h] + p8[1, b, h]).astype(BF16)

    @pl.when(jnp.logical_not(own))
    def _():
        self_in.wait_send()
        self_out.wait_send()

    for cp in sends:
        cp.wait_send()


def place(a, b, c, x, y, z):
    x[...] = a[...]
    y[...] = b[...]
    z[...] = c[...]


def local(block_order, queries, cache_keys, cache_values, attention_out, output_grad):
    dma = pltpu.SemaphoreType.DMA
    vm = pltpu.VMEM
    row = queries.shape
    scratch = [
        vm(row, BF16), vm(row, BF16), vm(row, BF16), vm((KR, GF), BF16), vm((KR, GF), BF16),
        vm((NS, HG + 1, 16, HD), BF16), vm((NB, HG + 1, 16, HD), BF16),
        vm((NZ, HG, NB, 16, HD), BF16), vm((NZ, QR, 128), F32),
        vm((NY, HG, 2, KR, HD), BF16), vm((HG, QW, HD), BF16), vm((HG, QW, HD), BF16), vm((QW, 128), F32),
        vm((HG, RT, KV), F32), vm((HG, QW, KV), BF16), vm((HG, QW, KV), BF16),
        vm((HG, QW, 128), F32), vm((HG, QW, 128), F32), vm((HG, QW, 128), F32),
        vm((2, 2, 16, 128), F32), vm((2, NZ, 16, 128), F32), vm((2, 5, 128, 128), F32),
        vm((HG, NZ, ZR, HD), F32), vm((2, 4, HG, ZR, HD), BF16), vm((2, 4, HG, ZR, HD), BF16),
        vm((HG, NY, 2, KR, HD), F32),
        vm((HG, 2, 2, KR, HD), BF16), vm((HG, 2, 2, KR, HD), BF16),
        vm((HG, 2, KR, HD), BF16), vm((HG, 2, KR, HD), BF16),
        vm((NB, HG, QR, HD), F32), vm((NX, NS, HG, QR, HD), F32),
        dma((5,)), dma((NS, NX)), dma((NX, NY)),
        dma((2, NT, 2)), dma((2, NT, 2)), dma((2, NT)), dma((2, NT)),
        dma((2, 2)), dma((2, 2)), dma((2, 2)), dma((2, 2)),
        dma((2, NZ)), dma((2, NZ)), dma((2,)), dma((2,)), dma((2, 4, 2)), dma((2, 4, 2)),
        dma((3, 2, HG)), dma((3, 2, HG)), dma((NY, NX)), dma((NX, NS)),
    ]
    vspec = pl.BlockSpec(memory_space=pltpu.VMEM)
    hbm = pl.BlockSpec(memory_space=pl.ANY)
    dq, dk, dv = pl.pallas_call(
        kernel,
        out_shape=(
            jax.ShapeDtypeStruct((1, QR, NS * GF), BF16),
            jax.ShapeDtypeStruct((KR, GF), BF16),
            jax.ShapeDtypeStruct((KR, GF), BF16),
        ),
        in_specs=[pl.BlockSpec(memory_space=pltpu.SMEM)] + [hbm] * 5,
        out_specs=(vspec, vspec, vspec),
        scratch_shapes=scratch,
        compiler_params=pltpu.CompilerParams(
            collective_id=0, has_side_effects=True, vmem_limit_bytes=56 << 20),
    )(block_order, queries, output_grad, attention_out, cache_keys, cache_values)
    return pl.pallas_call(
        place,
        out_shape=tuple(jax.ShapeDtypeStruct(v.shape, v.dtype) for v in (dq, dk, dv)),
        in_specs=[vspec] * 3,
        out_specs=(vspec,) * 3,
    )(dq, dk, dv)


def solution(mesh):
    in_specs = (
        P(),
        P("section", "ctx", None),
        P("ctx", "section"),
        P("ctx", "section"),
        P("section", "ctx", None),
        P("section", "ctx", None),
    )
    out_specs = (P("section", "ctx", None), P("ctx", "section"), P("ctx", "section"))
    return jax.shard_map(local, mesh=mesh, in_specs=in_specs, out_specs=out_specs, check_vma=False)
```
